32 devices in a mesh: ctx: 8 (over z, core), fsdp: 4 (over y, x).
Axes of the slice: x: 2, y: 2, z: 4, core: 2. Of those that a mesh axis runs over, the one named last changes fastest.
Arguments:
- tokens: float32 [4, 2048, 640], P('fsdp', 'ctx'), may hold values from -6 to 6
- cotangent: float32 [4, 2048, 640], P('fsdp', 'ctx'), may hold values from -6 to 6
- positions: int32 [4, 2048], P('fsdp', 'ctx'), may hold values from 0 to 1023, as said below
- block_order: int32 [16], replicated, may hold values from 0 to 15, as said below
- query_weight: bfloat16 [640, 1024], P('fsdp'), may hold values from -0.25 to 0.25
- key_weight: bfloat16 [640, 256], P('fsdp'), may hold values from -0.25 to 0.25
- value_weight: bfloat16 [640, 256], P('fsdp'), may hold values from -0.25 to 0.25
- output_weight: bfloat16 [1024, 640], P('fsdp'), may hold values from -0.1875 to 0.1875
- gate_weight: bfloat16 [640, 2048], P(None, 'fsdp'), may hold values from -0.25 to 0.25
- up_weight: bfloat16 [640, 2048], P(None, 'fsdp'), may hold values from -0.25 to 0.25
- down_weight: bfloat16 [2048, 640], P('fsdp'), may hold values from -0.125 to 0.125
- input_gain: bfloat16 [640], P('fsdp'), may hold values from -0.5 to 0.5
- query_gain: bfloat16 [256], P('fsdp'), may hold values from -0.5 to 0.5
- key_gain: bfloat16 [256], P('fsdp'), may hold values from -0.5 to 0.5
- mixer_gain: bfloat16 [640], P('fsdp'), may hold values from -0.5 to 0.5
- prefeed_gain: bfloat16 [640], P('fsdp'), may hold values from -0.5 to 0.5
- postfeed_gain: bfloat16 [640], P('fsdp'), may hold values from -0.5 to 0.5
Outputs:
- output: float32 [4, 2048, 640], P('fsdp', 'ctx')
- tokens_grad: float32 [4, 2048, 640], P('fsdp', 'ctx')
- query_grad: float32 [640, 1024], P('fsdp')
- key_grad: float32 [640, 256], P('fsdp')
- value_grad: float32 [640, 256], P('fsdp')
- outproj_grad: float32 [1024, 640], P('fsdp')
- gate_grad: float32 [640, 2048], P(None, 'fsdp')
- up_grad: float32 [640, 2048], P(None, 'fsdp')
- down_grad: float32 [2048, 640], P('fsdp')
- ingain_grad: float32 [640], P('fsdp')
- qgain_grad: float32 [256], P('fsdp')
- kgain_grad: float32 [256], P('fsdp')
- mixgain_grad: float32 [640], P('fsdp')
- pregain_grad: float32 [640], P('fsdp')
- postgain_grad: float32 [640], P('fsdp')
The draws below stay inside these ranges and needn't reach their ends.
Inputs may be any that keep to these rules, and one draw needn't show every extreme that they name: `block_order`: a permutation of 0 to 15 in which entries 2c and 2c + 1 sum to 15 for every c. `positions`: each token's index within its document: 0 at a document's first token, else one more than that of the token before it in sequence order; each sequence holds at most 4 documents, the first of them exactly 1024 tokens long.
All inputs are finite; a program needn't handle non-finite values.
Results may differ from the reference program's by a relative error of at most 0.015.
Values may be sent and summed in bfloat16 or wider, within the bound.
No kernel may reach another device: no remote copies, remote signals or barrier semaphores. Data moves between devices by JAX's collectives and lax.ppermute only.
A program may use at most 128 MiB of HBM per device.

```python
import jax
import jax.numpy as jnp
from jax import lax

D = 640
NH = 4
HD = 256
FF = 2048
BLK = 128
BLOCKS = 16
SEQ_LEN = 2048
SEQS = 4


def pair_order(key):
    pair_count = BLOCKS // 2
    chosen = jax.random.permutation(jax.random.fold_in(key, 11), pair_count)
    flip_bits = jax.random.randint(jax.random.fold_in(key, 12), (pair_count,), 0, 2)
    first_slot = jnp.where(flip_bits == 0, chosen, BLOCKS - 1 - chosen)
    second_slot = BLOCKS - 1 - first_slot
    return jnp.stack([first_slot, second_slot], axis=1).reshape(-1).astype(jnp.int32)


def draw_block_order(key, part):
    return pair_order(key)


def draw_positions(key, part):
    slot_order = pair_order(key)
    half_length = SEQ_LEN // 2
    later = jax.random.randint(jax.random.fold_in(key, 13), (SEQS, 2), half_length + 1, SEQ_LEN)
    fixed = jnp.full((SEQS, 1), half_length, jnp.int32)
    resets = jnp.concatenate([fixed, later.astype(jnp.int32)], axis=1)
    steps_all = jnp.arange(SEQ_LEN, dtype=jnp.int32)
    marked = jnp.any(steps_all[None, :, None] == resets[:, None, :], axis=2)
    starts = lax.cummax(jnp.where(marked, steps_all[None, :], 0), axis=1)
    within = steps_all[None, :] - starts
    storage = (slot_order[:, None] * BLK + jnp.arange(BLK, dtype=jnp.int32)[None, :]).reshape(-1)
    return jnp.take(within, storage, axis=1).astype(jnp.int32)


def block_scale(key, extent, cuts, least, top_value):
    level, own = 1.0, jax.random.fold_in(key, 6)
    for axis_at, blocks in cuts:
        steps = jnp.exp(jax.random.uniform(jax.random.fold_in(own, axis_at), (blocks,), jnp.float32, least / len(cuts), top_value / len(cuts)))
        level = level * jnp.repeat(steps, extent[axis_at] // blocks).reshape([-1 if axis == axis_at else 1 for axis in range(len(extent))])
    return level


def normal_values(stream_key, shape, spread, limit, cuts=(), kind=jnp.bfloat16):
    entries = jax.random.normal(stream_key, shape, jnp.float32) * spread
    if len(cuts) > 0:
        entries = block_scale(stream_key, shape, cuts, -0.22, 0.18) * entries
    return jnp.clip(entries, min=-limit, max=limit).astype(kind)


def setup_inputs(seed: int = 0) -> dict:
    arg_keys = jax.random.split(jax.random.key(seed), 18)
    tokens = normal_values(arg_keys[0], (SEQS, SEQ_LEN, D), 1.0, 6.0, ((0, 4), (1, 8)), jnp.float32)
    cotangent = normal_values(arg_keys[1], (SEQS, SEQ_LEN, D), 1.0, 6.0, ((0, 4), (1, 8)), jnp.float32)
    positions = draw_positions(jax.random.fold_in(arg_keys[17], 71), 0)
    block_order = draw_block_order(jax.random.fold_in(arg_keys[17], 71), 0)
    query_weight = normal_values(arg_keys[4], (D, NH * HD), D ** -0.5, 0.25, ((0, 4),))
    key_weight = normal_values(arg_keys[5], (D, HD), D ** -0.5, 0.25, ((0, 4),))
    value_weight = normal_values(arg_keys[6], (D, HD), D ** -0.5, 0.25, ((0, 4),))
    output_weight = normal_values(arg_keys[7], (NH * HD, D), (NH * HD) ** -0.5, 0.1875, ((0, 4),))
    gate_weight = normal_values(arg_keys[8], (D, FF), D ** -0.5, 0.25, ((1, 4),))
    up_weight = normal_values(arg_keys[9], (D, FF), D ** -0.5, 0.25, ((1, 4),))
    down_weight = normal_values(arg_keys[10], (FF, D), FF ** -0.5, 0.125, ((0, 4),))
    input_gain = jnp.clip(jax.random.uniform(arg_keys[11], (D,), jnp.float32, -0.5, 0.5) * block_scale(arg_keys[11], (D,), ((0, 4),), -0.4, 0.0), -0.5, 0.5).astype(jnp.bfloat16)
    query_gain = jnp.clip(jax.random.uniform(arg_keys[12], (HD,), jnp.float32, -0.5, 0.5) * block_scale(arg_keys[12], (HD,), ((0, 4),), -0.4, 0.0), -0.5, 0.5).astype(jnp.bfloat16)
    key_gain = jnp.clip(jax.random.uniform(arg_keys[13], (HD,), jnp.float32, -0.5, 0.5) * block_scale(arg_keys[13], (HD,), ((0, 4),), -0.4, 0.0), -0.5, 0.5).astype(jnp.bfloat16)
    mixer_gain = jnp.clip(jax.random.uniform(arg_keys[14], (D,), jnp.float32, -0.5, 0.5) * block_scale(arg_keys[14], (D,), ((0, 4),), -0.4, 0.0), -0.5, 0.5).astype(jnp.bfloat16)
    prefeed_gain = jnp.clip(jax.random.uniform(arg_keys[15], (D,), jnp.float32, -0.5, 0.5) * block_scale(arg_keys[15], (D,), ((0, 4),), -0.4, 0.0), -0.5, 0.5).astype(jnp.bfloat16)
    postfeed_gain = jnp.clip(jax.random.uniform(arg_keys[16], (D,), jnp.float32, -0.5, 0.5) * block_scale(arg_keys[16], (D,), ((0, 4),), -0.4, 0.0), -0.5, 0.5).astype(jnp.bfloat16)
    return dict(tokens=tokens, cotangent=cotangent, positions=positions, block_order=block_order, query_weight=query_weight, key_weight=key_weight, value_weight=value_weight, output_weight=output_weight, gate_weight=gate_weight, up_weight=up_weight, down_weight=down_weight, input_gain=input_gain, query_gain=query_gain, key_gain=key_gain, mixer_gain=mixer_gain, prefeed_gain=prefeed_gain, postfeed_gain=postfeed_gain)


norm_eps = 1e-06
rope_base = 1000000.0
tanh_coef = 0.7978845608028654
cubic_coef = 0.044715

def norm_factor(inputs):
    return lax.rsqrt(lax.optimization_barrier(jnp.mean(inputs * inputs, axis=-1, keepdims=True)) + norm_eps)

def norm_apply(inputs, gain):
    return inputs * norm_factor(inputs) * (1.0 + gain)

def norm_back(inputs, gain, upstream):
    factor = norm_factor(inputs)
    normal = inputs * factor
    weighted = upstream * (1.0 + gain)
    grad_inputs = factor * (weighted - normal * lax.optimization_barrier(jnp.mean(normal * weighted, axis=-1, keepdims=True)))
    grad_gain = lax.optimization_barrier(jnp.sum((upstream * normal).reshape(-1, inputs.shape[-1]), axis=0))
    return (grad_inputs, grad_gain)

def rope_tables(places, width):
    half_width = width // 2
    frequency = rope_base ** (-2.0 * jnp.arange(half_width, dtype=jnp.float32) / width)
    angles = places.astype(jnp.float32)[:, None] * frequency[None, :]
    return (jnp.cos(angles), jnp.sin(angles))

def rope_apply(inputs, cosines, sine_terms):
    half_width = inputs.shape[-1] // 2
    first_half = inputs[..., :half_width]
    second_half = inputs[..., half_width:]
    return jnp.concatenate([first_half * cosines - second_half * sine_terms, second_half * cosines + first_half * sine_terms], axis=-1)

def rope_back(upstream, cosines, sine_terms):
    half_width = upstream.shape[-1] // 2
    first_half = upstream[..., :half_width]
    second_half = upstream[..., half_width:]
    return jnp.concatenate([first_half * cosines + second_half * sine_terms, second_half * cosines - first_half * sine_terms], axis=-1)

def gelu_parts(inputs):
    tanh_part = jnp.tanh(tanh_coef * (inputs + cubic_coef * inputs * inputs * inputs))
    activated = 0.5 * inputs * (1.0 + tanh_part)
    gelu_slope = 0.5 * (1.0 + tanh_part) + 0.5 * inputs * (1.0 - tanh_part * tanh_part) * tanh_coef * (1.0 + 3.0 * cubic_coef * inputs * inputs)
    return (activated, gelu_slope)

def reference(tokens, cotangent, positions, block_order, query_weight, key_weight, value_weight, output_weight, gate_weight, up_weight, down_weight, input_gain, query_gain, key_gain, mixer_gain, prefeed_gain, postfeed_gain):
    seq_length = tokens.shape[1]
    block_rows = seq_length // block_order.shape[0]
    head_dim = key_weight.shape[1]
    head_count = query_weight.shape[1] // head_dim
    score_scale = head_dim ** (-0.5)
    offsets = jnp.arange(block_rows, dtype=jnp.int32)
    key_index = (block_order[:, None] * block_rows + offsets[None, :]).reshape(-1)
    query_last = jnp.repeat(key_index, head_count)
    span_rows = min(512, seq_length)
    span_count = seq_length // span_rows
    block_size = span_rows * head_count
    gain_input = input_gain.astype(jnp.float32)
    gain_query = query_gain.astype(jnp.float32)
    gain_key = key_gain.astype(jnp.float32)
    gain_mixer = mixer_gain.astype(jnp.float32)
    gain_prefeed = prefeed_gain.astype(jnp.float32)
    gain_postfeed = postfeed_gain.astype(jnp.float32)

    def one_sequence(totals, inputs):
        residual, upstream_out, places = inputs
        normed = norm_apply(residual, gain_input).astype(jnp.bfloat16)
        query_raw = jnp.dot(normed, query_weight, preferred_element_type=jnp.float32).reshape(seq_length, head_count, head_dim)
        key_raw = jnp.dot(normed, key_weight, preferred_element_type=jnp.float32)
        value_rows = jnp.dot(normed, value_weight, preferred_element_type=jnp.float32).astype(jnp.bfloat16)
        cosines, sine_terms = rope_tables(places, head_dim)
        query_rows = rope_apply(norm_apply(query_raw, gain_query), cosines[:, None, :], sine_terms[:, None, :]).astype(jnp.bfloat16).reshape(seq_length * head_count, head_dim)
        key_rows = rope_apply(norm_apply(key_raw, gain_key), cosines, sine_terms).astype(jnp.bfloat16)
        query_first = jnp.repeat(key_index - places, head_count)

        def score_rows(queries, last_ids, first_ids):
            scores = jnp.dot(queries, key_rows.T, preferred_element_type=jnp.float32) * score_scale
            allowed = (key_index[None, :] <= last_ids[:, None]) & (key_index[None, :] >= first_ids[:, None])
            return (scores, allowed)

        def forward_block(unused, pieces):
            queries, last_ids, first_ids = pieces
            scores, allowed = score_rows(queries, last_ids, first_ids)
            top_score = lax.optimization_barrier(jnp.max(jnp.where(allowed, scores, -1e+30), axis=1))
            log_total = top_score + jnp.log(lax.optimization_barrier(jnp.sum(jnp.where(allowed, jnp.exp(scores - top_score[:, None]), 0.0), axis=1)))
            probabilities = jnp.where(allowed, jnp.exp(scores - log_total[:, None]), 0.0).astype(jnp.bfloat16)
            attended = jnp.dot(probabilities, value_rows, preferred_element_type=jnp.float32).astype(jnp.bfloat16)
            return (unused, (attended, log_total))
        query_blocks = query_rows.reshape(span_count, block_size, head_dim)
        last_blocks = query_last.reshape(span_count, block_size)
        first_blocks = query_first.reshape(span_count, block_size)
        unused_out, (attended_blocks, log_blocks) = lax.scan(forward_block, jnp.zeros((), jnp.float32), (query_blocks, last_blocks, first_blocks))
        attended = attended_blocks.reshape(seq_length * head_count, head_dim)
        attended_flat = attended.reshape(seq_length, head_count * head_dim)
        projected = jnp.dot(attended_flat, output_weight, preferred_element_type=jnp.float32)
        hidden = residual + norm_apply(projected, gain_mixer)
        feed_in = norm_apply(hidden, gain_prefeed).astype(jnp.bfloat16)
        gate_vals = jnp.dot(feed_in, gate_weight, preferred_element_type=jnp.float32)
        up_vals = jnp.dot(feed_in, up_weight, preferred_element_type=jnp.float32)
        activated, gelu_slope = gelu_parts(gate_vals)
        mixed = (activated * up_vals).astype(jnp.bfloat16)
        feed_out = jnp.dot(mixed, down_weight, preferred_element_type=jnp.float32)
        output = hidden + norm_apply(feed_out, gain_postfeed)
        grad_feed, grad_postfeed = norm_back(feed_out, gain_postfeed, upstream_out)
        grad_feed_rows = grad_feed.astype(jnp.bfloat16)
        grad_mixed = jnp.dot(grad_feed_rows, down_weight.T, preferred_element_type=jnp.float32)
        down_grad = jnp.dot(mixed.T, grad_feed_rows, preferred_element_type=jnp.float32)
        grad_gate = (grad_mixed * up_vals * gelu_slope).astype(jnp.bfloat16)
        grad_up = (grad_mixed * activated).astype(jnp.bfloat16)
        gate_grad = jnp.dot(feed_in.T, grad_gate, preferred_element_type=jnp.float32)
        up_grad = jnp.dot(feed_in.T, grad_up, preferred_element_type=jnp.float32)
        grad_feed_in = jnp.dot(grad_gate, gate_weight.T, preferred_element_type=jnp.float32) + jnp.dot(grad_up, up_weight.T, preferred_element_type=jnp.float32)
        grad_hidden_part, grad_prefeed = norm_back(hidden, gain_prefeed, grad_feed_in)
        grad_hidden = upstream_out + grad_hidden_part
        grad_projected, grad_mixer = norm_back(projected, gain_mixer, grad_hidden)
        grad_proj_rows = grad_projected.astype(jnp.bfloat16)
        outproj_grad = jnp.dot(attended_flat.T, grad_proj_rows, preferred_element_type=jnp.float32)
        grad_attended = jnp.dot(grad_proj_rows, output_weight.T, preferred_element_type=jnp.float32).astype(jnp.bfloat16).reshape(seq_length * head_count, head_dim)
        row_delta = lax.optimization_barrier(jnp.sum(grad_attended.astype(jnp.float32) * attended.astype(jnp.float32), axis=1))

        def backward_block(carried, pieces):
            key_sum, value_sum = carried
            queries, upstream, delta_rows, log_total, last_ids, first_ids = pieces
            scores, allowed = score_rows(queries, last_ids, first_ids)
            probabilities = jnp.where(allowed, jnp.exp(scores - log_total[:, None]), 0.0)
            grad_probs = jnp.dot(upstream, value_rows.T, preferred_element_type=jnp.float32)
            grad_scores = (probabilities * (grad_probs - delta_rows[:, None]) * score_scale).astype(jnp.bfloat16)
            grad_queries = jnp.dot(grad_scores, key_rows, preferred_element_type=jnp.float32)
            key_sum = key_sum + jnp.dot(grad_scores.T, queries, preferred_element_type=jnp.float32)
            value_sum = value_sum + jnp.dot(probabilities.astype(jnp.bfloat16).T, upstream, preferred_element_type=jnp.float32)
            return ((key_sum, value_sum), grad_queries)
        zero_keys = jnp.zeros((seq_length, head_dim), jnp.float32)
        (grad_key_rows, grad_value_rows), grad_query_blocks = lax.scan(backward_block, (zero_keys, zero_keys), (query_blocks, grad_attended.reshape(span_count, block_size, head_dim), row_delta.reshape(span_count, block_size), log_blocks, last_blocks, first_blocks))
        grad_query_rot = rope_back(grad_query_blocks.reshape(seq_length, head_count, head_dim), cosines[:, None, :], sine_terms[:, None, :])
        grad_query_raw, grad_qgain = norm_back(query_raw, gain_query, grad_query_rot)
        grad_key_raw, grad_kgain = norm_back(key_raw, gain_key, rope_back(grad_key_rows, cosines, sine_terms))
        query_back = grad_query_raw.reshape(seq_length, head_count * head_dim).astype(jnp.bfloat16)
        key_back = grad_key_raw.astype(jnp.bfloat16)
        value_back = grad_value_rows.astype(jnp.bfloat16)
        query_grad = jnp.dot(normed.T, query_back, preferred_element_type=jnp.float32)
        key_grad = jnp.dot(normed.T, key_back, preferred_element_type=jnp.float32)
        value_grad = jnp.dot(normed.T, value_back, preferred_element_type=jnp.float32)
        grad_normed = jnp.dot(query_back, query_weight.T, preferred_element_type=jnp.float32) + jnp.dot(key_back, key_weight.T, preferred_element_type=jnp.float32) + jnp.dot(value_back, value_weight.T, preferred_element_type=jnp.float32)
        grad_input_part, grad_ingain = norm_back(residual, gain_input, grad_normed)
        tokens_grad = grad_hidden + grad_input_part
        terms = (query_grad, key_grad, value_grad, outproj_grad, gate_grad, up_grad, down_grad, grad_ingain, grad_qgain, grad_kgain, grad_mixer, grad_prefeed, grad_postfeed)
        totals = tuple((accum_part + term_part for accum_part, term_part in zip(totals, terms)))
        return (totals, (output, tokens_grad))
    start_totals = tuple((jnp.zeros(member.shape, jnp.float32) for member in (query_weight, key_weight, value_weight, output_weight, gate_weight, up_weight, down_weight, input_gain, query_gain, key_gain, mixer_gain, prefeed_gain, postfeed_gain)))
    totals, (outputs, input_grads) = lax.scan(one_sequence, start_totals, (tokens, cotangent, positions))
    return (outputs, input_grads, totals[0], totals[1], totals[2], totals[3], totals[4], totals[5], totals[6], totals[7], totals[8], totals[9], totals[10], totals[11], totals[12])
```

```python
import jax
import jax.numpy as jnp
from jax import lax
from jax.experimental import pallas as pl
from jax.experimental.pallas import tpu as pltpu
from jax.sharding import PartitionSpec as P

norm_eps = 1e-06
rope_base = 1000000.0
tanh_coef = 0.7978845608028654
cubic_coef = 0.044715
bf16 = jnp.bfloat16
f32 = jnp.float32


def norm_factor(inputs):
    return lax.rsqrt(jnp.mean(inputs * inputs, axis=-1, keepdims=True) + norm_eps)


def norm_apply(inputs, gain):
    return inputs * norm_factor(inputs) * (1.0 + gain)


def norm_back(inputs, gain, upstream):
    factor = norm_factor(inputs)
    normal = inputs * factor
    weighted = upstream * (1.0 + gain)
    grad_inputs = factor * (weighted - normal * jnp.mean(normal * weighted, axis=-1, keepdims=True))
    grad_gain = jnp.sum((upstream * normal).reshape(-1, inputs.shape[-1]), axis=0)
    return (grad_inputs, grad_gain)


def rope_tables(places, width):
    half_width = width // 2
    frequency = rope_base ** (-2.0 * jnp.arange(half_width, dtype=f32) / width)
    angles = places.astype(f32)[:, None] * frequency[None, :]
    return (jnp.cos(angles), jnp.sin(angles))


def rope_apply(inputs, cosines, sine_terms):
    half_width = inputs.shape[-1] // 2
    first_half = inputs[..., :half_width]
    second_half = inputs[..., half_width:]
    return jnp.concatenate(
        [
            first_half * cosines - second_half * sine_terms,
            second_half * cosines + first_half * sine_terms,
        ],
        axis=-1,
    )


def rope_back(upstream, cosines, sine_terms):
    half_width = upstream.shape[-1] // 2
    first_half = upstream[..., :half_width]
    second_half = upstream[..., half_width:]
    return jnp.concatenate(
        [
            first_half * cosines + second_half * sine_terms,
            second_half * cosines - first_half * sine_terms,
        ],
        axis=-1,
    )


def gelu_parts(inputs):
    tanh_part = jnp.tanh(tanh_coef * (inputs + cubic_coef * inputs * inputs * inputs))
    activated = 0.5 * inputs * (1.0 + tanh_part)
    gelu_slope = 0.5 * (1.0 + tanh_part) + 0.5 * inputs * (
        1.0 - tanh_part * tanh_part
    ) * tanh_coef * (1.0 + 3.0 * cubic_coef * inputs * inputs)
    return (activated, gelu_slope)


def dot(a, b, dims):
    return lax.dot_general(a, b, (dims, ((), ())), preferred_element_type=f32)


def attend_kernel(q_ref, k_ref, v_ref, last_ref, first_ref, ids_ref, out_ref, lse_ref):
    scale = q_ref.shape[-1] ** (-0.5)
    scores = dot(q_ref[0], k_ref[0], ((1,), (1,))) * scale
    ids = ids_ref[0]
    allowed = (ids <= last_ref[0]) & (ids >= first_ref[0])
    scores = jnp.where(allowed, scores, -1e30)
    top = jnp.max(scores, axis=1, keepdims=True)
    weights = jnp.where(allowed, jnp.exp(scores - top), 0.0)
    lse = top + jnp.log(jnp.sum(weights, axis=1, keepdims=True))
    probs = (weights * jnp.exp(top - lse)).astype(bf16)
    out_ref[0] = dot(probs, v_ref[0], ((1,), (0,))).astype(bf16)
    lse_ref[0] = lse


def attend_back_kernel(
    q_ref, k_ref, v_ref, go_ref, att_ref, lse_ref, last_ref, first_ref, ids_ref,
    dq_ref, dkv_ref,
):
    scale = q_ref.shape[-1] ** (-0.5)
    head_dim = q_ref.shape[-1]
    scores = dot(q_ref[0], k_ref[0], ((1,), (1,))) * scale
    ids = ids_ref[0]
    allowed = (ids <= last_ref[0]) & (ids >= first_ref[0])
    probs = jnp.where(allowed, jnp.exp(scores - lse_ref[0]), 0.0)
    upstream = go_ref[0]
    delta = jnp.sum(upstream.astype(f32) * att_ref[0].astype(f32), axis=1, keepdims=True)
    grad_probs = dot(upstream, v_ref[0], ((1,), (1,)))
    grad_scores = (probs * (grad_probs - delta) * scale).astype(bf16)
    dq_ref[0] = dot(grad_scores, k_ref[0], ((1,), (0,)))
    dkv_ref[0, :, :head_dim] = dot(grad_scores, q_ref[0], ((0,), (0,))).astype(bf16)
    dkv_ref[0, :, head_dim:] = dot(probs.astype(bf16), upstream, ((0,), (0,))).astype(bf16)


def part_spec(shape):
    return pl.BlockSpec((1,) + tuple(shape[1:]), lambda i: (i,) + (0,) * (len(shape) - 1))


def attend(queries, keys, values, last, first, ids):
    args = (queries, keys, values, last, first, ids)
    outs = (
        jax.ShapeDtypeStruct(queries.shape, bf16),
        jax.ShapeDtypeStruct(last.shape, f32),
    )
    return pl.pallas_call(
        attend_kernel,
        grid=(queries.shape[0],),
        in_specs=[part_spec(a.shape) for a in args],
        out_specs=[part_spec(a.shape) for a in outs],
        out_shape=outs,
        name="attend",
    )(*args)


def attend_back(queries, keys, values, upstream, attended, lse, last, first, ids):
    args = (queries, keys, values, upstream, attended, lse, last, first, ids)
    outs = (
        jax.ShapeDtypeStruct(queries.shape, f32),
        jax.ShapeDtypeStruct(keys.shape[:2] + (2 * keys.shape[2],), bf16),
    )
    return pl.pallas_call(
        attend_back_kernel,
        grid=(queries.shape[0],),
        in_specs=[part_spec(a.shape) for a in args],
        out_specs=[part_spec(a.shape) for a in outs],
        out_shape=outs,
        name="attend_back",
    )(*args)


def make_body(fsdp_size, ctx_size):
    chips = ctx_size // 2

    def from_peer(x, axis, offset):
        size = fsdp_size if axis == "fsdp" else ctx_size
        return lax.ppermute(x, axis, [((i + offset) % size, i) for i in range(size)])

    def swap(x):
        return lax.ppermute(x, "ctx", [(i, i ^ 1) for i in range(ctx_size)])

    def gather_fsdp(x):
        return [x] + [from_peer(x, "fsdp", k) for k in range(1, fsdp_size)]

    def scatter_fsdp(x, fsdp_place):
        def entry(k):
            return lax.dynamic_index_in_dim(x, (fsdp_place + k) % fsdp_size, 0, keepdims=False)

        total = entry(0).astype(f32)
        for k in range(1, fsdp_size):
            total = total + from_peer(entry(fsdp_size - k), "fsdp", k).astype(f32)
        return total

    def chip_sum(x, parity, ctx_place):
        rows, width = x.shape
        part = rows // ctx_size
        x = x.reshape(2, rows // 2, width).astype(bf16)
        mine = lax.dynamic_index_in_dim(x, parity, 0, keepdims=False)
        theirs = lax.dynamic_index_in_dim(x, 1 - parity, 0, keepdims=False)
        half = (mine.astype(f32) + swap(theirs).astype(f32)).reshape(chips, part, width)
        half = half.astype(bf16)
        chip_place = ctx_place // 2

        def entry(k):
            return lax.dynamic_index_in_dim(half, (chip_place + k) % chips, 0, keepdims=False)

        total = entry(0).astype(f32)
        for k in range(1, chips):
            total = total + from_peer(entry(chips - k), "ctx", 2 * k).astype(f32)
        total = total.astype(bf16)
        full = jnp.zeros((chips, part, width), bf16)
        full = lax.dynamic_update_index_in_dim(full, total, chip_place, 0)
        for k in range(1, chips):
            full = lax.dynamic_update_index_in_dim(
                full, from_peer(total, "ctx", 2 * k), (chip_place + k) % chips, 0
            )
        other = swap(full)
        full = full.reshape(rows // 2, width)
        other = other.reshape(rows // 2, width)
        first = jnp.where(parity == 0, full, other)
        second = jnp.where(parity == 0, other, full)
        return jnp.concatenate([first, second], axis=0)

    def body(
        tokens,
        cotangent,
        positions,
        block_order,
        query_weight,
        key_weight,
        value_weight,
        output_weight,
        gate_weight,
        up_weight,
        down_weight,
        input_gain,
        query_gain,
        key_gain,
        mixer_gain,
        prefeed_gain,
        postfeed_gain,
    ):
        row_count = tokens.shape[1]
        width = tokens.shape[2]
        block_rows = row_count // 2
        head_dim = key_weight.shape[1]
        query_width = query_weight.shape[1]
        head_count = query_width // head_dim
        proj_width = query_width + 2 * head_dim
        shard_rows = query_weight.shape[0]
        out_rows = output_weight.shape[0]
        hidden_rows = down_weight.shape[0]
        half_rows = hidden_rows // 2
        block_count = block_order.shape[0]
        ctx_place = lax.axis_index("ctx")
        fsdp_place = lax.axis_index("fsdp")
        parity = ctx_place % 2

        gains_own = jnp.concatenate(
            [input_gain, query_gain, key_gain, mixer_gain, prefeed_gain, postfeed_gain]
        )
        gain_count = gains_own.shape[0]
        gain_rows = jnp.pad(gains_own, (0, 16 * proj_width - gain_count)).reshape(16, proj_width)
        proj_own = jnp.concatenate(
            [jnp.concatenate([query_weight, key_weight, value_weight], axis=1), gain_rows], axis=0
        )
        proj_parts = gather_fsdp(proj_own)
        proj_full = jnp.zeros((fsdp_size * shard_rows, proj_width), bf16)
        gain_full = jnp.zeros((fsdp_size, gain_count), f32)
        for k, part in enumerate(proj_parts):
            place = (fsdp_place + k) % fsdp_size
            proj_full = lax.dynamic_update_slice(proj_full, part[:shard_rows], (place * shard_rows, 0))
            gain_full = lax.dynamic_update_slice(
                gain_full, part[shard_rows : shard_rows + 1, :gain_count].astype(f32), (place, 0)
            )
        own_gains = (input_gain, query_gain, key_gain, mixer_gain, prefeed_gain, postfeed_gain)
        gains = []
        at = 0
        for member in own_gains:
            gains.append(gain_full[:, at : at + member.shape[0]].reshape(-1))
            at += member.shape[0]
        gain_input, gain_query, gain_key, gain_mixer, gain_prefeed, gain_postfeed = gains

        output_parts = gather_fsdp(output_weight)
        output_full = jnp.zeros((fsdp_size * out_rows, width), bf16)
        for k, part in enumerate(output_parts):
            output_full = lax.dynamic_update_slice(
                output_full, part, (((fsdp_place + k) % fsdp_size) * out_rows, 0)
            )

        gate_half = lax.dynamic_slice_in_dim(gate_weight, parity * half_rows, half_rows, axis=1)
        up_half = lax.dynamic_slice_in_dim(up_weight, parity * half_rows, half_rows, axis=1)
        down_half = lax.dynamic_slice_in_dim(down_weight, parity * half_rows, half_rows, axis=0)
        pair_half = jnp.concatenate([gate_half, up_half], axis=1)
        pair_parts = jnp.stack([from_peer(pair_half, "fsdp", k) for k in range(1, fsdp_size)])
        down_parts = jnp.stack([from_peer(down_half, "fsdp", k) for k in range(1, fsdp_size)])
        pair_other = swap(pair_parts)
        down_other = swap(down_parts)
        pieces = [pair_parts[k] for k in range(fsdp_size - 1)]
        pieces += [pair_other[k] for k in range(fsdp_size - 1)]
        gate_use = jnp.concatenate([gate_weight] + [p[:, :half_rows] for p in pieces], axis=1)
        up_use = jnp.concatenate([up_weight] + [p[:, half_rows:] for p in pieces], axis=1)
        down_use = jnp.concatenate(
            [down_weight, down_parts.reshape(-1, width), down_other.reshape(-1, width)], axis=0
        )

        own_blocks = lax.dynamic_slice_in_dim(block_order, 2 * ctx_place, 2)
        straight = own_blocks[0] < own_blocks[1]

        def ordered(x):
            return jnp.where(
                straight, x, jnp.concatenate([x[block_rows:], x[:block_rows]], axis=0)
            )

        residual = ordered(tokens[0])
        upstream_out = ordered(cotangent[0])
        places = ordered(positions[0])
        offsets = jnp.arange(block_rows, dtype=jnp.int32)
        low_blocks = jnp.minimum(block_order[0::2], block_order[1::2])
        high_blocks = jnp.maximum(block_order[0::2], block_order[1::2])
        sorted_blocks = jnp.stack([low_blocks, high_blocks])
        query_blocks = lax.dynamic_slice_in_dim(sorted_blocks, ctx_place, 1, axis=1)
        query_index = (query_blocks * block_rows + offsets[None, :]).reshape(-1)
        query_last = jnp.repeat(query_index, head_count).reshape(2, block_rows * head_count, 1)
        query_first = jnp.repeat(query_index - places, head_count).reshape(query_last.shape)
        sources = jnp.concatenate(
            [
                (ctx_place + 2 * jnp.arange(chips)) % ctx_size,
                ((ctx_place ^ 1) + 2 * jnp.arange(chips)) % ctx_size,
            ]
        )
        key_blocks = jnp.take(sorted_blocks, sources, axis=1)
        key_ids = (key_blocks[:, :, None] * block_rows + offsets).reshape(2, 1, -1)

        normed = norm_apply(residual, gain_input).astype(bf16)
        projections = jnp.dot(normed, proj_full, preferred_element_type=f32)
        query_raw = projections[:, :query_width].reshape(row_count, head_count, head_dim)
        key_raw = projections[:, query_width : query_width + head_dim]
        value_rows = projections[:, query_width + head_dim :].astype(bf16)
        cosines, sine_terms = rope_tables(places, head_dim)
        key_rows = rope_apply(norm_apply(key_raw, gain_key), cosines, sine_terms).astype(bf16)
        query_rows = (
            rope_apply(
                norm_apply(query_raw, gain_query), cosines[:, None, :], sine_terms[:, None, :]
            )
            .astype(bf16)
            .reshape(2, block_rows * head_count, head_dim)
        )
        own_pair = jnp.concatenate([key_rows, value_rows], axis=1)
        pair_mine = jnp.stack(
            [own_pair] + [from_peer(own_pair, "ctx", 2 * k) for k in range(1, chips)]
        )
        pair_theirs = swap(pair_mine)
        pairs = jnp.concatenate([pair_mine, pair_theirs], axis=0)
        pairs = pairs.reshape(ctx_size, 2, block_rows, 2 * head_dim)
        pairs = pairs.transpose(1, 0, 2, 3).reshape(2, ctx_size * block_rows, 2 * head_dim)
        keys = pairs[:, :, :head_dim]
        values = pairs[:, :, head_dim:]
        attended, log_total = attend(query_rows, keys, values, query_last, query_first, key_ids)
        attended_flat = attended.reshape(row_count, query_width)
        projected = jnp.dot(attended_flat, output_full, preferred_element_type=f32)
        hidden = residual + norm_apply(projected, gain_mixer)
        feed_in = norm_apply(hidden, gain_prefeed).astype(bf16)
        feed_in_all = jnp.concatenate(gather_fsdp(feed_in), axis=0)
        gate_vals = jnp.dot(feed_in, gate_use, preferred_element_type=f32)
        up_vals = jnp.dot(feed_in, up_use, preferred_element_type=f32)
        activated, gelu_slope = gelu_parts(gate_vals)
        mixed = (activated * up_vals).astype(bf16)
        feed_terms = jnp.dot(mixed, down_use, preferred_element_type=f32)
        output = hidden + norm_apply(feed_terms, gain_postfeed)
        grad_feed, grad_postfeed = norm_back(feed_terms, gain_postfeed, upstream_out)
        grad_feed_rows = grad_feed.astype(bf16)
        grad_feed_all = jnp.concatenate(gather_fsdp(grad_feed_rows), axis=0)
        grad_mixed = dot(grad_feed_rows, down_use, ((1,), (1,)))
        grad_gate = (grad_mixed * up_vals * gelu_slope).astype(bf16)
        grad_up = (grad_mixed * activated).astype(bf16)
        feed_back = dot(grad_gate, gate_use, ((1,), (1,))) + dot(grad_up, up_use, ((1,), (1,)))
        grad_hidden_part, grad_prefeed = norm_back(hidden, gain_prefeed, feed_back)
        grad_hidden = upstream_out + grad_hidden_part
        grad_projected, grad_mixer = norm_back(projected, gain_mixer, grad_hidden)
        grad_proj_rows = grad_projected.astype(bf16)
        grad_attended = (
            dot(grad_proj_rows, output_full, ((1,), (1,)))
            .astype(bf16)
            .reshape(2, block_rows * head_count, head_dim)
        )
        grad_query_rows, grad_pairs = attend_back(
            query_rows, keys, values, grad_attended, attended, log_total,
            query_last, query_first, key_ids,
        )

        grad_pairs = grad_pairs.reshape(2, 2, chips, block_rows, 2 * head_dim)
        partner_part = swap(grad_pairs[:, 1])
        chip_part = grad_pairs[:, 0].astype(f32) + partner_part.astype(f32)
        chip_send = chip_part.astype(bf16)
        grad_pair_own = chip_part[:, 0]
        for k in range(1, chips):
            grad_pair_own = grad_pair_own + from_peer(
                chip_send[:, chips - k], "ctx", 2 * k
            ).astype(f32)
        grad_pair_own = grad_pair_own.reshape(row_count, 2 * head_dim)

        gate_own = jnp.dot(feed_in_all, gate_weight, preferred_element_type=f32)
        up_own = jnp.dot(feed_in_all, up_weight, preferred_element_type=f32)
        activated_own, slope_own = gelu_parts(gate_own)
        mixed_own = (activated_own * up_own).astype(bf16)
        grad_mixed_own = dot(grad_feed_all, down_weight, ((1,), (1,)))
        grad_gate_own = (grad_mixed_own * up_own * slope_own).astype(bf16)
        grad_up_own = (grad_mixed_own * activated_own).astype(bf16)
        feed_grads = jnp.concatenate(
            [
                dot(grad_gate_own, feed_in_all, ((0,), (0,))),
                dot(grad_up_own, feed_in_all, ((0,), (0,))),
                dot(mixed_own, grad_feed_all, ((0,), (0,))),
            ],
            axis=0,
        )
        outproj_grad = dot(attended_flat, grad_proj_rows, ((0,), (0,))).astype(bf16)
        outproj_own = scatter_fsdp(outproj_grad.reshape(fsdp_size, out_rows, width), fsdp_place)
        early = chip_sum(jnp.concatenate([feed_grads, outproj_own], axis=0), parity, ctx_place)
        gate_grad = early[:hidden_rows].astype(f32).T
        up_grad = early[hidden_rows : 2 * hidden_rows].astype(f32).T
        down_grad = early[2 * hidden_rows : 3 * hidden_rows].astype(f32)
        out_grad = early[3 * hidden_rows :].astype(f32)

        grad_query_rot = rope_back(
            grad_query_rows.reshape(row_count, head_count, head_dim),
            cosines[:, None, :],
            sine_terms[:, None, :],
        )
        grad_query_raw, grad_qgain = norm_back(query_raw, gain_query, grad_query_rot)
        grad_key_raw, grad_kgain = norm_back(
            key_raw, gain_key, rope_back(grad_pair_own[:, :head_dim], cosines, sine_terms)
        )
        proj_back = jnp.concatenate(
            [
                grad_query_raw.reshape(row_count, query_width).astype(bf16),
                grad_key_raw.astype(bf16),
                grad_pair_own[:, head_dim:].astype(bf16),
            ],
            axis=1,
        )
        proj_grad = dot(normed, proj_back, ((0,), (0,))).astype(bf16)
        grad_normed = dot(proj_back, proj_full, ((1,), (1,)))
        grad_input_part, grad_ingain = norm_back(residual, gain_input, grad_normed)
        tokens_grad = grad_hidden + grad_input_part

        gain_grads = jnp.concatenate(
            [
                g.reshape(fsdp_size, -1)
                for g in (grad_ingain, grad_qgain, grad_kgain, grad_mixer, grad_prefeed, grad_postfeed)
            ],
            axis=1,
        )
        tail_rows = -(-2 * gain_count // proj_width)
        late_rows = shard_rows + 16

        def split_terms(g):
            top_term = g.astype(bf16)
            rest = (g - top_term.astype(f32)).astype(bf16)
            both = jnp.stack([top_term, rest], axis=-2)
            return both

        terms = split_terms(gain_grads).reshape(fsdp_size, 2 * gain_count)
        terms = jnp.pad(terms, ((0, 0), (0, 16 * proj_width - 2 * gain_count)))
        late = jnp.concatenate(
            [proj_grad.reshape(fsdp_size, shard_rows, proj_width),
             terms.reshape(fsdp_size, 16, proj_width)], axis=1
        )
        late_own = scatter_fsdp(late, fsdp_place)
        gain_own = late_own[shard_rows:].reshape(-1)[: 2 * gain_count].reshape(2, gain_count)
        gain_own = lax.psum(gain_own[0] + gain_own[1], "ctx")
        proj_sum = chip_sum(late_own[:shard_rows], parity, ctx_place).astype(f32)
        gain_sums = []
        at = 0
        for member in own_gains:
            gain_sums.append(gain_own[at : at + member.shape[0]])
            at += member.shape[0]
        return (
            ordered(output)[None],
            ordered(tokens_grad)[None],
            proj_sum[:, :query_width],
            proj_sum[:, query_width : query_width + head_dim],
            proj_sum[:, query_width + head_dim :],
            out_grad,
            gate_grad,
            up_grad,
            down_grad,
        ) + tuple(gain_sums)

    return body


def solution(mesh):
    in_specs = (
        P("fsdp", "ctx", None),
        P("fsdp", "ctx", None),
        P("fsdp", "ctx"),
        P(),
        P("fsdp", None),
        P("fsdp", None),
        P("fsdp", None),
        P("fsdp", None),
        P(None, "fsdp"),
        P(None, "fsdp"),
        P("fsdp", None),
        P("fsdp"),
        P("fsdp"),
        P("fsdp"),
        P("fsdp"),
        P("fsdp"),
        P("fsdp"),
    )
    out_specs = (
        P("fsdp", "ctx", None),
        P("fsdp", "ctx", None),
        P("fsdp", None),
        P("fsdp", None),
        P("fsdp", None),
        P("fsdp", None),
        P(None, "fsdp"),
        P(None, "fsdp"),
        P("fsdp", None),
        P("fsdp"),
        P("fsdp"),
        P("fsdp"),
        P("fsdp"),
        P("fsdp"),
        P("fsdp"),
    )
    body = make_body(mesh.shape["fsdp"], mesh.shape["ctx"])
    return jax.shard_map(body, mesh=mesh, in_specs=in_specs, out_specs=out_specs, check_vma=False)
```

```python
import jax
import jax.numpy as jnp
from jax import lax
from jax.experimental import pallas as pl
from jax.experimental.pallas import tpu as pltpu
from jax.sharding import PartitionSpec as P


norm_eps = 1e-06
rope_base = 1000000.0
tanh_coef = 0.7978845608028654
cubic_coef = 0.044715
bf16 = jnp.bfloat16
f32 = jnp.float32


def norm_factor(inputs):
    return lax.rsqrt(jnp.mean(inputs * inputs, axis=-1, keepdims=True) + norm_eps)


def norm_apply(inputs, gain):
    return inputs * norm_factor(inputs) * (1.0 + gain)


def norm_back(inputs, gain, upstream):
    factor = norm_factor(inputs)
    normal = inputs * factor
    weighted = upstream * (1.0 + gain)
    grad_inputs = factor * (weighted - normal * jnp.mean(normal * weighted, axis=-1, keepdims=True))
    grad_gain = jnp.sum((upstream * normal).reshape(-1, inputs.shape[-1]), axis=0)
    return (grad_inputs, grad_gain)


def rope_tables(places, width):
    half_width = width // 2
    frequency = rope_base ** (-2.0 * jnp.arange(half_width, dtype=f32) / width)
    angles = places.astype(f32)[:, None] * frequency[None, :]
    return (jnp.cos(angles), jnp.sin(angles))


def rope_apply(inputs, cosines, sine_terms):
    half_width = inputs.shape[-1] // 2
    first_half = inputs[..., :half_width]
    second_half = inputs[..., half_width:]
    return jnp.concatenate(
        [
            first_half * cosines - second_half * sine_terms,
            second_half * cosines + first_half * sine_terms,
        ],
        axis=-1,
    )


def rope_back(upstream, cosines, sine_terms):
    half_width = upstream.shape[-1] // 2
    first_half = upstream[..., :half_width]
    second_half = upstream[..., half_width:]
    return jnp.concatenate(
        [
            first_half * cosines + second_half * sine_terms,
            second_half * cosines - first_half * sine_terms,
        ],
        axis=-1,
    )


def gelu_parts(inputs):
    tanh_part = jnp.tanh(tanh_coef * (inputs + cubic_coef * inputs * inputs * inputs))
    activated = 0.5 * inputs * (1.0 + tanh_part)
    gelu_slope = 0.5 * (1.0 + tanh_part) + 0.5 * inputs * (
        1.0 - tanh_part * tanh_part
    ) * tanh_coef * (1.0 + 3.0 * cubic_coef * inputs * inputs)
    return (activated, gelu_slope)


def dot(a, b, dims):
    return lax.dot_general(a, b, (dims, ((), ())), preferred_element_type=f32)


def put_rows(ref, order, low, high):
    rows = low.shape[0]
    at = pl.multiple_of(order * rows, rows)
    other = pl.multiple_of((1 - order) * rows, rows)
    ref[pl.ds(at, rows), :] = low
    ref[pl.ds(other, rows), :] = high


def get_rows(ref, order):
    rows = ref.shape[0] // 2
    at = pl.multiple_of(order * rows, rows)
    other = pl.multiple_of((1 - order) * rows, rows)
    return jnp.concatenate([ref[pl.ds(at, rows), :], ref[pl.ds(other, rows), :]], axis=0)


def rope_norm(raw, gain, cosines, sine_terms):
    return rope_apply(norm_apply(raw, gain), cosines, sine_terms)


def pre_kernel(ins, outs, scratch):
    place_ref, tok_ref, gains_ref, qk_gain_ref, cos_ref, sin_ref, qw_ref, kw_ref, vw_ref, mine, theirs = ins
    normed_ref, q_ref, kv_ref, qraw_ref, kraw_ref, full_ref = outs
    order, fsdp_place, parity = place_ref[0], place_ref[1], place_ref[2]
    count = len(mine)
    size = count + 1
    shard, half = mine[0].shape
    query_width, head_dim = qw_ref.shape[1], kw_ref.shape[1]
    gain_in, gain_q, gain_k = gains_ref[0:1, :], qk_gain_ref[0:1, :], qk_gain_ref[1:2, :]
    at = pl.multiple_of(fsdp_place * shard, 16)
    full_ref[pl.ds(at, shard), :query_width] = qw_ref[...]
    full_ref[pl.ds(at, shard), query_width : query_width + head_dim] = kw_ref[...]
    full_ref[pl.ds(at, shard), query_width + head_dim :] = vw_ref[...]
    left = pl.multiple_of(parity * half, 128)
    right = pl.multiple_of((1 - parity) * half, 128)
    for k in range(count):
        at = pl.multiple_of(lax.rem(fsdp_place + k + 1, size) * shard, 16)
        full_ref[pl.ds(at, shard), pl.ds(left, half)] = mine[k][...]
        full_ref[pl.ds(at, shard), pl.ds(right, half)] = theirs[k][...]
    residual = get_rows(tok_ref, order)
    normed = norm_apply(residual, gain_in).astype(bf16)
    normed_ref[...] = normed
    cosines, sine_terms = cos_ref[...], sin_ref[...]
    for at in range(0, query_width, head_dim):
        raw = dot(normed, full_ref[:, at : at + head_dim], ((1,), (0,)))
        qraw_ref[:, at : at + head_dim] = raw
        q_ref[:, at : at + head_dim] = rope_norm(
            raw, gain_q, cosines, sine_terms
        ).astype(bf16)
    raw = dot(normed, full_ref[:, query_width : query_width + head_dim], ((1,), (0,)))
    kraw_ref[...] = raw
    kv_ref[:, :head_dim] = rope_norm(raw, gain_k, cosines, sine_terms).astype(bf16)
    kv_ref[:, head_dim:] = dot(
        normed, full_ref[:, query_width + head_dim :], ((1,), (0,))
    ).astype(bf16)


def mask_bias(ids, last, first):
    return jnp.where((ids <= last) & (ids >= first), 0.0, -1e30)


def attend_kernel(ins, outs, scratch):
    (place_ref, tok_ref, q_ref, mine, theirs, last_ref, first_ref, ids_ref,
     outw_ref, outp, outt, gains_ref) = ins
    att_ref, lse_ref, kv_ref, outfull_ref, projected_ref, hidden_ref, feed_ref = outs
    order, fsdp_place, parity = place_ref[0], place_ref[1], place_ref[2]
    chips = len(mine)
    rows = mine[0].shape[0] // 2
    head_dim = mine[0].shape[1] // 2
    heads = q_ref.shape[1] // head_dim
    scale = head_dim ** (-0.5)
    size = len(outp) + 1
    shard = outw_ref.shape[0]
    half = shard // 2
    at = pl.multiple_of(fsdp_place * shard, 16)
    outfull_ref[pl.ds(at, shard), :] = outw_ref[...]
    for k in range(1, size):
        at = lax.rem(fsdp_place + k, size) * shard
        left = pl.multiple_of(at + parity * half, 16)
        right = pl.multiple_of(at + (1 - parity) * half, 16)
        outfull_ref[pl.ds(left, half), :] = outp[k - 1][...]
        outfull_ref[pl.ds(right, half), :] = outt[k - 1][...]
    for part in range(2):
        own = slice(part * rows, (part + 1) * rows)
        for k in range(chips):
            kv_ref[part, k * rows : (k + 1) * rows, :] = mine[k][own, :]
            kv_ref[part, (chips + k) * rows : (chips + k + 1) * rows, :] = theirs[k][own, :]
        queries = jnp.concatenate(
            [q_ref[own, h * head_dim : (h + 1) * head_dim] for h in range(heads)], axis=0
        )
        scores = dot(queries, kv_ref[part, :, :head_dim], ((1,), (1,))) * scale
        bias = mask_bias(ids_ref[part], last_ref[own, :], first_ref[own, :])
        pieces = []
        for h in range(heads):
            one = scores[h * rows : (h + 1) * rows] + bias
            top = jnp.max(one, axis=1, keepdims=True)
            weights = jnp.exp(one - top)
            lse = top + jnp.log(jnp.sum(weights, axis=1, keepdims=True))
            lse_ref[part, h * rows : (h + 1) * rows, :] = lse
            pieces.append((weights * jnp.exp(top - lse)).astype(bf16))
        probs = jnp.concatenate(pieces, axis=0)
        attended = dot(probs, kv_ref[part, :, head_dim:], ((1,), (0,))).astype(bf16)
        for h in range(heads):
            att_ref[own, h * head_dim : (h + 1) * head_dim] = attended[h * rows : (h + 1) * rows]
    projected = dot(att_ref[...], outfull_ref[...], ((1,), (0,)))
    projected_ref[...] = projected
    hidden = get_rows(tok_ref, order) + norm_apply(projected, gains_ref[1:2, :])
    hidden_ref[...] = hidden
    feed_ref[...] = norm_apply(hidden, gains_ref[2:3, :]).astype(bf16)


def norm_back_rows(inputs, gain, upstream):
    grad, grad_gain = norm_back(inputs, gain, upstream)
    return grad, grad_gain[None, :]


def feed_kernel(ins, outs, scratch):
    (place_ref, cot_ref, feed_ref, hidden_ref, projected_ref, outfull_ref, gains_ref,
     gate_ref, up_ref, down_ref, pair_refs, down_refs) = ins
    out_ref, gfeed_ref, ghidden_ref, gproj_ref, gatt_ref, mix_ref, pre_ref, post_ref = outs
    act_ref, slope_ref = scratch
    order = place_ref[0]
    rows = feed_ref.shape[0] // 2
    half = pair_refs[0].shape[1] // 2
    pieces = [(lambda: gate_ref[...], lambda: up_ref[...], lambda: down_ref[...], gate_ref.shape[1])]
    for pr, dr in zip(pair_refs, down_refs):
        pieces.append(
            (
                lambda pr=pr: pr[:, :half],
                lambda pr=pr: pr[:, half:],
                lambda dr=dr: dr[...],
                half,
            )
        )
    feed_in = feed_ref[...]
    total = jnp.zeros(hidden_ref.shape, f32)
    at = 0
    for gate, up, down, units in pieces:
        gate_vals = dot(feed_in, gate(), ((1,), (0,)))
        up_vals = dot(feed_in, up(), ((1,), (0,)))
        activated, slope = gelu_parts(gate_vals)
        act_ref[:, at : at + units] = activated
        slope_ref[:, at : at + units] = up_vals * slope
        total = total + dot((activated * up_vals).astype(bf16), down(), ((1,), (0,)))
        at += units
    hidden = hidden_ref[...]
    output = hidden + norm_apply(total, gains_ref[3:4, :])
    put_rows(out_ref, order, output[:rows], output[rows:])
    upstream = get_rows(cot_ref, order)
    grad_feed, post_ref[...] = norm_back_rows(total, gains_ref[3:4, :], upstream)
    grad_feed = grad_feed.astype(bf16)
    gfeed_ref[...] = grad_feed
    back = jnp.zeros(hidden_ref.shape, f32)
    at = 0
    for gate, up, down, units in pieces:
        grad_mixed = dot(grad_feed, down(), ((1,), (1,)))
        grad_gate = (grad_mixed * slope_ref[:, at : at + units]).astype(bf16)
        grad_up = (grad_mixed * act_ref[:, at : at + units]).astype(bf16)
        back = back + dot(grad_gate, gate(), ((1,), (1,))) + dot(grad_up, up(), ((1,), (1,)))
        at += units
    part, pre_ref[...] = norm_back_rows(hidden, gains_ref[2:3, :], back)
    grad_hidden = upstream + part
    ghidden_ref[...] = grad_hidden
    grad_proj, mix_ref[...] = norm_back_rows(projected_ref[...], gains_ref[1:2, :], grad_hidden)
    grad_proj = grad_proj.astype(bf16)
    gproj_ref[...] = grad_proj
    gatt_ref[...] = dot(grad_proj, outfull_ref[...], ((1,), (1,))).astype(bf16)


def attend_back_kernel(ins, outs, scratch):
    (q_ref, kv_ref, gatt_ref, att_ref, lse_ref, last_ref, first_ref, ids_ref,
     qraw_ref, qk_gain_ref, cos_ref, sin_ref) = ins
    gq_ref, mine_ref, theirs_ref, qgain_ref = outs
    chips, rows, head_dim = mine_ref.shape[0], mine_ref.shape[1] // 2, mine_ref.shape[2] // 2
    heads = q_ref.shape[1] // head_dim
    scale = head_dim ** (-0.5)
    gain_total = jnp.zeros(qgain_ref.shape, f32)
    for part in range(2):
        own = slice(part * rows, (part + 1) * rows)

        def stacked(ref):
            return jnp.concatenate(
                [ref[own, h * head_dim : (h + 1) * head_dim] for h in range(heads)], axis=0
            )

        queries, upstream, attended = stacked(q_ref), stacked(gatt_ref), stacked(att_ref)
        keys, values = kv_ref[part, :, :head_dim], kv_ref[part, :, head_dim:]
        delta = jnp.sum(upstream.astype(f32) * attended.astype(f32), axis=1, keepdims=True)
        scores = dot(queries, keys, ((1,), (1,))) * scale
        grad_probs = dot(upstream, values, ((1,), (1,)))
        bias = mask_bias(ids_ref[part], last_ref[own, :], first_ref[own, :])
        prob_list, score_list = [], []
        for h in range(heads):
            one = slice(h * rows, (h + 1) * rows)
            probs = jnp.exp(scores[one] + bias - lse_ref[part, one, :])
            prob_list.append(probs.astype(bf16))
            score_list.append((probs * (grad_probs[one] - delta[one]) * scale).astype(bf16))
        probs = jnp.concatenate(prob_list, axis=0)
        grad_scores = jnp.concatenate(score_list, axis=0)
        grad_keys = dot(grad_scores, queries, ((0,), (0,)))
        grad_values = dot(probs, upstream, ((0,), (0,)))
        for k in range(chips):
            for ref, base, kind in ((mine_ref, 0, f32), (theirs_ref, chips, bf16)):
                piece = slice((base + k) * rows, (base + k + 1) * rows)
                ref[k, own, :head_dim] = grad_keys[piece].astype(kind)
                ref[k, own, head_dim:] = grad_values[piece].astype(kind)
        grad_queries = dot(grad_scores, keys, ((1,), (0,)))
        cosines, sine_terms = cos_ref[own, :], sin_ref[own, :]
        for h in range(heads):
            cols = slice(h * head_dim, (h + 1) * head_dim)
            rotated = rope_back(grad_queries[h * rows : (h + 1) * rows], cosines, sine_terms)
            grad_raw, grad_gain = norm_back_rows(
                qraw_ref[own, cols], qk_gain_ref[0:1, :], rotated
            )
            gq_ref[own, cols] = grad_raw.astype(bf16)
            gain_total = gain_total + grad_gain
    qgain_ref[...] = gain_total


def weight_kernel(ins, outs, scratch):
    place_ref, feed_refs, grad_refs, gate_ref, up_ref, down_ref, att_ref, gproj_ref = ins
    mine_ref, theirs_ref = outs
    (grad_ref,) = scratch
    parity = place_ref[2]
    count = len(feed_refs) - 1
    units = down_ref.shape[0]
    half = units // 2
    feed_in = jnp.concatenate([ref[...] for ref in feed_refs], axis=0)
    grad_feed = jnp.concatenate([ref[...] for ref in grad_refs], axis=0)
    gate_vals = dot(feed_in, gate_ref[...], ((1,), (0,)))
    up_vals = dot(feed_in, up_ref[...], ((1,), (0,)))
    activated, slope = gelu_parts(gate_vals)
    mixed = (activated * up_vals).astype(bf16)
    grad_mixed = dot(grad_feed, down_ref[...], ((1,), (1,)))
    grad_gate = (grad_mixed * up_vals * slope).astype(bf16)
    grad_up = (grad_mixed * activated).astype(bf16)
    grad_ref[0:units, :] = dot(grad_gate, feed_in, ((0,), (0,)))
    grad_ref[units : 2 * units, :] = dot(grad_up, feed_in, ((0,), (0,)))
    grad_ref[2 * units : 3 * units, :] = dot(mixed, grad_feed, ((0,), (0,)))
    grad_ref[3 * units :, :] = dot(att_ref[...], gproj_ref[...], ((0,), (0,)))
    shard = att_ref.shape[1] // (count + 1)
    groups = [(k * units, k * half, half) for k in range(3)]
    groups += [
        (3 * units + k * shard, 3 * half + k * (shard // 2), shard // 2) for k in range(count + 1)
    ]
    for start, to, size in groups:
        mine = pl.multiple_of(start + parity * size, 16)
        theirs = pl.multiple_of(start + (1 - parity) * size, 16)
        mine_ref[to : to + size, :] = grad_ref[pl.ds(mine, size), :]
        theirs_ref[to : to + size, :] = grad_ref[pl.ds(theirs, size), :].astype(bf16)


def put_gains(ref, at, value):
    top = value.astype(bf16)
    count = value.shape[0]
    ref[at : at + count, :] = top
    ref[at + count : at + 2 * count, :] = (value - top.astype(f32)).astype(bf16)


def post_kernel(ins, outs, scratch):
    (place_ref, tok_ref, own_ref, parts, kraw_ref, gains_ref, qk_gain_ref, cos_ref, sin_ref,
     normed_ref, gq_ref, full_ref, ghidden_ref, qgain_ref, mix_ref, pre_ref, post_ref) = ins
    tgrad_ref, mine_ref, theirs_ref, terms_ref = outs
    back_ref, grad_ref, sums_ref = scratch
    order, parity = place_ref[0], place_ref[2]
    head_dim = kraw_ref.shape[1]
    query_width = gq_ref.shape[1]
    rows = normed_ref.shape[0] // 2
    half = mine_ref.shape[1]
    total = own_ref[...]
    for k in range(len(parts)):
        total = total + parts[k][...].astype(f32)
    rotated = rope_back(total[:, :head_dim], cos_ref[...], sin_ref[...])
    grad_key, key_gain = norm_back_rows(
        kraw_ref[...], qk_gain_ref[1:2, :], rotated
    )
    back_ref[:, :query_width] = gq_ref[...]
    back_ref[:, query_width : query_width + head_dim] = grad_key.astype(bf16)
    back_ref[:, query_width + head_dim :] = total[:, head_dim:].astype(bf16)
    grad_ref[...] = dot(normed_ref[...], back_ref[...], ((0,), (0,)))
    left = pl.multiple_of(parity * half, 128)
    right = pl.multiple_of((1 - parity) * half, 128)
    mine_ref[...] = grad_ref[:, pl.ds(left, half)]
    theirs_ref[...] = grad_ref[:, pl.ds(right, half)].astype(bf16)
    grad_normed = dot(back_ref[...], full_ref[...], ((1,), (1,)))
    part, in_gain = norm_back_rows(
        get_rows(tok_ref, order), gains_ref[0:1, :], grad_normed
    )
    grads = ghidden_ref[...] + part
    put_rows(tgrad_ref, order, grads[:rows], grads[rows:])
    sums_ref[...] = jnp.zeros(sums_ref.shape, f32)
    for row, value in enumerate(
        (in_gain, mix_ref[...], pre_ref[...], post_ref[...], qgain_ref[...], key_gain)
    ):
        sums_ref[row : row + 1, : value.shape[1]] = value
    put_gains(terms_ref, 0, sums_ref[...])


def late_pack_kernel(ins, outs, scratch):
    place_ref, mine_ref, other_ref, terms_ref = ins
    fsdp_place = place_ref[1]
    size = len(outs)
    shard = mine_ref.shape[0] // size
    for k in range(size):
        at = pl.multiple_of(lax.rem(fsdp_place + size - k, size) * shard, 16)
        chunk = mine_ref[pl.ds(at, shard), :] + other_ref[pl.ds(at, shard), :].astype(f32)
        outs[k][:shard, :] = chunk.astype(bf16)
        outs[k][shard:, :] = terms_ref[...]


def late_sum_kernel(ins, outs, scratch):
    (out_ref,) = outs
    total = ins[0][...].astype(f32)
    for ref in ins[1:]:
        total = total + ref[...].astype(f32)
    rows = total.shape[0] - 16
    out_ref[:rows, :] = total[:rows].astype(bf16)
    put_gains(out_ref, rows, total[rows : rows + 8] + total[rows + 8 :])


def late_last_kernel(ins, outs, scratch):
    place_ref, mine_ref, other_ref = ins
    q_ref, k_ref, v_ref, gains_ref = outs
    (full_ref,) = scratch
    parity = place_ref[2]
    rows, half = q_ref.shape[0], mine_ref.shape[1]
    left = pl.multiple_of(parity * half, 128)
    right = pl.multiple_of((1 - parity) * half, 128)
    full_ref[:, pl.ds(left, half)] = mine_ref[:rows, :].astype(f32)
    full_ref[:, pl.ds(right, half)] = other_ref[:rows, :].astype(f32)
    width, head_dim = q_ref.shape[1], k_ref.shape[1]
    q_ref[...] = full_ref[:, :width]
    k_ref[...] = full_ref[:, width : width + head_dim]
    v_ref[...] = full_ref[:, width + head_dim :]
    both = mine_ref[rows:, :].astype(f32) + other_ref[rows:, :].astype(f32)
    gains_ref[...] = both[:8] + both[8:]


def early_pack_kernel(ins, outs, scratch):
    place_ref, mine_ref, other_ref = ins
    feed_ref, chunks = outs
    fsdp_place = place_ref[1]
    size = len(chunks)
    base, shard = feed_ref.shape[0], chunks[0].shape[0]
    feed_ref[...] = (mine_ref[:base, :] + other_ref[:base, :].astype(f32)).astype(bf16)
    for k in range(size):
        at = pl.multiple_of(base + lax.rem(fsdp_place + size - k, size) * shard, 16)
        chunk = mine_ref[pl.ds(at, shard), :] + other_ref[pl.ds(at, shard), :].astype(f32)
        chunks[k][...] = chunk.astype(bf16)


def early_last_kernel(ins, outs, scratch):
    place_ref, mine_ref, other_ref = ins
    gate_ref, up_ref, down_ref, out_ref = outs
    parity = place_ref[2]
    half = down_ref.shape[0] // 2
    out_half = out_ref.shape[0] // 2
    for ref, side in ((mine_ref, parity), (other_ref, 1 - parity)):
        cols = pl.multiple_of(side * half, 128)
        gate_ref[:, pl.ds(cols, half)] = ref[:half, :].astype(f32).T
        up_ref[:, pl.ds(cols, half)] = ref[half : 2 * half, :].astype(f32).T
        at = pl.multiple_of(side * half, 16)
        down_ref[pl.ds(at, half), :] = ref[2 * half : 3 * half, :].astype(f32)
        at = pl.multiple_of(side * out_half, 16)
        out_ref[pl.ds(at, out_half), :] = ref[3 * half :, :].astype(f32)


def run_kernel(kernel, args, outs, scratch=()):
    vmem = pl.BlockSpec(memory_space=pltpu.VMEM)
    smem = pl.BlockSpec(memory_space=pltpu.SMEM)
    flat, in_tree = jax.tree.flatten(args)
    shapes = jax.tree.map(
        lambda o: jax.ShapeDtypeStruct(*o), outs, is_leaf=lambda o: not isinstance(o[0][0], tuple)
    )
    flat_out, out_tree = jax.tree.flatten(shapes)

    def wrapped(*refs):
        ins = jax.tree.unflatten(in_tree, refs[: len(flat)])
        targets = jax.tree.unflatten(out_tree, refs[len(flat) : len(flat) + len(flat_out)])
        kernel(ins, targets, refs[len(flat) + len(flat_out) :])

    call = pl.pallas_call(
        wrapped,
        in_specs=[smem if a.ndim == 1 else vmem for a in flat],
        out_specs=[vmem for _ in flat_out],
        out_shape=flat_out,
        scratch_shapes=[pltpu.VMEM(s, d) for s, d in scratch],
        compiler_params=pltpu.CompilerParams(vmem_limit_bytes=56 * 2**20),
    )
    return jax.tree.unflatten(out_tree, call(*flat))


def make_body(fsdp_size, ctx_size):
    chips = ctx_size // 2

    def from_peer(x, axis, offset):
        size = fsdp_size if axis == "fsdp" else ctx_size
        return lax.ppermute(x, axis, [((i + offset) % size, i) for i in range(size)])

    def with_partner(x, bit=1):
        return lax.ppermute(x, "ctx", [(i, i ^ bit) for i in range(ctx_size)])

    def others_fsdp(x):
        return [from_peer(x, "fsdp", k) for k in range(1, fsdp_size)]

    def with_partners(parts):
        return [with_partner(p) for p in parts]

    def after(x, *others):
        return lax.optimization_barrier((x,) + others)[0]

    def pick(x, at, axis=0):
        return lax.dynamic_index_in_dim(x, at, axis, keepdims=False)

    def sum_chips(half, ctx_place):
        _, width = half.shape
        steps = []
        bit = 2
        while bit < ctx_size:
            side = (ctx_place // bit) % 2
            half = half.reshape(2, -1, width)
            sent = with_partner(pick(half, 1 - side), bit)
            half = (pick(half, side).astype(f32) + sent.astype(f32)).astype(bf16)
            steps.append((bit, side))
            bit *= 2
        for bit, side in reversed(steps):
            other = with_partner(half, bit)
            first = jnp.where(side == 0, half, other)
            second = jnp.where(side == 0, other, half)
            half = jnp.concatenate([first, second], axis=0)
        return half

    def body(
        tokens,
        cotangent,
        positions,
        block_order,
        query_weight,
        key_weight,
        value_weight,
        output_weight,
        gate_weight,
        up_weight,
        down_weight,
        input_gain,
        query_gain,
        key_gain,
        mixer_gain,
        prefeed_gain,
        postfeed_gain,
    ):
        row_count = tokens.shape[1]
        width = tokens.shape[2]
        block_rows = row_count // 2
        head_dim = key_weight.shape[1]
        query_width = query_weight.shape[1]
        head_count = query_width // head_dim
        proj_width = query_width + 2 * head_dim
        proj_half = proj_width // 2
        shard_rows = query_weight.shape[0]
        out_rows = output_weight.shape[0]
        hidden_rows = down_weight.shape[0]
        half_rows = hidden_rows // 2
        ctx_place = lax.axis_index("ctx")
        fsdp_place = lax.axis_index("fsdp")
        parity = ctx_place % 2

        proj_send = jnp.where(
            parity == 0,
            query_weight[:, :proj_half],
            jnp.concatenate([query_weight[:, proj_half:], key_weight, value_weight], axis=1),
        )
        proj_mine = others_fsdp(proj_send)

        wide = (input_gain, mixer_gain, prefeed_gain, postfeed_gain)
        narrow = (query_gain, key_gain)
        gain_cols, head_cols = input_gain.shape[0], query_gain.shape[0]
        gains_own = jnp.stack(
            [g.astype(f32) for g in wide]
            + [jnp.pad(g.astype(f32), (0, gain_cols - head_cols)) for g in narrow]
        )
        gain_parts = [gains_own] + others_fsdp(gains_own)
        gain_full = jnp.zeros((fsdp_size,) + gains_own.shape, f32)
        for k, part in enumerate(gain_parts):
            gain_full = lax.dynamic_update_index_in_dim(
                gain_full, part, (fsdp_place + k) % fsdp_size, 0
            )
        gain_full = gain_full.transpose(1, 0, 2)
        gains = gain_full[:4].reshape(4, width)
        qk_gains = gain_full[4:, :, :head_cols].reshape(2, head_dim)

        own_blocks = lax.dynamic_slice_in_dim(block_order, 2 * ctx_place, 2)
        flipped = (own_blocks[0] > own_blocks[1]).astype(jnp.int32)
        place = jnp.stack([flipped, fsdp_place, parity]).astype(jnp.int32)
        places = jnp.where(flipped == 0, positions[0], jnp.roll(positions[0], block_rows))
        offsets = jnp.arange(block_rows, dtype=jnp.int32)
        low_blocks = jnp.minimum(block_order[0::2], block_order[1::2])
        high_blocks = jnp.maximum(block_order[0::2], block_order[1::2])
        sorted_blocks = jnp.stack([low_blocks, high_blocks])
        query_blocks = lax.dynamic_slice_in_dim(sorted_blocks, ctx_place, 1, axis=1)
        query_index = (query_blocks * block_rows + offsets[None, :]).reshape(-1)
        query_last = query_index[:, None]
        query_first = (query_index - places)[:, None]
        sources = jnp.concatenate(
            [
                (ctx_place + 2 * jnp.arange(chips)) % ctx_size,
                ((ctx_place ^ 1) + 2 * jnp.arange(chips)) % ctx_size,
            ]
        )
        key_blocks = jnp.take(sorted_blocks, sources, axis=1)
        key_ids = (key_blocks[:, :, None] * block_rows + offsets).reshape(2, 1, -1)
        cosines, sine_terms = rope_tables(places, head_dim)
        tok, cot = tokens[0], cotangent[0]
        rows_width = (row_count, width)
        proj_ready = list(
            lax.optimization_barrier((*proj_mine, gains, qk_gains, place, cosines, sine_terms))
        )[: fsdp_size - 1]
        proj_theirs = with_partners(proj_ready)

        gate_half = lax.dynamic_slice_in_dim(gate_weight, parity * half_rows, half_rows, axis=1)
        up_half = lax.dynamic_slice_in_dim(up_weight, parity * half_rows, half_rows, axis=1)
        down_half = lax.dynamic_slice_in_dim(down_weight, parity * half_rows, half_rows, axis=0)
        out_half = lax.dynamic_slice_in_dim(
            output_weight, parity * (out_rows // 2), out_rows // 2, axis=0
        )
        pair_half = jnp.concatenate([gate_half, up_half], axis=1)
        pair_half = after(pair_half, *proj_mine)
        out_mine = others_fsdp(out_half)
        pair_mine = others_fsdp(pair_half)

        normed, query_rows, own_pair, query_raw, key_raw, proj_full = run_kernel(
            pre_kernel,
            (place, tok, gains, qk_gains, cosines, sine_terms,
             query_weight, key_weight, value_weight, proj_ready, proj_theirs),
            (
                (rows_width, bf16),
                ((row_count, query_width), bf16),
                ((row_count, 2 * head_dim), bf16),
                ((row_count, query_width), f32),
                ((row_count, head_dim), f32),
                ((fsdp_size * shard_rows, proj_width), bf16),
            ),
        )
        kv_mine = [own_pair] + [from_peer(own_pair, "ctx", 2 * k) for k in range(1, chips)]
        kv_ready = after(own_pair, query_last, query_first, key_ids)
        kv_theirs = [with_partner(kv_ready)] + with_partners(kv_mine[1:])
        down_mine = others_fsdp(after(down_half, own_pair))
        out_theirs = with_partners(out_mine)
        pair_ready = list(lax.optimization_barrier((*pair_mine, *kv_mine[1:])))[: fsdp_size - 1]
        pair_theirs = with_partners(pair_ready)
        down_theirs = with_partners(down_mine)
        attended, log_total, key_pairs, output_full, projected, hidden, feed_in = run_kernel(
            attend_kernel,
            (place, tok, query_rows, kv_mine, kv_theirs, query_last, query_first, key_ids,
             output_weight, out_mine, out_theirs, gains),
            (
                ((row_count, query_width), bf16),
                ((2, head_count * block_rows, 1), f32),
                ((2, ctx_size * block_rows, 2 * head_dim), bf16),
                ((fsdp_size * out_rows, width), bf16),
                (rows_width, f32),
                (rows_width, f32),
                (rows_width, bf16),
            ),
        )
        feed_all = [feed_in] + others_fsdp(feed_in)
        output, grad_feed, grad_hidden, grad_proj, grad_attended, gmix, gpre, gpost = run_kernel(
            feed_kernel,
            (place, cot, feed_in, hidden, projected, output_full, gains,
             gate_weight, up_weight, down_weight,
             pair_ready + pair_theirs, down_mine + down_theirs),
            (
                (rows_width, f32),
                (rows_width, bf16),
                (rows_width, f32),
                (rows_width, bf16),
                ((row_count, query_width), bf16),
                ((1, width), f32),
                ((1, width), f32),
                ((1, width), f32),
            ),
            (((row_count, fsdp_size * hidden_rows), f32),) * 2,
        )
        grad_all = [grad_feed] + others_fsdp(grad_feed)
        query_back, pairs_mine, pairs_theirs, gqgain = run_kernel(
            attend_back_kernel,
            (query_rows, key_pairs, grad_attended, attended, log_total,
             query_last, query_first, key_ids, query_raw, qk_gains, cosines, sine_terms),
            (
                ((row_count, query_width), bf16),
                ((chips, row_count, 2 * head_dim), f32),
                ((chips, row_count, 2 * head_dim), bf16),
                ((1, head_dim), f32),
            ),
        )

        pairs_other = with_partner(pairs_theirs)
        chip_part = pairs_mine + pairs_other.astype(f32)
        chip_send = [chip_part[chips - k].astype(bf16) for k in range(1, chips)]
        chip_own = chip_part[0]
        back_parts = [from_peer(chip_send[k - 1], "ctx", 2 * k) for k in range(1, chips)]

        early_rows = 3 * half_rows + fsdp_size * out_rows // 2
        early_mine, early_theirs = run_kernel(
            weight_kernel,
            (place, feed_all, grad_all, gate_weight, up_weight, down_weight, attended, grad_proj),
            (
                ((early_rows, width), f32),
                ((early_rows, width), bf16),
            ),
            (((2 * early_rows, width), f32),),
        )
        early_feed, out_chunks = run_kernel(
            early_pack_kernel,
            (place, early_mine, with_partner(early_theirs)),
            (
                ((3 * half_rows, width), bf16),
                [((out_rows // 2, width), bf16)] * fsdp_size,
            ),
        )
        out_sum = out_chunks[0].astype(f32)
        for k in range(1, fsdp_size):
            out_sum = out_sum + from_peer(out_chunks[k], "fsdp", k).astype(f32)
        early = sum_chips(jnp.concatenate([early_feed, out_sum.astype(bf16)], axis=0), ctx_place)
        gate_grad, up_grad, down_grad, out_grad = run_kernel(
            early_last_kernel,
            (place, early, with_partner(early)),
            (
                ((width, hidden_rows), f32),
                ((width, hidden_rows), f32),
                ((hidden_rows, width), f32),
                ((out_rows, width), f32),
            ),
        )

        tokens_grad, late_mine, late_theirs, late_terms = run_kernel(
            post_kernel,
            (place, tok, chip_own, back_parts, key_raw, gains, qk_gains,
             cosines, sine_terms, normed, query_back, proj_full, grad_hidden,
             gqgain, gmix, gpre, gpost),
            (
                (rows_width, f32),
                ((width, proj_half), f32),
                ((width, proj_half), bf16),
                ((16, proj_half), bf16),
            ),
            (
                ((row_count, proj_width), bf16),
                ((width, proj_width), f32),
                ((8, proj_half), f32),
            ),
        )
        late_shape = ((shard_rows + 16, proj_half), bf16)
        late_chunks = run_kernel(
            late_pack_kernel,
            (place, late_mine, with_partner(late_theirs), late_terms),
            [late_shape] * fsdp_size,
        )
        late_parts = [late_chunks[0]] + [
            from_peer(late_chunks[k], "fsdp", k) for k in range(1, fsdp_size)
        ]
        (late,) = run_kernel(late_sum_kernel, late_parts, [late_shape])
        bit = 2
        while bit < ctx_size:
            other = with_partner(late, bit)
            (late,) = run_kernel(late_sum_kernel, [late, other], [late_shape])
            bit *= 2
        query_grad, key_grad, value_grad, gain_sums = run_kernel(
            late_last_kernel,
            (place, late, with_partner(late)),
            (
                ((shard_rows, query_width), f32),
                ((shard_rows, head_dim), f32),
                ((shard_rows, head_dim), f32),
                ((8, proj_half), f32),
            ),
            (((shard_rows, proj_width), f32),),
        )
        wide_sums = lax.dynamic_slice(gain_sums, (0, fsdp_place * gain_cols), (4, gain_cols))
        head_sums = lax.dynamic_slice(gain_sums, (4, fsdp_place * head_cols), (2, head_cols))
        return (
            output[None],
            tokens_grad[None],
            query_grad,
            key_grad,
            value_grad,
            out_grad,
            gate_grad,
            up_grad,
            down_grad,
            wide_sums[0],
            head_sums[0],
            head_sums[1],
            wide_sums[1],
            wide_sums[2],
            wide_sums[3],
        )

    return body


def solution(mesh):
    in_specs = (
        P("fsdp", "ctx", None),
        P("fsdp", "ctx", None),
        P("fsdp", "ctx"),
        P(),
        P("fsdp", None),
        P("fsdp", None),
        P("fsdp", None),
        P("fsdp", None),
        P(None, "fsdp"),
        P(None, "fsdp"),
        P("fsdp", None),
        P("fsdp"),
        P("fsdp"),
        P("fsdp"),
        P("fsdp"),
        P("fsdp"),
        P("fsdp"),
    )
    out_specs = (
        P("fsdp", "ctx", None),
        P("fsdp", "ctx", None),
        P("fsdp", None),
        P("fsdp", None),
        P("fsdp", None),
        P("fsdp", None),
        P(None, "fsdp"),
        P(None, "fsdp"),
        P("fsdp", None),
        P("fsdp"),
        P("fsdp"),
        P("fsdp"),
        P("fsdp"),
        P("fsdp"),
        P("fsdp"),
    )
    inner = make_body(mesh.shape["fsdp"], mesh.shape["ctx"])

    return jax.shard_map(inner, mesh=mesh, in_specs=in_specs, out_specs=out_specs, check_vma=False)
```

```python
import jax
import jax.numpy as jnp
from jax import lax
from jax.experimental import pallas as pl
from jax.experimental.pallas import tpu as pltpu
from jax.sharding import PartitionSpec as P


norm_eps = 1e-06
rope_base = 1000000.0
tanh_coef = 0.7978845608028654
cubic_coef = 0.044715
bf16 = jnp.bfloat16
f32 = jnp.float32


def norm_factor(inputs):
    return lax.rsqrt(jnp.mean(inputs * inputs, axis=-1, keepdims=True) + norm_eps)


def norm_apply(inputs, gain):
    return inputs * norm_factor(inputs) * (1.0 + gain)


def norm_back(inputs, gain, upstream):
    factor = norm_factor(inputs)
    normal = inputs * factor
    weighted = upstream * (1.0 + gain)
    grad_inputs = factor * (weighted - normal * jnp.mean(normal * weighted, axis=-1, keepdims=True))
    grad_gain = jnp.sum((upstream * normal).reshape(-1, inputs.shape[-1]), axis=0)
    return (grad_inputs, grad_gain)


def rope_apply(inputs, cosines, sine_terms):
    half_width = inputs.shape[-1] // 2
    first_half = inputs[..., :half_width]
    second_half = inputs[..., half_width:]
    return jnp.concatenate(
        [
            first_half * cosines - second_half * sine_terms,
            second_half * cosines + first_half * sine_terms,
        ],
        axis=-1,
    )


def rope_back(upstream, cosines, sine_terms):
    half_width = upstream.shape[-1] // 2
    first_half = upstream[..., :half_width]
    second_half = upstream[..., half_width:]
    return jnp.concatenate(
        [
            first_half * cosines + second_half * sine_terms,
            second_half * cosines - first_half * sine_terms,
        ],
        axis=-1,
    )


def gelu_parts(inputs):
    tanh_part = jnp.tanh(tanh_coef * (inputs + cubic_coef * inputs * inputs * inputs))
    activated = 0.5 * inputs * (1.0 + tanh_part)
    gelu_slope = 0.5 * (1.0 + tanh_part) + 0.5 * inputs * (
        1.0 - tanh_part * tanh_part
    ) * tanh_coef * (1.0 + 3.0 * cubic_coef * inputs * inputs)
    return (activated, gelu_slope)


def dot(a, b, dims):
    return lax.dot_general(a, b, (dims, ((), ())), preferred_element_type=f32)


def scalars(place_ref):
    ctx_place, fsdp_place, parity = place_ref[0], place_ref[1], place_ref[2]
    first, second = place_ref[3 + 2 * ctx_place], place_ref[4 + 2 * ctx_place]
    return (first > second).astype(jnp.int32), ctx_place, fsdp_place, parity


def put_rows(ref, order, low, high):
    rows = low.shape[0]
    at = pl.multiple_of(order * rows, rows)
    other = pl.multiple_of((1 - order) * rows, rows)
    ref[pl.ds(at, rows), :] = low
    ref[pl.ds(other, rows), :] = high


def get_rows(ref, order):
    rows = ref.shape[0] // 2
    at = pl.multiple_of(order * rows, rows)
    other = pl.multiple_of((1 - order) * rows, rows)
    return jnp.concatenate([ref[pl.ds(at, rows), :], ref[pl.ds(other, rows), :]], axis=0)


def rope_norm(raw, gain, cosines, sine_terms):
    return rope_apply(norm_apply(raw, gain), cosines, sine_terms)


def first_kernel(ins, outs, scratch):
    parity_ref, qw_ref, kw_ref, vw_ref = ins
    (send_ref,) = outs
    parity = parity_ref[0]
    half = send_ref.shape[1]
    rest = qw_ref.shape[1] - half
    head_dim = kw_ref.shape[1]

    @pl.when(parity == 0)
    def _():
        send_ref[...] = qw_ref[:, :half]

    @pl.when(parity == 1)
    def _():
        send_ref[:, :rest] = qw_ref[:, half:]
        send_ref[:, rest : rest + head_dim] = kw_ref[...]
        send_ref[:, rest + head_dim :] = vw_ref[...]


def halves_kernel(ins, outs, scratch):
    place_ref, outw_ref, gate_ref, up_ref, down_ref = ins
    out_ref, pair_ref, dn_ref = outs
    parity = place_ref[2]
    half, out_half = dn_ref.shape[0], out_ref.shape[0]
    cols = pl.multiple_of(parity * half, 128)
    pair_ref[:, :half] = gate_ref[:, pl.ds(cols, half)]
    pair_ref[:, half:] = up_ref[:, pl.ds(cols, half)]
    dn_ref[...] = down_ref[pl.ds(pl.multiple_of(parity * half, 16), half), :]
    out_ref[...] = outw_ref[pl.ds(pl.multiple_of(parity * out_half, 16), out_half), :]


def table_kernel(ins, outs, scratch):
    place_ref, pos_ref, freq_ref = ins
    cos_ref, sin_ref, last_ref, first_ref, ids_ref = outs
    order, ctx_place, _, _ = scalars(place_ref)
    rows = pos_ref.shape[0] // 2
    size = ids_ref.shape[2] // rows
    places = get_rows(pos_ref, order)
    angles = places.astype(f32) * freq_ref[...]
    cos_ref[...] = jnp.cos(angles)
    sin_ref[...] = jnp.sin(angles)

    def blocks(at):
        one, two = place_ref[3 + 2 * at], place_ref[4 + 2 * at]
        return jnp.minimum(one, two), jnp.maximum(one, two)

    own = blocks(ctx_place)
    column = lax.broadcasted_iota(jnp.int32, (rows, 1), 0)
    line = lax.broadcasted_iota(jnp.int32, (1, rows), 1)
    for part in range(2):
        index = column + own[part] * rows
        at = slice(part * rows, (part + 1) * rows)
        last_ref[at, :] = index
        first_ref[at, :] = index - places[at]
    for slot in range(size):
        base = ctx_place if slot < size // 2 else ctx_place + 1 - 2 * place_ref[2]
        source = blocks(lax.rem(base + 2 * (slot % (size // 2)), size))
        for part in range(2):
            ids_ref[part, :, slot * rows : (slot + 1) * rows] = line + source[part] * rows


def pre_kernel(ins, outs, scratch):
    place_ref, tok_ref, gains_ref, qk_gain_ref, cos_ref, sin_ref, qw_ref, kw_ref, vw_ref, mine, theirs = ins
    normed_ref, q_ref, kv_ref, qraw_ref, kraw_ref, full_ref = outs
    order, _, fsdp_place, parity = scalars(place_ref)
    count = len(mine)
    size = count + 1
    shard, half = mine[0].shape
    query_width, head_dim = qw_ref.shape[1], kw_ref.shape[1]
    gain_in, gain_q, gain_k = gains_ref[0:1, :], qk_gain_ref[0:1, :], qk_gain_ref[1:2, :]
    at = pl.multiple_of(fsdp_place * shard, 16)
    full_ref[pl.ds(at, shard), :query_width] = qw_ref[...]
    full_ref[pl.ds(at, shard), query_width : query_width + head_dim] = kw_ref[...]
    full_ref[pl.ds(at, shard), query_width + head_dim :] = vw_ref[...]
    left = pl.multiple_of(parity * half, 128)
    right = pl.multiple_of((1 - parity) * half, 128)
    for k in range(count):
        at = pl.multiple_of(lax.rem(fsdp_place + k + 1, size) * shard, 16)
        full_ref[pl.ds(at, shard), pl.ds(left, half)] = mine[k][...]
        full_ref[pl.ds(at, shard), pl.ds(right, half)] = theirs[k][...]
    residual = get_rows(tok_ref, order)
    normed = norm_apply(residual, gain_in).astype(bf16)
    normed_ref[...] = normed
    cosines, sine_terms = cos_ref[...], sin_ref[...]
    for at in range(0, query_width, head_dim):
        raw = dot(normed, full_ref[:, at : at + head_dim], ((1,), (0,)))
        qraw_ref[:, at : at + head_dim] = raw
        q_ref[:, at : at + head_dim] = rope_norm(
            raw, gain_q, cosines, sine_terms
        ).astype(bf16)
    raw = dot(normed, full_ref[:, query_width : query_width + head_dim], ((1,), (0,)))
    kraw_ref[...] = raw
    kv_ref[:, :head_dim] = rope_norm(raw, gain_k, cosines, sine_terms).astype(bf16)
    kv_ref[:, head_dim:] = dot(
        normed, full_ref[:, query_width + head_dim :], ((1,), (0,))
    ).astype(bf16)


def mask_bias(ids, last, first):
    return jnp.where((ids <= last) & (ids >= first), 0.0, -1e30)


def attend_kernel(ins, outs, scratch):
    (place_ref, tok_ref, q_ref, mine, theirs, last_ref, first_ref, ids_ref,
     outw_ref, outp, outt, gains_ref) = ins
    att_ref, lse_ref, kv_ref, outfull_ref, projected_ref, hidden_ref, feed_ref = outs
    order, _, fsdp_place, parity = scalars(place_ref)
    chips = len(mine)
    rows = mine[0].shape[0] // 2
    head_dim = mine[0].shape[1] // 2
    heads = q_ref.shape[1] // head_dim
    scale = head_dim ** (-0.5)
    size = len(outp) + 1
    shard = outw_ref.shape[0]
    half = shard // 2
    at = pl.multiple_of(fsdp_place * shard, 16)
    outfull_ref[pl.ds(at, shard), :] = outw_ref[...]
    for k in range(1, size):
        at = lax.rem(fsdp_place + k, size) * shard
        left = pl.multiple_of(at + parity * half, 16)
        right = pl.multiple_of(at + (1 - parity) * half, 16)
        outfull_ref[pl.ds(left, half), :] = outp[k - 1][...]
        outfull_ref[pl.ds(right, half), :] = outt[k - 1][...]
    for part in range(2):
        own = slice(part * rows, (part + 1) * rows)
        for k in range(chips):
            kv_ref[part, k * rows : (k + 1) * rows, :] = mine[k][own, :]
            kv_ref[part, (chips + k) * rows : (chips + k + 1) * rows, :] = theirs[k][own, :]
        queries = jnp.concatenate(
            [q_ref[own, h * head_dim : (h + 1) * head_dim] for h in range(heads)], axis=0
        )
        scores = dot(queries, kv_ref[part, :, :head_dim], ((1,), (1,))) * scale
        bias = mask_bias(ids_ref[part], last_ref[own, :], first_ref[own, :])
        pieces = []
        for h in range(heads):
            one = scores[h * rows : (h + 1) * rows] + bias
            top = jnp.max(one, axis=1, keepdims=True)
            weights = jnp.exp(one - top)
            lse = top + jnp.log(jnp.sum(weights, axis=1, keepdims=True))
            lse_ref[part, h * rows : (h + 1) * rows, :] = lse
            pieces.append((weights * jnp.exp(top - lse)).astype(bf16))
        probs = jnp.concatenate(pieces, axis=0)
        attended = dot(probs, kv_ref[part, :, head_dim:], ((1,), (0,))).astype(bf16)
        for h in range(heads):
            att_ref[own, h * head_dim : (h + 1) * head_dim] = attended[h * rows : (h + 1) * rows]
    projected = dot(att_ref[...], outfull_ref[...], ((1,), (0,)))
    projected_ref[...] = projected
    hidden = get_rows(tok_ref, order) + norm_apply(projected, gains_ref[1:2, :])
    hidden_ref[...] = hidden
    feed_ref[...] = norm_apply(hidden, gains_ref[2:3, :]).astype(bf16)


def norm_back_rows(inputs, gain, upstream):
    grad, grad_gain = norm_back(inputs, gain, upstream)
    return grad, grad_gain[None, :]


def split_halves(ref, parity, size, mine_ref, theirs_ref):
    half = size // 2
    for k in range(ref.shape[0] // size):
        mine = pl.multiple_of(k * size + parity * half, 16)
        theirs = pl.multiple_of(k * size + (1 - parity) * half, 16)
        mine_ref[k * half : (k + 1) * half, :] = ref[pl.ds(mine, half), :]
        theirs_ref[k * half : (k + 1) * half, :] = ref[pl.ds(theirs, half), :].astype(bf16)


def feed_kernel(ins, outs, scratch):
    (place_ref, cot_ref, feed_ref, hidden_ref, projected_ref, outfull_ref, gains_ref,
     att_ref, gate_ref, up_ref, down_ref, pair_refs, down_refs) = ins
    (out_ref, gfeed_ref, ghidden_ref, gatt_ref, mix_ref, pre_ref, post_ref,
     omine_ref, otheirs_ref) = outs
    act_ref, slope_ref, ograd_ref = scratch
    order, _, _, parity = scalars(place_ref)
    rows = feed_ref.shape[0] // 2
    half = pair_refs[0].shape[1] // 2
    pieces = [(lambda: gate_ref[...], lambda: up_ref[...], lambda: down_ref[...], gate_ref.shape[1])]
    for pr, dr in zip(pair_refs, down_refs):
        pieces.append(
            (
                lambda pr=pr: pr[:, :half],
                lambda pr=pr: pr[:, half:],
                lambda dr=dr: dr[...],
                half,
            )
        )
    feed_in = feed_ref[...]
    total = jnp.zeros(hidden_ref.shape, f32)
    at = 0
    for gate, up, down, units in pieces:
        gate_vals = dot(feed_in, gate(), ((1,), (0,)))
        up_vals = dot(feed_in, up(), ((1,), (0,)))
        activated, slope = gelu_parts(gate_vals)
        act_ref[:, at : at + units] = activated
        slope_ref[:, at : at + units] = up_vals * slope
        total = total + dot((activated * up_vals).astype(bf16), down(), ((1,), (0,)))
        at += units
    hidden = hidden_ref[...]
    output = hidden + norm_apply(total, gains_ref[3:4, :])
    put_rows(out_ref, order, output[:rows], output[rows:])
    upstream = get_rows(cot_ref, order)
    grad_feed, post_ref[...] = norm_back_rows(total, gains_ref[3:4, :], upstream)
    grad_feed = grad_feed.astype(bf16)
    gfeed_ref[...] = grad_feed
    back = jnp.zeros(hidden_ref.shape, f32)
    at = 0
    for gate, up, down, units in pieces:
        grad_mixed = dot(grad_feed, down(), ((1,), (1,)))
        grad_gate = (grad_mixed * slope_ref[:, at : at + units]).astype(bf16)
        grad_up = (grad_mixed * act_ref[:, at : at + units]).astype(bf16)
        back = back + dot(grad_gate, gate(), ((1,), (1,))) + dot(grad_up, up(), ((1,), (1,)))
        at += units
    part, pre_ref[...] = norm_back_rows(hidden, gains_ref[2:3, :], back)
    grad_hidden = upstream + part
    ghidden_ref[...] = grad_hidden
    grad_proj, mix_ref[...] = norm_back_rows(projected_ref[...], gains_ref[1:2, :], grad_hidden)
    grad_proj = grad_proj.astype(bf16)
    gatt_ref[...] = dot(grad_proj, outfull_ref[...], ((1,), (1,))).astype(bf16)
    ograd_ref[...] = dot(att_ref[...], grad_proj, ((0,), (0,)))
    units = gate_ref.shape[1]
    shard = ograd_ref.shape[0] // (act_ref.shape[1] // units)
    split_halves(ograd_ref, parity, shard, omine_ref, otheirs_ref)


def attend_back_kernel(ins, outs, scratch):
    (q_ref, kv_ref, gatt_ref, att_ref, lse_ref, last_ref, first_ref, ids_ref,
     qraw_ref, qk_gain_ref, cos_ref, sin_ref) = ins
    gq_ref, mine_ref, theirs_ref, qgain_ref = outs
    chips, rows, head_dim = mine_ref.shape[0], mine_ref.shape[1] // 2, mine_ref.shape[2] // 2
    heads = q_ref.shape[1] // head_dim
    scale = head_dim ** (-0.5)
    gain_total = jnp.zeros(qgain_ref.shape, f32)
    for part in range(2):
        own = slice(part * rows, (part + 1) * rows)

        def stacked(ref):
            return jnp.concatenate(
                [ref[own, h * head_dim : (h + 1) * head_dim] for h in range(heads)], axis=0
            )

        queries, upstream, attended = stacked(q_ref), stacked(gatt_ref), stacked(att_ref)
        keys, values = kv_ref[part, :, :head_dim], kv_ref[part, :, head_dim:]
        delta = jnp.sum(upstream.astype(f32) * attended.astype(f32), axis=1, keepdims=True)
        scores = dot(queries, keys, ((1,), (1,))) * scale
        grad_probs = dot(upstream, values, ((1,), (1,)))
        bias = mask_bias(ids_ref[part], last_ref[own, :], first_ref[own, :])
        prob_list, score_list = [], []
        for h in range(heads):
            one = slice(h * rows, (h + 1) * rows)
            probs = jnp.exp(scores[one] + bias - lse_ref[part, one, :])
            prob_list.append(probs.astype(bf16))
            score_list.append((probs * (grad_probs[one] - delta[one]) * scale).astype(bf16))
        probs = jnp.concatenate(prob_list, axis=0)
        grad_scores = jnp.concatenate(score_list, axis=0)
        grad_keys = dot(grad_scores, queries, ((0,), (0,)))
        grad_values = dot(probs, upstream, ((0,), (0,)))
        for k in range(chips):
            for ref, base, kind in ((mine_ref, 0, f32), (theirs_ref, chips, bf16)):
                piece = slice((base + k) * rows, (base + k + 1) * rows)
                ref[k, own, :head_dim] = grad_keys[piece].astype(kind)
                ref[k, own, head_dim:] = grad_values[piece].astype(kind)
        grad_queries = dot(grad_scores, keys, ((1,), (0,)))
        cosines, sine_terms = cos_ref[own, :], sin_ref[own, :]
        for h in range(heads):
            cols = slice(h * head_dim, (h + 1) * head_dim)
            rotated = rope_back(grad_queries[h * rows : (h + 1) * rows], cosines, sine_terms)
            grad_raw, grad_gain = norm_back_rows(
                qraw_ref[own, cols], qk_gain_ref[0:1, :], rotated
            )
            gq_ref[own, cols] = grad_raw.astype(bf16)
            gain_total = gain_total + grad_gain
    qgain_ref[...] = gain_total


def weight_kernel(ins, outs, scratch):
    place_ref, feed_refs, grad_refs, gate_ref, up_ref, down_ref = ins
    mine_ref, theirs_ref = outs
    (grad_ref,) = scratch
    parity = place_ref[2]
    units = down_ref.shape[0]
    feed_in = jnp.concatenate([ref[...] for ref in feed_refs], axis=0)
    grad_feed = jnp.concatenate([ref[...] for ref in grad_refs], axis=0)
    gate_vals = dot(feed_in, gate_ref[...], ((1,), (0,)))
    up_vals = dot(feed_in, up_ref[...], ((1,), (0,)))
    activated, slope = gelu_parts(gate_vals)
    mixed = (activated * up_vals).astype(bf16)
    grad_mixed = dot(grad_feed, down_ref[...], ((1,), (1,)))
    grad_gate = (grad_mixed * up_vals * slope).astype(bf16)
    grad_up = (grad_mixed * activated).astype(bf16)
    grad_ref[0:units, :] = dot(grad_gate, feed_in, ((0,), (0,)))
    grad_ref[units : 2 * units, :] = dot(grad_up, feed_in, ((0,), (0,)))
    grad_ref[2 * units : 3 * units, :] = dot(mixed, grad_feed, ((0,), (0,)))
    split_halves(grad_ref, parity, units, mine_ref, theirs_ref)


def put_gains(ref, at, value):
    top = value.astype(bf16)
    count = value.shape[0]
    ref[at : at + count, :] = top
    ref[at + count : at + 2 * count, :] = (value - top.astype(f32)).astype(bf16)


def post_kernel(ins, outs, scratch):
    (place_ref, tok_ref, own_ref, parts, kraw_ref, gains_ref, qk_gain_ref, cos_ref, sin_ref,
     normed_ref, gq_ref, full_ref, ghidden_ref, qgain_ref, mix_ref, pre_ref, post_ref) = ins
    tgrad_ref, mine_ref, theirs_ref, terms_ref = outs
    back_ref, grad_ref, sums_ref = scratch
    order, _, _, parity = scalars(place_ref)
    head_dim = kraw_ref.shape[1]
    query_width = gq_ref.shape[1]
    rows = normed_ref.shape[0] // 2
    half = mine_ref.shape[1]
    total = own_ref[...]
    for k in range(len(parts)):
        total = total + parts[k][...].astype(f32)
    rotated = rope_back(total[:, :head_dim], cos_ref[...], sin_ref[...])
    grad_key, key_gain = norm_back_rows(
        kraw_ref[...], qk_gain_ref[1:2, :], rotated
    )
    back_ref[:, :query_width] = gq_ref[...]
    back_ref[:, query_width : query_width + head_dim] = grad_key.astype(bf16)
    back_ref[:, query_width + head_dim :] = total[:, head_dim:].astype(bf16)
    grad_ref[...] = dot(normed_ref[...], back_ref[...], ((0,), (0,)))
    left = pl.multiple_of(parity * half, 128)
    right = pl.multiple_of((1 - parity) * half, 128)
    mine_ref[...] = grad_ref[:, pl.ds(left, half)]
    theirs_ref[...] = grad_ref[:, pl.ds(right, half)].astype(bf16)
    grad_normed = dot(back_ref[...], full_ref[...], ((1,), (1,)))
    part, in_gain = norm_back_rows(
        get_rows(tok_ref, order), gains_ref[0:1, :], grad_normed
    )
    grads = ghidden_ref[...] + part
    put_rows(tgrad_ref, order, grads[:rows], grads[rows:])
    sums_ref[...] = jnp.zeros(sums_ref.shape, f32)
    for row, value in enumerate(
        (in_gain, mix_ref[...], pre_ref[...], post_ref[...], qgain_ref[...], key_gain)
    ):
        sums_ref[row : row + 1, : value.shape[1]] = value
    put_gains(terms_ref, 0, sums_ref[...])


def late_pack_kernel(ins, outs, scratch):
    place_ref, mine_ref, other_ref, terms_ref = ins
    fsdp_place = place_ref[1]
    size = len(outs)
    shard = mine_ref.shape[0] // size
    for k in range(size):
        at = pl.multiple_of(lax.rem(fsdp_place + size - k, size) * shard, 16)
        chunk = mine_ref[pl.ds(at, shard), :] + other_ref[pl.ds(at, shard), :].astype(f32)
        outs[k][:shard, :] = chunk.astype(bf16)
        outs[k][shard:, :] = terms_ref[...]


def late_sum_kernel(ins, outs, scratch):
    (out_ref,) = outs
    total = ins[0][...].astype(f32)
    for ref in ins[1:]:
        total = total + ref[...].astype(f32)
    rows = total.shape[0] - 16
    out_ref[:rows, :] = total[:rows].astype(bf16)
    put_gains(out_ref, rows, total[rows : rows + 8] + total[rows + 8 :])


def late_last_kernel(ins, outs, scratch):
    place_ref, mine_ref, other_ref = ins
    q_ref, k_ref, v_ref, wide_ref, narrow_ref = outs
    (full_ref,) = scratch
    parity = place_ref[2]
    fsdp_place = place_ref[1]
    rows, half = q_ref.shape[0], mine_ref.shape[1]
    left = pl.multiple_of(parity * half, 128)
    right = pl.multiple_of((1 - parity) * half, 128)
    full_ref[:, pl.ds(left, half)] = mine_ref[:rows, :].astype(f32)
    full_ref[:, pl.ds(right, half)] = other_ref[:rows, :].astype(f32)
    width, head_dim = q_ref.shape[1], k_ref.shape[1]
    q_ref[...] = full_ref[:, :width]
    k_ref[...] = full_ref[:, width : width + head_dim]
    v_ref[...] = full_ref[:, width + head_dim :]
    both = mine_ref[rows:, :].astype(f32) + other_ref[rows:, :].astype(f32)
    sums = both[:8] + both[8:]
    for ref in (wide_ref, narrow_ref):
        cols = ref.shape[1]
        ref[...] = pltpu.roll(sums, lax.rem(half - fsdp_place * cols, half), 1)[:, :cols]


def out_pack_kernel(ins, outs, scratch):
    place_ref, mine_ref, other_ref = ins
    fsdp_place = place_ref[1]
    size = len(outs)
    shard = outs[0].shape[0]
    for k in range(size):
        at = pl.multiple_of(lax.rem(fsdp_place + size - k, size) * shard, 16)
        chunk = mine_ref[pl.ds(at, shard), :] + other_ref[pl.ds(at, shard), :].astype(f32)
        outs[k][...] = chunk.astype(bf16)


def early_pack_kernel(ins, outs, scratch):
    place_ref, mine_ref, other_ref, parts = ins
    keep_ref, send_ref = outs
    (all_ref,) = scratch
    base = mine_ref.shape[0]
    all_ref[:base, :] = (mine_ref[...] + other_ref[...].astype(f32)).astype(bf16)
    total = parts[0][...].astype(f32)
    for ref in parts[1:]:
        total = total + ref[...].astype(f32)
    all_ref[base:, :] = total.astype(bf16)
    rows = keep_ref.shape[0]
    side = lax.rem(lax.div(place_ref[0], 2), 2)
    keep_ref[...] = all_ref[pl.ds(pl.multiple_of(side * rows, 16), rows), :]
    send_ref[...] = all_ref[pl.ds(pl.multiple_of((1 - side) * rows, 16), rows), :]


def early_last_kernel(ins, outs, scratch):
    place_ref, mine_ref, other_ref = ins
    gate_ref, up_ref, down_ref, out_ref = outs
    parity = place_ref[2]
    half = down_ref.shape[0] // 2
    out_half = out_ref.shape[0] // 2
    for ref, side in ((mine_ref, parity), (other_ref, 1 - parity)):
        cols = pl.multiple_of(side * half, 128)
        gate_ref[:, pl.ds(cols, half)] = ref[:half, :].astype(f32).T
        up_ref[:, pl.ds(cols, half)] = ref[half : 2 * half, :].astype(f32).T
        at = pl.multiple_of(side * half, 16)
        down_ref[pl.ds(at, half), :] = ref[2 * half : 3 * half, :].astype(f32)
        at = pl.multiple_of(side * out_half, 16)
        out_ref[pl.ds(at, out_half), :] = ref[3 * half :, :].astype(f32)


def run_kernel(kernel, args, outs, scratch=()):
    vmem = pl.BlockSpec(memory_space=pltpu.VMEM)
    smem = pl.BlockSpec(memory_space=pltpu.SMEM)
    flat, in_tree = jax.tree.flatten(args)
    shapes = jax.tree.map(
        lambda o: jax.ShapeDtypeStruct(*o), outs, is_leaf=lambda o: not isinstance(o[0][0], tuple)
    )
    flat_out, out_tree = jax.tree.flatten(shapes)

    def wrapped(*refs):
        ins = jax.tree.unflatten(in_tree, refs[: len(flat)])
        targets = jax.tree.unflatten(out_tree, refs[len(flat) : len(flat) + len(flat_out)])
        kernel(ins, targets, refs[len(flat) + len(flat_out) :])

    call = pl.pallas_call(
        wrapped,
        in_specs=[smem if a.ndim == 1 else vmem for a in flat],
        out_specs=[vmem for _ in flat_out],
        out_shape=flat_out,
        scratch_shapes=[pltpu.VMEM(s, d) for s, d in scratch],
        compiler_params=pltpu.CompilerParams(vmem_limit_bytes=56 * 2**20),
    )
    return jax.tree.unflatten(out_tree, call(*flat))


def make_body(fsdp_size, ctx_size):
    chips = ctx_size // 2

    def from_peer(x, axis, offset):
        size = fsdp_size if axis == "fsdp" else ctx_size
        return lax.ppermute(x, axis, [((i + offset) % size, i) for i in range(size)])

    def with_partner(x, bit=1):
        return lax.ppermute(x, "ctx", [(i, i ^ bit) for i in range(ctx_size)])

    def others_fsdp(x):
        return [from_peer(x, "fsdp", k) for k in range(1, fsdp_size)]

    def with_partners(parts):
        return [with_partner(p) for p in parts]

    def after(x, *others):
        return lax.optimization_barrier((x,) + others)[0]

    def pick(x, at, axis=0):
        return lax.dynamic_index_in_dim(x, at, axis, keepdims=False)

    def sum_chips(keep, send, ctx_place):
        width = keep.shape[1]
        steps = []
        bit = 2
        while bit < ctx_size:
            side = (ctx_place // bit) % 2
            sent = with_partner(send, bit)
            total = (keep.astype(f32) + sent.astype(f32)).astype(bf16)
            if 2 * bit < ctx_size:
                parts = total.reshape(2, -1, width)
                ahead = (ctx_place // (2 * bit)) % 2
                keep, send = pick(parts, ahead), pick(parts, 1 - ahead)
            steps.append((bit, side))
            bit *= 2
        for bit, side in reversed(steps):
            other = with_partner(total, bit)
            first = jnp.where(side == 0, total, other)
            second = jnp.where(side == 0, other, total)
            total = jnp.concatenate([first, second], axis=0)
        return total

    def body(
        tokens,
        cotangent,
        positions,
        block_order,
        query_weight,
        key_weight,
        value_weight,
        output_weight,
        gate_weight,
        up_weight,
        down_weight,
        input_gain,
        query_gain,
        key_gain,
        mixer_gain,
        prefeed_gain,
        postfeed_gain,
    ):
        row_count = tokens.shape[1]
        width = tokens.shape[2]
        block_rows = row_count // 2
        head_dim = key_weight.shape[1]
        query_width = query_weight.shape[1]
        head_count = query_width // head_dim
        proj_width = query_width + 2 * head_dim
        proj_half = proj_width // 2
        shard_rows = query_weight.shape[0]
        out_rows = output_weight.shape[0]
        hidden_rows = down_weight.shape[0]
        half_rows = hidden_rows // 2
        ctx_place = lax.axis_index("ctx")
        fsdp_place = lax.axis_index("fsdp")
        parity = ctx_place % 2

        place = jnp.concatenate(
            [jnp.stack([ctx_place, fsdp_place, parity]).astype(jnp.int32), block_order]
        )
        tok, cot = tokens[0], cotangent[0]
        rows_width = (row_count, width)
        (proj_send,) = run_kernel(
            first_kernel,
            (parity.astype(jnp.int32).reshape(1), query_weight, key_weight, value_weight),
            (((shard_rows, proj_half), bf16),),
        )
        proj_mine = others_fsdp(proj_send)
        gain_cols, head_cols = input_gain.shape[0], query_gain.shape[0]
        gains_own = jnp.stack(
            [g.astype(f32) for g in (input_gain, mixer_gain, prefeed_gain, postfeed_gain)]
            + [jnp.pad(g.astype(f32), (0, gain_cols - head_cols)) for g in (query_gain, key_gain)]
        )
        gain_parts = [gains_own] + others_fsdp(gains_own)
        gain_full = jnp.zeros((fsdp_size,) + gains_own.shape, f32)
        for k, part in enumerate(gain_parts):
            gain_full = lax.dynamic_update_index_in_dim(
                gain_full, part, (fsdp_place + k) % fsdp_size, 0
            )
        gain_full = gain_full.transpose(1, 0, 2)
        gains = gain_full[:4].reshape(4, width)
        qk_gains = gain_full[4:, :, :head_cols].reshape(2, head_dim)

        frequency = rope_base ** (-2.0 * jnp.arange(head_dim // 2, dtype=f32) / head_dim)
        cosines, sine_terms, query_last, query_first, key_ids = run_kernel(
            table_kernel,
            (place, positions[0][:, None], frequency[None]),
            (
                ((row_count, head_dim // 2), f32),
                ((row_count, head_dim // 2), f32),
                ((row_count, 1), jnp.int32),
                ((row_count, 1), jnp.int32),
                ((2, 1, ctx_size * block_rows), jnp.int32),
            ),
        )
        proj_ready = list(
            lax.optimization_barrier((*proj_mine, gains, qk_gains, cosines, sine_terms))
        )[: fsdp_size - 1]
        proj_theirs = with_partners(proj_ready)

        out_half, pair_half, down_half = run_kernel(
            halves_kernel,
            (place, output_weight, gate_weight, up_weight, down_weight),
            (
                ((out_rows // 2, width), bf16),
                ((width, 2 * half_rows), bf16),
                ((half_rows, width), bf16),
            ),
        )
        pair_half = after(pair_half, *proj_mine)
        out_mine = others_fsdp(out_half)
        pair_mine = others_fsdp(pair_half)

        normed, query_rows, own_pair, query_raw, key_raw, proj_full = run_kernel(
            pre_kernel,
            (place, tok, gains, qk_gains, cosines, sine_terms,
             query_weight, key_weight, value_weight, proj_ready, proj_theirs),
            (
                (rows_width, bf16),
                ((row_count, query_width), bf16),
                ((row_count, 2 * head_dim), bf16),
                ((row_count, query_width), f32),
                ((row_count, head_dim), f32),
                ((fsdp_size * shard_rows, proj_width), bf16),
            ),
        )
        kv_mine = [own_pair] + [from_peer(own_pair, "ctx", 2 * k) for k in range(1, chips)]
        kv_theirs = [with_partner(own_pair)] + with_partners(kv_mine[1:])
        down_mine = others_fsdp(after(down_half, own_pair))
        out_theirs = with_partners(out_mine)
        pair_ready = list(lax.optimization_barrier((*pair_mine, *kv_mine[1:])))[: fsdp_size - 1]
        pair_theirs = with_partners(pair_ready)
        down_theirs = with_partners(down_mine)
        attended, log_total, key_pairs, output_full, projected, hidden, feed_in = run_kernel(
            attend_kernel,
            (place, tok, query_rows, kv_mine, kv_theirs, query_last, query_first, key_ids,
             output_weight, out_mine, out_theirs, gains),
            (
                ((row_count, query_width), bf16),
                ((2, head_count * block_rows, 1), f32),
                ((2, ctx_size * block_rows, 2 * head_dim), bf16),
                ((fsdp_size * out_rows, width), bf16),
                (rows_width, f32),
                (rows_width, f32),
                (rows_width, bf16),
            ),
        )
        feed_all = [feed_in] + others_fsdp(feed_in)
        (output, grad_feed, grad_hidden, grad_attended, gmix, gpre, gpost,
         out_own, out_other) = run_kernel(
            feed_kernel,
            (place, cot, feed_in, hidden, projected, output_full, gains,
             attended, gate_weight, up_weight, down_weight,
             pair_ready + pair_theirs, down_mine + down_theirs),
            (
                (rows_width, f32),
                (rows_width, bf16),
                (rows_width, f32),
                ((row_count, query_width), bf16),
                ((1, width), f32),
                ((1, width), f32),
                ((1, width), f32),
                ((fsdp_size * out_rows // 2, width), f32),
                ((fsdp_size * out_rows // 2, width), bf16),
            ),
            (((row_count, fsdp_size * hidden_rows), f32),) * 2
            + (((fsdp_size * out_rows, width), f32),),
        )
        out_other = with_partner(out_other)
        grad_all = [grad_feed] + others_fsdp(grad_feed)
        query_back, pairs_mine, pairs_theirs, gqgain = run_kernel(
            attend_back_kernel,
            (query_rows, key_pairs, grad_attended, attended, log_total,
             query_last, query_first, key_ids, query_raw, qk_gains, cosines, sine_terms),
            (
                ((row_count, query_width), bf16),
                ((chips, row_count, 2 * head_dim), f32),
                ((chips, row_count, 2 * head_dim), bf16),
                ((1, head_dim), f32),
            ),
        )

        pairs_other = with_partner(pairs_theirs)
        chip_part = pairs_mine + pairs_other.astype(f32)
        chip_send = [chip_part[chips - k].astype(bf16) for k in range(1, chips)]
        chip_own = chip_part[0]
        back_parts = [from_peer(chip_send[k - 1], "ctx", 2 * k) for k in range(1, chips)]

        out_chunks = run_kernel(
            out_pack_kernel,
            (place, out_own, out_other),
            [((out_rows // 2, width), bf16)] * fsdp_size,
        )
        out_parts = [out_chunks[0]] + [
            from_peer(out_chunks[k], "fsdp", k) for k in range(1, fsdp_size)
        ]

        feed_rows = 3 * half_rows
        early_mine, early_theirs = run_kernel(
            weight_kernel,
            (place, [after(feed_in, out_chunks[0])] + feed_all[1:], grad_all,
             gate_weight, up_weight, down_weight),
            (
                ((feed_rows, width), f32),
                ((feed_rows, width), bf16),
            ),
            (((2 * feed_rows, width), f32),),
        )
        early_rows = feed_rows + out_rows // 2
        keep, send = run_kernel(
            early_pack_kernel,
            (place, early_mine, with_partner(early_theirs), out_parts),
            (((early_rows // 2, width), bf16),) * 2,
            (((early_rows, width), bf16),),
        )
        early = sum_chips(keep, send, ctx_place)
        gate_grad, up_grad, down_grad, out_grad = run_kernel(
            early_last_kernel,
            (place, early, with_partner(early)),
            (
                ((width, hidden_rows), f32),
                ((width, hidden_rows), f32),
                ((hidden_rows, width), f32),
                ((out_rows, width), f32),
            ),
        )

        tokens_grad, late_mine, late_theirs, late_terms = run_kernel(
            post_kernel,
            (place, tok, chip_own, back_parts, key_raw, gains, qk_gains,
             cosines, sine_terms, normed, query_back, proj_full, grad_hidden,
             gqgain, gmix, gpre, gpost),
            (
                (rows_width, f32),
                ((width, proj_half), f32),
                ((width, proj_half), bf16),
                ((16, proj_half), bf16),
            ),
            (
                ((row_count, proj_width), bf16),
                ((width, proj_width), f32),
                ((8, proj_half), f32),
            ),
        )
        late_shape = ((shard_rows + 16, proj_half), bf16)
        late_chunks = run_kernel(
            late_pack_kernel,
            (place, late_mine, with_partner(late_theirs), late_terms),
            [late_shape] * fsdp_size,
        )
        late_parts = [late_chunks[0]] + [
            from_peer(late_chunks[k], "fsdp", k) for k in range(1, fsdp_size)
        ]
        (late,) = run_kernel(late_sum_kernel, late_parts, [late_shape])
        bit = 2
        while bit < ctx_size:
            other = with_partner(late, bit)
            (late,) = run_kernel(late_sum_kernel, [late, other], [late_shape])
            bit *= 2
        query_grad, key_grad, value_grad, wide_sums, narrow_sums = run_kernel(
            late_last_kernel,
            (place, late, with_partner(late)),
            (
                ((shard_rows, query_width), f32),
                ((shard_rows, head_dim), f32),
                ((shard_rows, head_dim), f32),
                ((8, gain_cols), f32),
                ((8, head_cols), f32),
            ),
            (((shard_rows, proj_width), f32),),
        )
        return (
            output[None],
            tokens_grad[None],
            query_grad,
            key_grad,
            value_grad,
            out_grad,
            gate_grad,
            up_grad,
            down_grad,
            wide_sums[0],
            narrow_sums[4],
            narrow_sums[5],
            wide_sums[1],
            wide_sums[2],
            wide_sums[3],
        )

    return body


def solution(mesh):
    in_specs = (
        P("fsdp", "ctx", None),
        P("fsdp", "ctx", None),
        P("fsdp", "ctx"),
        P(),
        P("fsdp", None),
        P("fsdp", None),
        P("fsdp", None),
        P("fsdp", None),
        P(None, "fsdp"),
        P(None, "fsdp"),
        P("fsdp", None),
        P("fsdp"),
        P("fsdp"),
        P("fsdp"),
        P("fsdp"),
        P("fsdp"),
        P("fsdp"),
    )
    out_specs = (
        P("fsdp", "ctx", None),
        P("fsdp", "ctx", None),
        P("fsdp", None),
        P("fsdp", None),
        P("fsdp", None),
        P("fsdp", None),
        P(None, "fsdp"),
        P(None, "fsdp"),
        P("fsdp", None),
        P("fsdp"),
        P("fsdp"),
        P("fsdp"),
        P("fsdp"),
        P("fsdp"),
        P("fsdp"),
    )
    inner = make_body(mesh.shape["fsdp"], mesh.shape["ctx"])

    return jax.shard_map(inner, mesh=mesh, in_specs=in_specs, out_specs=out_specs, check_vma=False)
```

```python
import jax
import jax.numpy as jnp
from jax import lax
from jax.experimental import pallas as pl
from jax.experimental.pallas import tpu as pltpu
from jax.sharding import PartitionSpec as P


norm_eps = 1e-06
rope_base = 1000000.0
tanh_coef = 0.7978845608028654
cubic_coef = 0.044715
bf16 = jnp.bfloat16
f32 = jnp.float32


def norm_factor(inputs):
    return lax.rsqrt(jnp.mean(inputs * inputs, axis=-1, keepdims=True) + norm_eps)


def norm_apply(inputs, gain):
    return inputs * norm_factor(inputs) * (1.0 + gain)


def norm_back(inputs, gain, upstream):
    factor = norm_factor(inputs)
    normal = inputs * factor
    weighted = upstream * (1.0 + gain)
    grad_inputs = factor * (weighted - normal * jnp.mean(normal * weighted, axis=-1, keepdims=True))
    grad_gain = jnp.sum((upstream * normal).reshape(-1, inputs.shape[-1]), axis=0)
    return (grad_inputs, grad_gain)


def rope_apply(inputs, cosines, sine_terms):
    half_width = inputs.shape[-1] // 2
    first_half = inputs[..., :half_width]
    second_half = inputs[..., half_width:]
    return jnp.concatenate(
        [
            first_half * cosines - second_half * sine_terms,
            second_half * cosines + first_half * sine_terms,
        ],
        axis=-1,
    )


def rope_back(upstream, cosines, sine_terms):
    half_width = upstream.shape[-1] // 2
    first_half = upstream[..., :half_width]
    second_half = upstream[..., half_width:]
    return jnp.concatenate(
        [
            first_half * cosines + second_half * sine_terms,
            second_half * cosines - first_half * sine_terms,
        ],
        axis=-1,
    )


def gelu_parts(inputs):
    tanh_part = jnp.tanh(tanh_coef * (inputs + cubic_coef * inputs * inputs * inputs))
    activated = 0.5 * inputs * (1.0 + tanh_part)
    gelu_slope = 0.5 * (1.0 + tanh_part) + 0.5 * inputs * (
        1.0 - tanh_part * tanh_part
    ) * tanh_coef * (1.0 + 3.0 * cubic_coef * inputs * inputs)
    return (activated, gelu_slope)


def dot(a, b, dims):
    return lax.dot_general(a, b, (dims, ((), ())), preferred_element_type=f32)


def scalars(place_ref):
    ctx_place, fsdp_place, parity = place_ref[0], place_ref[1], place_ref[2]
    first, second = place_ref[3 + 2 * ctx_place], place_ref[4 + 2 * ctx_place]
    return (first > second).astype(jnp.int32), ctx_place, fsdp_place, parity


def put_rows(ref, order, low, high):
    rows = low.shape[0]
    at = pl.multiple_of(order * rows, rows)
    other = pl.multiple_of((1 - order) * rows, rows)
    ref[pl.ds(at, rows), :] = low
    ref[pl.ds(other, rows), :] = high


def get_rows(ref, order):
    rows = ref.shape[0] // 2
    at = pl.multiple_of(order * rows, rows)
    other = pl.multiple_of((1 - order) * rows, rows)
    return jnp.concatenate([ref[pl.ds(at, rows), :], ref[pl.ds(other, rows), :]], axis=0)


def rope_norm(raw, gain, cosines, sine_terms):
    return rope_apply(norm_apply(raw, gain), cosines, sine_terms)


def first_kernel(ins, outs, scratch):
    parity_ref, qw_ref, kw_ref, vw_ref = ins
    (send_ref,) = outs
    parity = parity_ref[0]
    half = send_ref.shape[1]
    rest = qw_ref.shape[1] - half
    head_dim = kw_ref.shape[1]

    @pl.when(parity == 0)
    def _():
        send_ref[...] = qw_ref[:, :half]

    @pl.when(parity == 1)
    def _():
        send_ref[:, :rest] = qw_ref[:, half:]
        send_ref[:, rest : rest + head_dim] = kw_ref[...]
        send_ref[:, rest + head_dim :] = vw_ref[...]


def halves_kernel(ins, outs, scratch):
    place_ref, outw_ref, gate_ref, up_ref, down_ref = ins
    out_ref, pair_ref, dn_ref = outs
    parity = place_ref[2]
    half, out_half = dn_ref.shape[0], out_ref.shape[0]
    cols = pl.multiple_of(parity * half, 128)
    pair_ref[:, :half] = gate_ref[:, pl.ds(cols, half)]
    pair_ref[:, half:] = up_ref[:, pl.ds(cols, half)]
    dn_ref[...] = down_ref[pl.ds(pl.multiple_of(parity * half, 16), half), :]
    out_ref[...] = outw_ref[pl.ds(pl.multiple_of(parity * out_half, 16), out_half), :]


def table_kernel(ins, outs, scratch):
    place_ref, pos_ref, freq_ref = ins
    cos_ref, sin_ref, last_ref, first_ref, ids_ref = outs
    order, ctx_place, _, _ = scalars(place_ref)
    rows = pos_ref.shape[0] // 2
    size = ids_ref.shape[2] // rows
    places = get_rows(pos_ref, order)
    angles = places.astype(f32) * freq_ref[...]
    cos_ref[...] = jnp.cos(angles)
    sin_ref[...] = jnp.sin(angles)

    def blocks(at):
        one, two = place_ref[3 + 2 * at], place_ref[4 + 2 * at]
        return jnp.minimum(one, two), jnp.maximum(one, two)

    own = blocks(ctx_place)
    column = lax.broadcasted_iota(jnp.int32, (rows, 1), 0)
    line = lax.broadcasted_iota(jnp.int32, (1, rows), 1)
    for part in range(2):
        index = column + own[part] * rows
        at = slice(part * rows, (part + 1) * rows)
        last_ref[at, :] = index
        first_ref[at, :] = index - places[at]
    for slot in range(size):
        base = ctx_place if slot < size // 2 else ctx_place + 1 - 2 * place_ref[2]
        source = blocks(lax.rem(base + 2 * (slot % (size // 2)), size))
        for part in range(2):
            ids_ref[part, :, slot * rows : (slot + 1) * rows] = line + source[part] * rows


def pre_kernel(ins, outs, scratch):
    place_ref, tok_ref, gains_ref, qk_gain_ref, cos_ref, sin_ref, qw_ref, kw_ref, vw_ref, mine, theirs = ins
    normed_ref, q_ref, kv_ref, qraw_ref, kraw_ref, full_ref = outs
    order, _, fsdp_place, parity = scalars(place_ref)
    count = len(mine)
    size = count + 1
    shard, half = mine[0].shape
    query_width, head_dim = qw_ref.shape[1], kw_ref.shape[1]
    gain_in, gain_q, gain_k = gains_ref[0:1, :], qk_gain_ref[0:1, :], qk_gain_ref[1:2, :]
    at = pl.multiple_of(fsdp_place * shard, 16)
    full_ref[pl.ds(at, shard), :query_width] = qw_ref[...]
    full_ref[pl.ds(at, shard), query_width : query_width + head_dim] = kw_ref[...]
    full_ref[pl.ds(at, shard), query_width + head_dim :] = vw_ref[...]
    left = pl.multiple_of(parity * half, 128)
    right = pl.multiple_of((1 - parity) * half, 128)
    for k in range(count):
        at = pl.multiple_of(lax.rem(fsdp_place + k + 1, size) * shard, 16)
        full_ref[pl.ds(at, shard), pl.ds(left, half)] = mine[k][...]
        full_ref[pl.ds(at, shard), pl.ds(right, half)] = theirs[k][...]
    residual = get_rows(tok_ref, order)
    normed = norm_apply(residual, gain_in).astype(bf16)
    normed_ref[...] = normed
    cosines, sine_terms = cos_ref[...], sin_ref[...]
    for at in range(0, query_width, head_dim):
        raw = dot(normed, full_ref[:, at : at + head_dim], ((1,), (0,)))
        qraw_ref[:, at : at + head_dim] = raw
        q_ref[:, at : at + head_dim] = rope_norm(
            raw, gain_q, cosines, sine_terms
        ).astype(bf16)
    raw = dot(normed, full_ref[:, query_width : query_width + head_dim], ((1,), (0,)))
    kraw_ref[...] = raw
    kv_ref[:, :head_dim] = rope_norm(raw, gain_k, cosines, sine_terms).astype(bf16)
    kv_ref[:, head_dim:] = dot(
        normed, full_ref[:, query_width + head_dim :], ((1,), (0,))
    ).astype(bf16)


def mask_bias(ids, last, first):
    return jnp.where((ids <= last) & (ids >= first), 0.0, -1e30)


def attend_kernel(ins, outs, scratch):
    (place_ref, tok_ref, q_ref, mine, theirs, last_ref, first_ref, ids_ref,
     outw_ref, outp, outt, gains_ref) = ins
    att_ref, lse_ref, kv_ref, outfull_ref, projected_ref, hidden_ref, feed_ref = outs
    order, _, fsdp_place, parity = scalars(place_ref)
    chips = len(mine)
    rows = mine[0].shape[0] // 2
    head_dim = mine[0].shape[1] // 2
    heads = q_ref.shape[1] // head_dim
    scale = head_dim ** (-0.5)
    size = len(outp) + 1
    shard = outw_ref.shape[0]
    half = shard // 2
    at = pl.multiple_of(fsdp_place * shard, 16)
    outfull_ref[pl.ds(at, shard), :] = outw_ref[...]
    for k in range(1, size):
        at = lax.rem(fsdp_place + k, size) * shard
        left = pl.multiple_of(at + parity * half, 16)
        right = pl.multiple_of(at + (1 - parity) * half, 16)
        outfull_ref[pl.ds(left, half), :] = outp[k - 1][...]
        outfull_ref[pl.ds(right, half), :] = outt[k - 1][...]
    for part in range(2):
        own = slice(part * rows, (part + 1) * rows)
        for k in range(chips):
            kv_ref[part, k * rows : (k + 1) * rows, :] = mine[k][own, :]
            kv_ref[part, (chips + k) * rows : (chips + k + 1) * rows, :] = theirs[k][own, :]
        queries = jnp.concatenate(
            [q_ref[own, h * head_dim : (h + 1) * head_dim] for h in range(heads)], axis=0
        )
        scores = dot(queries, kv_ref[part, :, :head_dim], ((1,), (1,))) * scale
        bias = mask_bias(ids_ref[part], last_ref[own, :], first_ref[own, :])
        pieces = []
        for h in range(heads):
            one = scores[h * rows : (h + 1) * rows] + bias
            top = jnp.max(one, axis=1, keepdims=True)
            weights = jnp.exp(one - top)
            lse = top + jnp.log(jnp.sum(weights, axis=1, keepdims=True))
            lse_ref[part, h * rows : (h + 1) * rows, :] = lse
            pieces.append((weights * jnp.exp(top - lse)).astype(bf16))
        probs = jnp.concatenate(pieces, axis=0)
        attended = dot(probs, kv_ref[part, :, head_dim:], ((1,), (0,))).astype(bf16)
        for h in range(heads):
            att_ref[own, h * head_dim : (h + 1) * head_dim] = attended[h * rows : (h + 1) * rows]
    projected = dot(att_ref[...], outfull_ref[...], ((1,), (0,)))
    projected_ref[...] = projected
    hidden = get_rows(tok_ref, order) + norm_apply(projected, gains_ref[1:2, :])
    hidden_ref[...] = hidden
    feed_ref[...] = norm_apply(hidden, gains_ref[2:3, :]).astype(bf16)


def norm_back_rows(inputs, gain, upstream):
    grad, grad_gain = norm_back(inputs, gain, upstream)
    return grad, grad_gain[None, :]


def split_halves(ref, parity, size, mine_ref, theirs_ref):
    half = size // 2
    for k in range(ref.shape[0] // size):
        mine = pl.multiple_of(k * size + parity * half, 16)
        theirs = pl.multiple_of(k * size + (1 - parity) * half, 16)
        mine_ref[k * half : (k + 1) * half, :] = ref[pl.ds(mine, half), :]
        theirs_ref[k * half : (k + 1) * half, :] = ref[pl.ds(theirs, half), :].astype(bf16)


def feed_kernel(ins, outs, scratch):
    (place_ref, cot_ref, feed_ref, hidden_ref, projected_ref, outfull_ref, gains_ref,
     att_ref, gate_ref, up_ref, down_ref, pair_refs, down_refs) = ins
    (out_ref, gfeed_ref, ghidden_ref, gatt_ref, mix_ref, pre_ref, post_ref,
     omine_ref, otheirs_ref) = outs
    act_ref, slope_ref, ograd_ref = scratch
    order, _, _, parity = scalars(place_ref)
    rows = feed_ref.shape[0] // 2
    half = pair_refs[0].shape[1] // 2
    pieces = [(lambda: gate_ref[...], lambda: up_ref[...], lambda: down_ref[...], gate_ref.shape[1])]
    for pr, dr in zip(pair_refs, down_refs):
        pieces.append(
            (
                lambda pr=pr: pr[:, :half],
                lambda pr=pr: pr[:, half:],
                lambda dr=dr: dr[...],
                half,
            )
        )
    feed_in = feed_ref[...]
    total = jnp.zeros(hidden_ref.shape, f32)
    at = 0
    for gate, up, down, units in pieces:
        gate_vals = dot(feed_in, gate(), ((1,), (0,)))
        up_vals = dot(feed_in, up(), ((1,), (0,)))
        activated, slope = gelu_parts(gate_vals)
        act_ref[:, at : at + units] = activated
        slope_ref[:, at : at + units] = up_vals * slope
        total = total + dot((activated * up_vals).astype(bf16), down(), ((1,), (0,)))
        at += units
    hidden = hidden_ref[...]
    output = hidden + norm_apply(total, gains_ref[3:4, :])
    put_rows(out_ref, order, output[:rows], output[rows:])
    upstream = get_rows(cot_ref, order)
    grad_feed, post_ref[...] = norm_back_rows(total, gains_ref[3:4, :], upstream)
    grad_feed = grad_feed.astype(bf16)
    gfeed_ref[...] = grad_feed
    back = jnp.zeros(hidden_ref.shape, f32)
    at = 0
    for gate, up, down, units in pieces:
        grad_mixed = dot(grad_feed, down(), ((1,), (1,)))
        grad_gate = (grad_mixed * slope_ref[:, at : at + units]).astype(bf16)
        grad_up = (grad_mixed * act_ref[:, at : at + units]).astype(bf16)
        back = back + dot(grad_gate, gate(), ((1,), (1,))) + dot(grad_up, up(), ((1,), (1,)))
        at += units
    part, pre_ref[...] = norm_back_rows(hidden, gains_ref[2:3, :], back)
    grad_hidden = upstream + part
    ghidden_ref[...] = grad_hidden
    grad_proj, mix_ref[...] = norm_back_rows(projected_ref[...], gains_ref[1:2, :], grad_hidden)
    grad_proj = grad_proj.astype(bf16)
    gatt_ref[...] = dot(grad_proj, outfull_ref[...], ((1,), (1,))).astype(bf16)
    ograd_ref[...] = dot(att_ref[...], grad_proj, ((0,), (0,)))
    units = gate_ref.shape[1]
    shard = ograd_ref.shape[0] // (act_ref.shape[1] // units)
    split_halves(ograd_ref, parity, shard, omine_ref, otheirs_ref)


def attend_back_kernel(ins, outs, scratch):
    (q_ref, kv_ref, gatt_ref, att_ref, lse_ref, last_ref, first_ref, ids_ref,
     qraw_ref, qk_gain_ref, cos_ref, sin_ref) = ins
    gq_ref, mine_ref, theirs_ref, qgain_ref = outs
    chips, rows, head_dim = mine_ref.shape[0], mine_ref.shape[1] // 2, mine_ref.shape[2] // 2
    heads = q_ref.shape[1] // head_dim
    scale = head_dim ** (-0.5)
    gain_total = jnp.zeros(qgain_ref.shape, f32)
    for part in range(2):
        own = slice(part * rows, (part + 1) * rows)

        def stacked(ref):
            return jnp.concatenate(
                [ref[own, h * head_dim : (h + 1) * head_dim] for h in range(heads)], axis=0
            )

        queries, upstream, attended = stacked(q_ref), stacked(gatt_ref), stacked(att_ref)
        keys, values = kv_ref[part, :, :head_dim], kv_ref[part, :, head_dim:]
        delta = jnp.sum(upstream.astype(f32) * attended.astype(f32), axis=1, keepdims=True)
        scores = dot(queries, keys, ((1,), (1,))) * scale
        grad_probs = dot(upstream, values, ((1,), (1,)))
        bias = mask_bias(ids_ref[part], last_ref[own, :], first_ref[own, :])
        prob_list, score_list = [], []
        for h in range(heads):
            one = slice(h * rows, (h + 1) * rows)
            probs = jnp.exp(scores[one] + bias - lse_ref[part, one, :])
            prob_list.append(probs.astype(bf16))
            score_list.append((probs * (grad_probs[one] - delta[one]) * scale).astype(bf16))
        probs = jnp.concatenate(prob_list, axis=0)
        grad_scores = jnp.concatenate(score_list, axis=0)
        grad_keys = dot(grad_scores, queries, ((0,), (0,)))
        grad_values = dot(probs, upstream, ((0,), (0,)))
        for k in range(chips):
            for ref, base, kind in ((mine_ref, 0, f32), (theirs_ref, chips, bf16)):
                piece = slice((base + k) * rows, (base + k + 1) * rows)
                ref[k, own, :head_dim] = grad_keys[piece].astype(kind)
                ref[k, own, head_dim:] = grad_values[piece].astype(kind)
        grad_queries = dot(grad_scores, keys, ((1,), (0,)))
        cosines, sine_terms = cos_ref[own, :], sin_ref[own, :]
        for h in range(heads):
            cols = slice(h * head_dim, (h + 1) * head_dim)
            rotated = rope_back(grad_queries[h * rows : (h + 1) * rows], cosines, sine_terms)
            grad_raw, grad_gain = norm_back_rows(
                qraw_ref[own, cols], qk_gain_ref[0:1, :], rotated
            )
            gq_ref[own, cols] = grad_raw.astype(bf16)
            gain_total = gain_total + grad_gain
    qgain_ref[...] = gain_total


def weight_kernel(ins, outs, scratch):
    place_ref, feed_refs, grad_refs, gate_ref, up_ref, down_ref, omine_ref, oother_ref = ins
    mine_ref, theirs_ref, chunks = outs
    fsdp_place, size = place_ref[1], len(chunks)
    shard = chunks[0].shape[0]
    for k in range(size):
        at = pl.multiple_of(lax.rem(fsdp_place + size - k, size) * shard, 16)
        chunk = omine_ref[pl.ds(at, shard), :] + oother_ref[pl.ds(at, shard), :].astype(f32)
        chunks[k][...] = chunk.astype(bf16)
    (grad_ref,) = scratch
    parity = place_ref[2]
    units = down_ref.shape[0]
    feed_in = jnp.concatenate([ref[...] for ref in feed_refs], axis=0)
    grad_feed = jnp.concatenate([ref[...] for ref in grad_refs], axis=0)
    gate_vals = dot(feed_in, gate_ref[...], ((1,), (0,)))
    up_vals = dot(feed_in, up_ref[...], ((1,), (0,)))
    activated, slope = gelu_parts(gate_vals)
    mixed = (activated * up_vals).astype(bf16)
    grad_mixed = dot(grad_feed, down_ref[...], ((1,), (1,)))
    grad_gate = (grad_mixed * up_vals * slope).astype(bf16)
    grad_up = (grad_mixed * activated).astype(bf16)
    grad_ref[0:units, :] = dot(grad_gate, feed_in, ((0,), (0,)))
    grad_ref[units : 2 * units, :] = dot(grad_up, feed_in, ((0,), (0,)))
    grad_ref[2 * units : 3 * units, :] = dot(mixed, grad_feed, ((0,), (0,)))
    split_halves(grad_ref, parity, units, mine_ref, theirs_ref)


def put_gains(ref, at, value):
    top = value.astype(bf16)
    count = value.shape[0]
    ref[at : at + count, :] = top
    ref[at + count : at + 2 * count, :] = (value - top.astype(f32)).astype(bf16)


def post_kernel(ins, outs, scratch):
    (place_ref, tok_ref, own_ref, parts, kraw_ref, gains_ref, qk_gain_ref, cos_ref, sin_ref,
     normed_ref, gq_ref, full_ref, ghidden_ref, qgain_ref, mix_ref, pre_ref, post_ref) = ins
    tgrad_ref, mine_ref, theirs_ref, terms_ref = outs
    back_ref, grad_ref, sums_ref = scratch
    order, _, _, parity = scalars(place_ref)
    head_dim = kraw_ref.shape[1]
    query_width = gq_ref.shape[1]
    rows = normed_ref.shape[0] // 2
    half = mine_ref.shape[1]
    total = own_ref[...]
    for k in range(len(parts)):
        total = total + parts[k][...].astype(f32)
    rotated = rope_back(total[:, :head_dim], cos_ref[...], sin_ref[...])
    grad_key, key_gain = norm_back_rows(
        kraw_ref[...], qk_gain_ref[1:2, :], rotated
    )
    back_ref[:, :query_width] = gq_ref[...]
    back_ref[:, query_width : query_width + head_dim] = grad_key.astype(bf16)
    back_ref[:, query_width + head_dim :] = total[:, head_dim:].astype(bf16)
    grad_ref[...] = dot(normed_ref[...], back_ref[...], ((0,), (0,)))
    left = pl.multiple_of(parity * half, 128)
    right = pl.multiple_of((1 - parity) * half, 128)
    mine_ref[...] = grad_ref[:, pl.ds(left, half)]
    theirs_ref[...] = grad_ref[:, pl.ds(right, half)].astype(bf16)
    grad_normed = dot(back_ref[...], full_ref[...], ((1,), (1,)))
    part, in_gain = norm_back_rows(
        get_rows(tok_ref, order), gains_ref[0:1, :], grad_normed
    )
    grads = ghidden_ref[...] + part
    put_rows(tgrad_ref, order, grads[:rows], grads[rows:])
    sums_ref[...] = jnp.zeros(sums_ref.shape, f32)
    for row, value in enumerate(
        (in_gain, mix_ref[...], pre_ref[...], post_ref[...], qgain_ref[...], key_gain)
    ):
        sums_ref[row : row + 1, : value.shape[1]] = value
    put_gains(terms_ref, 0, sums_ref[...])


def late_pack_kernel(ins, outs, scratch):
    place_ref, mine_ref, other_ref, terms_ref = ins
    fsdp_place = place_ref[1]
    size = len(outs)
    shard = mine_ref.shape[0] // size
    for k in range(size):
        at = pl.multiple_of(lax.rem(fsdp_place + size - k, size) * shard, 16)
        chunk = mine_ref[pl.ds(at, shard), :] + other_ref[pl.ds(at, shard), :].astype(f32)
        outs[k][:shard, :] = chunk.astype(bf16)
        outs[k][shard:, :] = terms_ref[...]


def late_sum_kernel(ins, outs, scratch):
    (out_ref,) = outs
    total = ins[0][...].astype(f32)
    for ref in ins[1:]:
        total = total + ref[...].astype(f32)
    rows = total.shape[0] - 16
    out_ref[:rows, :] = total[:rows].astype(bf16)
    put_gains(out_ref, rows, total[rows : rows + 8] + total[rows + 8 :])


def late_last_kernel(ins, outs, scratch):
    place_ref, mine_ref, other_ref = ins
    q_ref, k_ref, v_ref, wide_ref, narrow_ref = outs
    (full_ref,) = scratch
    parity = place_ref[2]
    fsdp_place = place_ref[1]
    rows, half = q_ref.shape[0], mine_ref.shape[1]
    left = pl.multiple_of(parity * half, 128)
    right = pl.multiple_of((1 - parity) * half, 128)
    full_ref[:, pl.ds(left, half)] = mine_ref[:rows, :].astype(f32)
    full_ref[:, pl.ds(right, half)] = other_ref[:rows, :].astype(f32)
    width, head_dim = q_ref.shape[1], k_ref.shape[1]
    q_ref[...] = full_ref[:, :width]
    k_ref[...] = full_ref[:, width : width + head_dim]
    v_ref[...] = full_ref[:, width + head_dim :]
    both = mine_ref[rows:, :].astype(f32) + other_ref[rows:, :].astype(f32)
    sums = both[:8] + both[8:]
    for ref in (wide_ref, narrow_ref):
        cols = ref.shape[1]
        ref[...] = pltpu.roll(sums, lax.rem(half - fsdp_place * cols, half), 1)[:, :cols]


def early_pack_kernel(ins, outs, scratch):
    place_ref, mine_ref, other_ref, parts = ins
    (all_ref,) = scratch
    base = mine_ref.shape[0]
    all_ref[:base, :] = (mine_ref[...] + other_ref[...].astype(f32)).astype(bf16)
    total = parts[0][...].astype(f32)
    for ref in parts[1:]:
        total = total + ref[...].astype(f32)
    all_ref[base:, :] = total.astype(bf16)
    rows = outs[0].shape[0]
    chip_place = lax.div(place_ref[0], 2)
    base = chip_place if len(outs) == 4 else lax.rem(chip_place, 2)
    for k, ref in enumerate(outs):
        at = pl.multiple_of(lax.bitwise_xor(base, k) * rows, 16)
        ref[...] = all_ref[pl.ds(at, rows), :]


def early_last_kernel(ins, outs, scratch):
    place_ref, mine, other = ins
    gate_ref, up_ref, down_ref, out_ref = outs
    mine_ref, other_ref = scratch
    parity = place_ref[2]
    chip_place = lax.div(place_ref[0], 2)
    rows = mine[0].shape[0]
    for k in range(len(mine)):
        at = 0 if len(mine) == 1 else pl.multiple_of(lax.bitwise_xor(chip_place, k) * rows, 16)
        mine_ref[pl.ds(at, rows), :] = mine[k][...]
        other_ref[pl.ds(at, rows), :] = other[k][...]
    half = down_ref.shape[0] // 2
    out_half = out_ref.shape[0] // 2
    for ref, side in ((mine_ref, parity), (other_ref, 1 - parity)):
        cols = pl.multiple_of(side * half, 128)
        gate_ref[:, pl.ds(cols, half)] = ref[:half, :].astype(f32).T
        up_ref[:, pl.ds(cols, half)] = ref[half : 2 * half, :].astype(f32).T
        at = pl.multiple_of(side * half, 16)
        down_ref[pl.ds(at, half), :] = ref[2 * half : 3 * half, :].astype(f32)
        at = pl.multiple_of(side * out_half, 16)
        out_ref[pl.ds(at, out_half), :] = ref[3 * half :, :].astype(f32)


def run_kernel(kernel, args, outs, scratch=()):
    vmem = pl.BlockSpec(memory_space=pltpu.VMEM)
    smem = pl.BlockSpec(memory_space=pltpu.SMEM)
    flat, in_tree = jax.tree.flatten(args)
    shapes = jax.tree.map(
        lambda o: jax.ShapeDtypeStruct(*o), outs, is_leaf=lambda o: not isinstance(o[0][0], tuple)
    )
    flat_out, out_tree = jax.tree.flatten(shapes)

    def wrapped(*refs):
        ins = jax.tree.unflatten(in_tree, refs[: len(flat)])
        targets = jax.tree.unflatten(out_tree, refs[len(flat) : len(flat) + len(flat_out)])
        kernel(ins, targets, refs[len(flat) + len(flat_out) :])

    call = pl.pallas_call(
        wrapped,
        in_specs=[smem if a.ndim == 1 else vmem for a in flat],
        out_specs=[vmem for _ in flat_out],
        out_shape=flat_out,
        scratch_shapes=[pltpu.VMEM(s, d) for s, d in scratch],
        compiler_params=pltpu.CompilerParams(vmem_limit_bytes=56 * 2**20),
    )
    return jax.tree.unflatten(out_tree, call(*flat))


def make_body(fsdp_size, ctx_size):
    chips = ctx_size // 2

    def from_peer(x, axis, offset):
        size = fsdp_size if axis == "fsdp" else ctx_size
        return lax.ppermute(x, axis, [((i + offset) % size, i) for i in range(size)])

    def with_partner(x, bit=1):
        return lax.ppermute(x, "ctx", [(i, i ^ bit) for i in range(ctx_size)])

    def others_fsdp(x):
        return [from_peer(x, "fsdp", k) for k in range(1, fsdp_size)]

    def with_partners(parts):
        return [with_partner(p) for p in parts]

    def after(x, *others):
        return lax.optimization_barrier((x,) + others)[0]

    def pick(x, at, axis=0):
        return lax.dynamic_index_in_dim(x, at, axis, keepdims=False)

    def sum_chips(parts, ctx_place):
        if len(parts) == 4:
            far = with_partner(parts[3], 2)
            near = with_partner(parts[1], 2)
            passed = (parts[2].astype(f32) + far.astype(f32)).astype(bf16)
            across = with_partner(passed, 4)
            total = parts[0].astype(f32) + near.astype(f32) + across.astype(f32)
            total = total.astype(bf16)
            second = with_partner(total, 4)
            first = with_partner(total, 2)
            return [total, first, second, with_partner(second, 2)]
        keep, send = parts
        width = keep.shape[1]
        steps = []
        bit = 2
        while bit < ctx_size:
            side = (ctx_place // bit) % 2
            sent = with_partner(send, bit)
            total = (keep.astype(f32) + sent.astype(f32)).astype(bf16)
            if 2 * bit < ctx_size:
                halves = total.reshape(2, -1, width)
                ahead = (ctx_place // (2 * bit)) % 2
                keep, send = pick(halves, ahead), pick(halves, 1 - ahead)
            steps.append((bit, side))
            bit *= 2
        for bit, side in reversed(steps):
            other = with_partner(total, bit)
            first = jnp.where(side == 0, total, other)
            second = jnp.where(side == 0, other, total)
            total = jnp.concatenate([first, second], axis=0)
        return [total]

    def body(
        tokens,
        cotangent,
        positions,
        block_order,
        query_weight,
        key_weight,
        value_weight,
        output_weight,
        gate_weight,
        up_weight,
        down_weight,
        input_gain,
        query_gain,
        key_gain,
        mixer_gain,
        prefeed_gain,
        postfeed_gain,
    ):
        row_count = tokens.shape[1]
        width = tokens.shape[2]
        block_rows = row_count // 2
        head_dim = key_weight.shape[1]
        query_width = query_weight.shape[1]
        head_count = query_width // head_dim
        proj_width = query_width + 2 * head_dim
        proj_half = proj_width // 2
        shard_rows = query_weight.shape[0]
        out_rows = output_weight.shape[0]
        hidden_rows = down_weight.shape[0]
        half_rows = hidden_rows // 2
        ctx_place = lax.axis_index("ctx")
        fsdp_place = lax.axis_index("fsdp")
        parity = ctx_place % 2

        place = jnp.concatenate(
            [jnp.stack([ctx_place, fsdp_place, parity]).astype(jnp.int32), block_order]
        )
        tok, cot = tokens[0], cotangent[0]
        rows_width = (row_count, width)
        (proj_send,) = run_kernel(
            first_kernel,
            (parity.astype(jnp.int32).reshape(1), query_weight, key_weight, value_weight),
            (((shard_rows, proj_half), bf16),),
        )
        proj_mine = others_fsdp(proj_send)
        gain_cols, head_cols = input_gain.shape[0], query_gain.shape[0]
        gains_own = jnp.stack(
            [g.astype(f32) for g in (input_gain, mixer_gain, prefeed_gain, postfeed_gain)]
            + [jnp.pad(g.astype(f32), (0, gain_cols - head_cols)) for g in (query_gain, key_gain)]
        )
        gain_parts = [gains_own] + others_fsdp(gains_own)
        gain_full = jnp.zeros((fsdp_size,) + gains_own.shape, f32)
        for k, part in enumerate(gain_parts):
            gain_full = lax.dynamic_update_index_in_dim(
                gain_full, part, (fsdp_place + k) % fsdp_size, 0
            )
        gain_full = gain_full.transpose(1, 0, 2)
        gains = gain_full[:4].reshape(4, width)
        qk_gains = gain_full[4:, :, :head_cols].reshape(2, head_dim)

        frequency = rope_base ** (-2.0 * jnp.arange(head_dim // 2, dtype=f32) / head_dim)
        cosines, sine_terms, query_last, query_first, key_ids = run_kernel(
            table_kernel,
            (place, positions[0][:, None], frequency[None]),
            (
                ((row_count, head_dim // 2), f32),
                ((row_count, head_dim // 2), f32),
                ((row_count, 1), jnp.int32),
                ((row_count, 1), jnp.int32),
                ((2, 1, ctx_size * block_rows), jnp.int32),
            ),
        )
        proj_ready = list(
            lax.optimization_barrier((*proj_mine, gains, qk_gains, cosines, sine_terms))
        )[: fsdp_size - 1]
        proj_theirs = with_partners(proj_ready)

        out_half, pair_half, down_half = run_kernel(
            halves_kernel,
            (place, output_weight, gate_weight, up_weight, down_weight),
            (
                ((out_rows // 2, width), bf16),
                ((width, 2 * half_rows), bf16),
                ((half_rows, width), bf16),
            ),
        )
        pair_half = after(pair_half, *proj_mine)
        out_mine = others_fsdp(out_half)
        pair_mine = others_fsdp(pair_half)

        normed, query_rows, own_pair, query_raw, key_raw, proj_full = run_kernel(
            pre_kernel,
            (place, tok, gains, qk_gains, cosines, sine_terms,
             query_weight, key_weight, value_weight, proj_ready, proj_theirs),
            (
                (rows_width, bf16),
                ((row_count, query_width), bf16),
                ((row_count, 2 * head_dim), bf16),
                ((row_count, query_width), f32),
                ((row_count, head_dim), f32),
                ((fsdp_size * shard_rows, proj_width), bf16),
            ),
        )
        kv_mine = [own_pair] + [from_peer(own_pair, "ctx", 2 * k) for k in range(1, chips)]
        kv_theirs = [with_partner(own_pair)] + with_partners(kv_mine[1:])
        down_mine = others_fsdp(after(down_half, own_pair))
        out_theirs = with_partners(out_mine)
        pair_ready = list(lax.optimization_barrier((*pair_mine, *kv_mine[1:])))[: fsdp_size - 1]
        pair_theirs = with_partners(pair_ready)
        down_theirs = with_partners(down_mine)
        attended, log_total, key_pairs, output_full, projected, hidden, feed_in = run_kernel(
            attend_kernel,
            (place, tok, query_rows, kv_mine, kv_theirs, query_last, query_first, key_ids,
             output_weight, out_mine, out_theirs, gains),
            (
                ((row_count, query_width), bf16),
                ((2, head_count * block_rows, 1), f32),
                ((2, ctx_size * block_rows, 2 * head_dim), bf16),
                ((fsdp_size * out_rows, width), bf16),
                (rows_width, f32),
                (rows_width, f32),
                (rows_width, bf16),
            ),
        )
        feed_all = [feed_in] + others_fsdp(feed_in)
        (output, grad_feed, grad_hidden, grad_attended, gmix, gpre, gpost,
         out_own, out_other) = run_kernel(
            feed_kernel,
            (place, cot, feed_in, hidden, projected, output_full, gains,
             attended, gate_weight, up_weight, down_weight,
             pair_ready + pair_theirs, down_mine + down_theirs),
            (
                (rows_width, f32),
                (rows_width, bf16),
                (rows_width, f32),
                ((row_count, query_width), bf16),
                ((1, width), f32),
                ((1, width), f32),
                ((1, width), f32),
                ((fsdp_size * out_rows // 2, width), f32),
                ((fsdp_size * out_rows // 2, width), bf16),
            ),
            (((row_count, fsdp_size * hidden_rows), f32),) * 2
            + (((fsdp_size * out_rows, width), f32),),
        )
        out_other = with_partner(out_other)
        grad_all = [grad_feed] + others_fsdp(grad_feed)
        query_back, pairs_mine, pairs_theirs, gqgain = run_kernel(
            attend_back_kernel,
            (query_rows, key_pairs, grad_attended, attended, log_total,
             query_last, query_first, key_ids, query_raw, qk_gains, cosines, sine_terms),
            (
                ((row_count, query_width), bf16),
                ((chips, row_count, 2 * head_dim), f32),
                ((chips, row_count, 2 * head_dim), bf16),
                ((1, head_dim), f32),
            ),
        )

        pairs_other = with_partner(pairs_theirs)
        chip_part = pairs_mine + pairs_other.astype(f32)
        chip_send = [chip_part[chips - k].astype(bf16) for k in range(1, chips)]
        chip_own = chip_part[0]
        back_parts = [from_peer(chip_send[k - 1], "ctx", 2 * k) for k in range(1, chips)]

        feed_rows = 3 * half_rows
        early_mine, early_theirs, out_chunks = run_kernel(
            weight_kernel,
            (place, feed_all, grad_all, gate_weight, up_weight, down_weight, out_own, out_other),
            (
                ((feed_rows, width), f32),
                ((feed_rows, width), bf16),
                [((out_rows // 2, width), bf16)] * fsdp_size,
            ),
            (((2 * feed_rows, width), f32),),
        )
        out_parts = [out_chunks[0]] + [
            from_peer(out_chunks[k], "fsdp", k) for k in range(1, fsdp_size)
        ]
        early_rows = feed_rows + out_rows // 2
        pieces = 4 if chips == 4 else 2
        early_parts = run_kernel(
            early_pack_kernel,
            (place, early_mine, with_partner(early_theirs), out_parts),
            [((early_rows // pieces, width), bf16)] * pieces,
            (((early_rows, width), bf16),),
        )
        early = sum_chips(early_parts, ctx_place)
        gate_grad, up_grad, down_grad, out_grad = run_kernel(
            early_last_kernel,
            (place, early, with_partners(early)),
            (
                ((width, hidden_rows), f32),
                ((width, hidden_rows), f32),
                ((hidden_rows, width), f32),
                ((out_rows, width), f32),
            ),
            (((early_rows, width), bf16),) * 2,
        )

        tokens_grad, late_mine, late_theirs, late_terms = run_kernel(
            post_kernel,
            (place, tok, chip_own, back_parts, key_raw, gains, qk_gains,
             cosines, sine_terms, normed, query_back, proj_full, grad_hidden,
             gqgain, gmix, gpre, gpost),
            (
                (rows_width, f32),
                ((width, proj_half), f32),
                ((width, proj_half), bf16),
                ((16, proj_half), bf16),
            ),
            (
                ((row_count, proj_width), bf16),
                ((width, proj_width), f32),
                ((8, proj_half), f32),
            ),
        )
        late_shape = ((shard_rows + 16, proj_half), bf16)
        late_chunks = run_kernel(
            late_pack_kernel,
            (place, late_mine, with_partner(late_theirs), late_terms),
            [late_shape] * fsdp_size,
        )
        late_parts = [late_chunks[0]] + [
            from_peer(late_chunks[k], "fsdp", k) for k in range(1, fsdp_size)
        ]
        (late,) = run_kernel(late_sum_kernel, late_parts, [late_shape])
        bit = 2
        while bit < ctx_size:
            other = with_partner(late, bit)
            (late,) = run_kernel(late_sum_kernel, [late, other], [late_shape])
            bit *= 2
        query_grad, key_grad, value_grad, wide_sums, narrow_sums = run_kernel(
            late_last_kernel,
            (place, late, with_partner(late)),
            (
                ((shard_rows, query_width), f32),
                ((shard_rows, head_dim), f32),
                ((shard_rows, head_dim), f32),
                ((8, gain_cols), f32),
                ((8, head_cols), f32),
            ),
            (((shard_rows, proj_width), f32),),
        )
        return (
            output[None],
            tokens_grad[None],
            query_grad,
            key_grad,
            value_grad,
            out_grad,
            gate_grad,
            up_grad,
            down_grad,
            wide_sums[0],
            narrow_sums[4],
            narrow_sums[5],
            wide_sums[1],
            wide_sums[2],
            wide_sums[3],
        )

    return body


def solution(mesh):
    in_specs = (
        P("fsdp", "ctx", None),
        P("fsdp", "ctx", None),
        P("fsdp", "ctx"),
        P(),
        P("fsdp", None),
        P("fsdp", None),
        P("fsdp", None),
        P("fsdp", None),
        P(None, "fsdp"),
        P(None, "fsdp"),
        P("fsdp", None),
        P("fsdp"),
        P("fsdp"),
        P("fsdp"),
        P("fsdp"),
        P("fsdp"),
        P("fsdp"),
    )
    out_specs = (
        P("fsdp", "ctx", None),
        P("fsdp", "ctx", None),
        P("fsdp", None),
        P("fsdp", None),
        P("fsdp", None),
        P("fsdp", None),
        P(None, "fsdp"),
        P(None, "fsdp"),
        P("fsdp", None),
        P("fsdp"),
        P("fsdp"),
        P("fsdp"),
        P("fsdp"),
        P("fsdp"),
        P("fsdp"),
    )
    inner = make_body(mesh.shape["fsdp"], mesh.shape["ctx"])

    return jax.shard_map(inner, mesh=mesh, in_specs=in_specs, out_specs=out_specs, check_vma=False)
```

```python
import jax
import jax.numpy as jnp
from jax import lax
from jax.experimental import pallas as pl
from jax.experimental.pallas import tpu as pltpu
from jax.sharding import PartitionSpec as P


norm_eps = 1e-06
rope_base = 1000000.0
tanh_coef = 0.7978845608028654
cubic_coef = 0.044715
bf16 = jnp.bfloat16
f32 = jnp.float32


def norm_factor(inputs):
    return lax.rsqrt(jnp.mean(inputs * inputs, axis=-1, keepdims=True) + norm_eps)


def norm_apply(inputs, gain):
    return inputs * norm_factor(inputs) * (1.0 + gain)


def norm_back(inputs, gain, upstream):
    factor = norm_factor(inputs)
    normal = inputs * factor
    weighted = upstream * (1.0 + gain)
    grad_inputs = factor * (weighted - normal * jnp.mean(normal * weighted, axis=-1, keepdims=True))
    grad_gain = jnp.sum((upstream * normal).reshape(-1, inputs.shape[-1]), axis=0)
    return (grad_inputs, grad_gain)


def rope_apply(inputs, cosines, sine_terms):
    half_width = inputs.shape[-1] // 2
    first_half = inputs[..., :half_width]
    second_half = inputs[..., half_width:]
    return jnp.concatenate(
        [
            first_half * cosines - second_half * sine_terms,
            second_half * cosines + first_half * sine_terms,
        ],
        axis=-1,
    )


def rope_back(upstream, cosines, sine_terms):
    half_width = upstream.shape[-1] // 2
    first_half = upstream[..., :half_width]
    second_half = upstream[..., half_width:]
    return jnp.concatenate(
        [
            first_half * cosines + second_half * sine_terms,
            second_half * cosines - first_half * sine_terms,
        ],
        axis=-1,
    )


def gelu_parts(inputs):
    tanh_part = jnp.tanh(tanh_coef * (inputs + cubic_coef * inputs * inputs * inputs))
    activated = 0.5 * inputs * (1.0 + tanh_part)
    gelu_slope = 0.5 * (1.0 + tanh_part) + 0.5 * inputs * (
        1.0 - tanh_part * tanh_part
    ) * tanh_coef * (1.0 + 3.0 * cubic_coef * inputs * inputs)
    return (activated, gelu_slope)


def dot(a, b, dims):
    return lax.dot_general(a, b, (dims, ((), ())), preferred_element_type=f32)


def scalars(place_ref):
    ctx_place, fsdp_place, parity = place_ref[0], place_ref[1], place_ref[2]
    first, second = place_ref[3 + 2 * ctx_place], place_ref[4 + 2 * ctx_place]
    return (first > second).astype(jnp.int32), ctx_place, fsdp_place, parity


def put_rows(ref, order, low, high):
    rows = low.shape[0]
    at = pl.multiple_of(order * rows, rows)
    other = pl.multiple_of((1 - order) * rows, rows)
    ref[pl.ds(at, rows), :] = low
    ref[pl.ds(other, rows), :] = high


def get_rows(ref, order):
    rows = ref.shape[0] // 2
    at = pl.multiple_of(order * rows, rows)
    other = pl.multiple_of((1 - order) * rows, rows)
    return jnp.concatenate([ref[pl.ds(at, rows), :], ref[pl.ds(other, rows), :]], axis=0)


def rope_norm(raw, gain, cosines, sine_terms):
    return rope_apply(norm_apply(raw, gain), cosines, sine_terms)


def first_kernel(ins, outs, scratch):
    parity_ref, qw_ref, kw_ref, vw_ref = ins
    (send_ref,) = outs
    parity = parity_ref[0]
    half = send_ref.shape[1]
    rest = qw_ref.shape[1] - half
    head_dim = kw_ref.shape[1]

    @pl.when(parity == 0)
    def _():
        send_ref[...] = qw_ref[:, :half]

    @pl.when(parity == 1)
    def _():
        send_ref[:, :rest] = qw_ref[:, half:]
        send_ref[:, rest : rest + head_dim] = kw_ref[...]
        send_ref[:, rest + head_dim :] = vw_ref[...]


def gains_kernel(ins, outs, scratch):
    (gains_ref,) = outs
    gains_ref[...] = jnp.zeros(gains_ref.shape, f32)
    for row, ref in enumerate(ins):
        gains_ref[row, : ref.shape[0]] = ref[...].astype(f32)


def halves_kernel(ins, outs, scratch):
    place_ref, outw_ref, gate_ref, up_ref, down_ref = ins
    out_ref, pair_ref, dn_ref = outs
    parity = place_ref[2]
    half, out_half = dn_ref.shape[0], out_ref.shape[0]
    cols = pl.multiple_of(parity * half, 128)
    pair_ref[:, :half] = gate_ref[:, pl.ds(cols, half)]
    pair_ref[:, half:] = up_ref[:, pl.ds(cols, half)]
    dn_ref[...] = down_ref[pl.ds(pl.multiple_of(parity * half, 16), half), :]
    out_ref[...] = outw_ref[pl.ds(pl.multiple_of(parity * out_half, 16), out_half), :]


def table_kernel(ins, outs, scratch):
    place_ref, pos_ref, freq_ref = ins
    cos_ref, sin_ref, last_ref, first_ref, ids_ref = outs
    order, ctx_place, _, _ = scalars(place_ref)
    rows = pos_ref.shape[0] // 2
    size = ids_ref.shape[2] // rows
    places = get_rows(pos_ref, order)
    angles = places.astype(f32) * freq_ref[...]
    cos_ref[...] = jnp.cos(angles)
    sin_ref[...] = jnp.sin(angles)

    def blocks(at):
        one, two = place_ref[3 + 2 * at], place_ref[4 + 2 * at]
        return jnp.minimum(one, two), jnp.maximum(one, two)

    own = blocks(ctx_place)
    column = lax.broadcasted_iota(jnp.int32, (rows, 1), 0)
    line = lax.broadcasted_iota(jnp.int32, (1, rows), 1)
    for part in range(2):
        index = column + own[part] * rows
        at = slice(part * rows, (part + 1) * rows)
        last_ref[at, :] = index
        first_ref[at, :] = index - places[at]
    for slot in range(size):
        base = ctx_place if slot < size // 2 else ctx_place + 1 - 2 * place_ref[2]
        source = blocks(lax.rem(base + 2 * (slot % (size // 2)), size))
        for part in range(2):
            ids_ref[part, :, slot * rows : (slot + 1) * rows] = line + source[part] * rows


def pre_kernel(ins, outs, scratch):
    place_ref, tok_ref, gains_ref, qk_gain_ref, cos_ref, sin_ref, qw_ref, kw_ref, vw_ref, mine, theirs = ins
    normed_ref, q_ref, kv_ref, qraw_ref, kraw_ref, full_ref = outs
    order, _, fsdp_place, parity = scalars(place_ref)
    count = len(mine)
    size = count + 1
    shard, half = mine[0].shape
    query_width, head_dim = qw_ref.shape[1], kw_ref.shape[1]
    gain_in, gain_q, gain_k = gains_ref[0:1, :], qk_gain_ref[0:1, :], qk_gain_ref[1:2, :]
    at = pl.multiple_of(fsdp_place * shard, 16)
    full_ref[pl.ds(at, shard), :query_width] = qw_ref[...]
    full_ref[pl.ds(at, shard), query_width : query_width + head_dim] = kw_ref[...]
    full_ref[pl.ds(at, shard), query_width + head_dim :] = vw_ref[...]
    left = pl.multiple_of(parity * half, 128)
    right = pl.multiple_of((1 - parity) * half, 128)
    for k in range(count):
        at = pl.multiple_of(lax.rem(fsdp_place + k + 1, size) * shard, 16)
        full_ref[pl.ds(at, shard), pl.ds(left, half)] = mine[k][...]
        full_ref[pl.ds(at, shard), pl.ds(right, half)] = theirs[k][...]
    residual = get_rows(tok_ref, order)
    normed = norm_apply(residual, gain_in).astype(bf16)
    normed_ref[...] = normed
    cosines, sine_terms = cos_ref[...], sin_ref[...]
    for at in range(0, query_width, head_dim):
        raw = dot(normed, full_ref[:, at : at + head_dim], ((1,), (0,)))
        qraw_ref[:, at : at + head_dim] = raw
        q_ref[:, at : at + head_dim] = rope_norm(
            raw, gain_q, cosines, sine_terms
        ).astype(bf16)
    raw = dot(normed, full_ref[:, query_width : query_width + head_dim], ((1,), (0,)))
    kraw_ref[...] = raw
    kv_ref[:, :head_dim] = rope_norm(raw, gain_k, cosines, sine_terms).astype(bf16)
    kv_ref[:, head_dim:] = dot(
        normed, full_ref[:, query_width + head_dim :], ((1,), (0,))
    ).astype(bf16)


def mask_bias(ids, last, first):
    return jnp.where((ids <= last) & (ids >= first), 0.0, -1e30)


def attend_kernel(ins, outs, scratch):
    (place_ref, tok_ref, q_ref, mine, theirs, last_ref, first_ref, ids_ref,
     outw_ref, outp, outt, gains_ref) = ins
    att_ref, lse_ref, kv_ref, outfull_ref, projected_ref, hidden_ref, feed_ref = outs
    order, _, fsdp_place, parity = scalars(place_ref)
    chips = len(mine)
    rows = mine[0].shape[0] // 2
    head_dim = mine[0].shape[1] // 2
    heads = q_ref.shape[1] // head_dim
    scale = head_dim ** (-0.5)
    size = len(outp) + 1
    shard = outw_ref.shape[0]
    half = shard // 2
    at = pl.multiple_of(fsdp_place * shard, 16)
    outfull_ref[pl.ds(at, shard), :] = outw_ref[...]
    for k in range(1, size):
        at = lax.rem(fsdp_place + k, size) * shard
        left = pl.multiple_of(at + parity * half, 16)
        right = pl.multiple_of(at + (1 - parity) * half, 16)
        outfull_ref[pl.ds(left, half), :] = outp[k - 1][...]
        outfull_ref[pl.ds(right, half), :] = outt[k - 1][...]
    for part in range(2):
        own = slice(part * rows, (part + 1) * rows)
        for k in range(chips):
            kv_ref[part, k * rows : (k + 1) * rows, :] = mine[k][own, :]
            kv_ref[part, (chips + k) * rows : (chips + k + 1) * rows, :] = theirs[k][own, :]
        queries = jnp.concatenate(
            [q_ref[own, h * head_dim : (h + 1) * head_dim] for h in range(heads)], axis=0
        )
        scores = dot(queries, kv_ref[part, :, :head_dim], ((1,), (1,))) * scale
        bias = mask_bias(ids_ref[part], last_ref[own, :], first_ref[own, :])
        pieces = []
        for h in range(heads):
            one = scores[h * rows : (h + 1) * rows] + bias
            top = jnp.max(one, axis=1, keepdims=True)
            weights = jnp.exp(one - top)
            lse = top + jnp.log(jnp.sum(weights, axis=1, keepdims=True))
            lse_ref[part, h * rows : (h + 1) * rows, :] = lse
            pieces.append((weights * jnp.exp(top - lse)).astype(bf16))
        probs = jnp.concatenate(pieces, axis=0)
        attended = dot(probs, kv_ref[part, :, head_dim:], ((1,), (0,))).astype(bf16)
        for h in range(heads):
            att_ref[own, h * head_dim : (h + 1) * head_dim] = attended[h * rows : (h + 1) * rows]
    projected = dot(att_ref[...], outfull_ref[...], ((1,), (0,)))
    projected_ref[...] = projected
    hidden = get_rows(tok_ref, order) + norm_apply(projected, gains_ref[1:2, :])
    hidden_ref[...] = hidden
    feed_ref[...] = norm_apply(hidden, gains_ref[2:3, :]).astype(bf16)


def norm_back_rows(inputs, gain, upstream):
    grad, grad_gain = norm_back(inputs, gain, upstream)
    return grad, grad_gain[None, :]


def split_halves(ref, parity, size, mine_ref, theirs_ref):
    half = size // 2
    for k in range(ref.shape[0] // size):
        mine = pl.multiple_of(k * size + parity * half, 16)
        theirs = pl.multiple_of(k * size + (1 - parity) * half, 16)
        mine_ref[k * half : (k + 1) * half, :] = ref[pl.ds(mine, half), :]
        theirs_ref[k * half : (k + 1) * half, :] = ref[pl.ds(theirs, half), :].astype(bf16)


def feed_kernel(ins, outs, scratch):
    (place_ref, cot_ref, feed_ref, hidden_ref, projected_ref, outfull_ref, gains_ref,
     att_ref, gate_ref, up_ref, down_ref, pair_refs, down_refs) = ins
    (out_ref, gfeed_ref, ghidden_ref, gatt_ref, mix_ref, pre_ref, post_ref,
     omine_ref, otheirs_ref) = outs
    act_ref, slope_ref, ograd_ref = scratch
    order, _, _, parity = scalars(place_ref)
    rows = feed_ref.shape[0] // 2
    half = pair_refs[0].shape[1] // 2
    pieces = [(lambda: gate_ref[...], lambda: up_ref[...], lambda: down_ref[...], gate_ref.shape[1])]
    for pr, dr in zip(pair_refs, down_refs):
        pieces.append(
            (
                lambda pr=pr: pr[:, :half],
                lambda pr=pr: pr[:, half:],
                lambda dr=dr: dr[...],
                half,
            )
        )
    feed_in = feed_ref[...]
    total = jnp.zeros(hidden_ref.shape, f32)
    at = 0
    for gate, up, down, units in pieces:
        gate_vals = dot(feed_in, gate(), ((1,), (0,)))
        up_vals = dot(feed_in, up(), ((1,), (0,)))
        activated, slope = gelu_parts(gate_vals)
        act_ref[:, at : at + units] = activated
        slope_ref[:, at : at + units] = up_vals * slope
        total = total + dot((activated * up_vals).astype(bf16), down(), ((1,), (0,)))
        at += units
    hidden = hidden_ref[...]
    output = hidden + norm_apply(total, gains_ref[3:4, :])
    put_rows(out_ref, order, output[:rows], output[rows:])
    upstream = get_rows(cot_ref, order)
    grad_feed, post_ref[...] = norm_back_rows(total, gains_ref[3:4, :], upstream)
    grad_feed = grad_feed.astype(bf16)
    gfeed_ref[...] = grad_feed
    back = jnp.zeros(hidden_ref.shape, f32)
    at = 0
    for gate, up, down, units in pieces:
        grad_mixed = dot(grad_feed, down(), ((1,), (1,)))
        grad_gate = (grad_mixed * slope_ref[:, at : at + units]).astype(bf16)
        grad_up = (grad_mixed * act_ref[:, at : at + units]).astype(bf16)
        back = back + dot(grad_gate, gate(), ((1,), (1,))) + dot(grad_up, up(), ((1,), (1,)))
        at += units
    part, pre_ref[...] = norm_back_rows(hidden, gains_ref[2:3, :], back)
    grad_hidden = upstream + part
    ghidden_ref[...] = grad_hidden
    grad_proj, mix_ref[...] = norm_back_rows(projected_ref[...], gains_ref[1:2, :], grad_hidden)
    grad_proj = grad_proj.astype(bf16)
    gatt_ref[...] = dot(grad_proj, outfull_ref[...], ((1,), (1,))).astype(bf16)
    ograd_ref[...] = dot(att_ref[...], grad_proj, ((0,), (0,)))
    units = gate_ref.shape[1]
    shard = ograd_ref.shape[0] // (act_ref.shape[1] // units)
    split_halves(ograd_ref, parity, shard, omine_ref, otheirs_ref)


def attend_back_kernel(ins, outs, scratch):
    (q_ref, kv_ref, gatt_ref, att_ref, lse_ref, last_ref, first_ref, ids_ref,
     qraw_ref, qk_gain_ref, cos_ref, sin_ref) = ins
    gq_ref, mine_ref, theirs_ref, qgain_ref = outs
    chips, rows, head_dim = mine_ref.shape[0], mine_ref.shape[1] // 2, mine_ref.shape[2] // 2
    heads = q_ref.shape[1] // head_dim
    scale = head_dim ** (-0.5)
    gain_total = jnp.zeros(qgain_ref.shape, f32)
    for part in range(2):
        own = slice(part * rows, (part + 1) * rows)

        def stacked(ref):
            return jnp.concatenate(
                [ref[own, h * head_dim : (h + 1) * head_dim] for h in range(heads)], axis=0
            )

        queries, upstream, attended = stacked(q_ref), stacked(gatt_ref), stacked(att_ref)
        keys, values = kv_ref[part, :, :head_dim], kv_ref[part, :, head_dim:]
        delta = jnp.sum(upstream.astype(f32) * attended.astype(f32), axis=1, keepdims=True)
        scores = dot(queries, keys, ((1,), (1,))) * scale
        grad_probs = dot(upstream, values, ((1,), (1,)))
        bias = mask_bias(ids_ref[part], last_ref[own, :], first_ref[own, :])
        prob_list, score_list = [], []
        for h in range(heads):
            one = slice(h * rows, (h + 1) * rows)
            probs = jnp.exp(scores[one] + bias - lse_ref[part, one, :])
            prob_list.append(probs.astype(bf16))
            score_list.append((probs * (grad_probs[one] - delta[one]) * scale).astype(bf16))
        probs = jnp.concatenate(prob_list, axis=0)
        grad_scores = jnp.concatenate(score_list, axis=0)
        grad_keys = dot(grad_scores, queries, ((0,), (0,)))
        grad_values = dot(probs, upstream, ((0,), (0,)))
        for k in range(chips):
            for ref, base, kind in ((mine_ref, 0, f32), (theirs_ref, chips, bf16)):
                piece = slice((base + k) * rows, (base + k + 1) * rows)
                ref[k, own, :head_dim] = grad_keys[piece].astype(kind)
                ref[k, own, head_dim:] = grad_values[piece].astype(kind)
        grad_queries = dot(grad_scores, keys, ((1,), (0,)))
        cosines, sine_terms = cos_ref[own, :], sin_ref[own, :]
        for h in range(heads):
            cols = slice(h * head_dim, (h + 1) * head_dim)
            rotated = rope_back(grad_queries[h * rows : (h + 1) * rows], cosines, sine_terms)
            grad_raw, grad_gain = norm_back_rows(
                qraw_ref[own, cols], qk_gain_ref[0:1, :], rotated
            )
            gq_ref[own, cols] = grad_raw.astype(bf16)
            gain_total = gain_total + grad_gain
    qgain_ref[...] = gain_total


def weight_kernel(ins, outs, scratch):
    place_ref, feed_refs, grad_refs, gate_ref, up_ref, down_ref, omine_ref, oother_ref = ins
    mine_ref, theirs_ref, chunks = outs
    fsdp_place, size = place_ref[1], len(chunks)
    shard = chunks[0].shape[0]
    for k in range(size):
        at = pl.multiple_of(lax.rem(fsdp_place + size - k, size) * shard, 16)
        chunk = omine_ref[pl.ds(at, shard), :] + oother_ref[pl.ds(at, shard), :].astype(f32)
        chunks[k][...] = chunk.astype(bf16)
    (grad_ref,) = scratch
    parity = place_ref[2]
    units = down_ref.shape[0]
    feed_in = jnp.concatenate([ref[...] for ref in feed_refs], axis=0)
    grad_feed = jnp.concatenate([ref[...] for ref in grad_refs], axis=0)
    gate_vals = dot(feed_in, gate_ref[...], ((1,), (0,)))
    up_vals = dot(feed_in, up_ref[...], ((1,), (0,)))
    activated, slope = gelu_parts(gate_vals)
    mixed = (activated * up_vals).astype(bf16)
    grad_mixed = dot(grad_feed, down_ref[...], ((1,), (1,)))
    grad_gate = (grad_mixed * up_vals * slope).astype(bf16)
    grad_up = (grad_mixed * activated).astype(bf16)
    grad_ref[0:units, :] = dot(grad_gate, feed_in, ((0,), (0,)))
    grad_ref[units : 2 * units, :] = dot(grad_up, feed_in, ((0,), (0,)))
    grad_ref[2 * units : 3 * units, :] = dot(mixed, grad_feed, ((0,), (0,)))
    split_halves(grad_ref, parity, units, mine_ref, theirs_ref)


def put_gains(ref, at, value):
    top = value.astype(bf16)
    count = value.shape[0]
    ref[at : at + count, :] = top
    ref[at + count : at + 2 * count, :] = (value - top.astype(f32)).astype(bf16)


def post_kernel(ins, outs, scratch):
    (place_ref, tok_ref, own_ref, parts, kraw_ref, gains_ref, qk_gain_ref, cos_ref, sin_ref,
     normed_ref, gq_ref, full_ref, ghidden_ref, qgain_ref, mix_ref, pre_ref, post_ref) = ins
    tgrad_ref, mine_ref, theirs_ref, terms_ref = outs
    back_ref, grad_ref, sums_ref = scratch
    order, _, _, parity = scalars(place_ref)
    head_dim = kraw_ref.shape[1]
    query_width = gq_ref.shape[1]
    rows = normed_ref.shape[0] // 2
    half = mine_ref.shape[1]
    total = own_ref[...]
    for k in range(len(parts)):
        total = total + parts[k][...].astype(f32)
    rotated = rope_back(total[:, :head_dim], cos_ref[...], sin_ref[...])
    grad_key, key_gain = norm_back_rows(
        kraw_ref[...], qk_gain_ref[1:2, :], rotated
    )
    back_ref[:, :query_width] = gq_ref[...]
    back_ref[:, query_width : query_width + head_dim] = grad_key.astype(bf16)
    back_ref[:, query_width + head_dim :] = total[:, head_dim:].astype(bf16)
    grad_ref[...] = dot(normed_ref[...], back_ref[...], ((0,), (0,)))
    left = pl.multiple_of(parity * half, 128)
    right = pl.multiple_of((1 - parity) * half, 128)
    mine_ref[...] = grad_ref[:, pl.ds(left, half)]
    theirs_ref[...] = grad_ref[:, pl.ds(right, half)].astype(bf16)
    grad_normed = dot(back_ref[...], full_ref[...], ((1,), (1,)))
    part, in_gain = norm_back_rows(
        get_rows(tok_ref, order), gains_ref[0:1, :], grad_normed
    )
    grads = ghidden_ref[...] + part
    put_rows(tgrad_ref, order, grads[:rows], grads[rows:])
    sums_ref[...] = jnp.zeros(sums_ref.shape, f32)
    for row, value in enumerate(
        (in_gain, mix_ref[...], pre_ref[...], post_ref[...], qgain_ref[...], key_gain)
    ):
        sums_ref[row : row + 1, : value.shape[1]] = value
    put_gains(terms_ref, 0, sums_ref[...])


def late_pack_kernel(ins, outs, scratch):
    place_ref, mine_ref, other_ref, terms_ref = ins
    fsdp_place = place_ref[1]
    size = len(outs)
    shard = mine_ref.shape[0] // size
    for k in range(size):
        at = pl.multiple_of(lax.rem(fsdp_place + size - k, size) * shard, 16)
        chunk = mine_ref[pl.ds(at, shard), :] + other_ref[pl.ds(at, shard), :].astype(f32)
        outs[k][:shard, :] = chunk.astype(bf16)
        outs[k][shard:, :] = terms_ref[...]


def late_sum_kernel(ins, outs, scratch):
    (out_ref,) = outs
    total = ins[0][...].astype(f32)
    for ref in ins[1:]:
        total = total + ref[...].astype(f32)
    rows = total.shape[0] - 16
    out_ref[:rows, :] = total[:rows].astype(bf16)
    put_gains(out_ref, rows, total[rows : rows + 8] + total[rows + 8 :])


def late_last_kernel(ins, outs, scratch):
    place_ref, mine_ref, other_ref = ins
    q_ref, k_ref, v_ref, wide_refs, narrow_refs = outs
    (full_ref,) = scratch
    parity = place_ref[2]
    fsdp_place = place_ref[1]
    rows, half = q_ref.shape[0], mine_ref.shape[1]
    left = pl.multiple_of(parity * half, 128)
    right = pl.multiple_of((1 - parity) * half, 128)
    full_ref[:, pl.ds(left, half)] = mine_ref[:rows, :].astype(f32)
    full_ref[:, pl.ds(right, half)] = other_ref[:rows, :].astype(f32)
    width, head_dim = q_ref.shape[1], k_ref.shape[1]
    q_ref[...] = full_ref[:, :width]
    k_ref[...] = full_ref[:, width : width + head_dim]
    v_ref[...] = full_ref[:, width + head_dim :]
    both = mine_ref[rows:, :].astype(f32) + other_ref[rows:, :].astype(f32)
    sums = both[:8] + both[8:]
    for refs, row in ((wide_refs, 0), (narrow_refs, len(wide_refs))):
        cols = refs[0].shape[0]
        shard = pltpu.roll(sums, lax.rem(half - fsdp_place * cols, half), 1)
        for k, ref in enumerate(refs):
            ref[...] = shard[row + k, :cols]


def early_pack_kernel(ins, outs, scratch):
    place_ref, mine_ref, other_ref, parts = ins
    (all_ref,) = scratch
    base = mine_ref.shape[0]
    all_ref[:base, :] = (mine_ref[...] + other_ref[...].astype(f32)).astype(bf16)
    total = parts[0][...].astype(f32)
    for ref in parts[1:]:
        total = total + ref[...].astype(f32)
    all_ref[base:, :] = total.astype(bf16)
    rows = outs[0].shape[0]
    chip_place = lax.div(place_ref[0], 2)
    base = chip_place if len(outs) == 4 else lax.rem(chip_place, 2)
    for k, ref in enumerate(outs):
        at = pl.multiple_of(lax.bitwise_xor(base, k) * rows, 16)
        ref[...] = all_ref[pl.ds(at, rows), :]


def early_last_kernel(ins, outs, scratch):
    place_ref, mine, other = ins
    gate_ref, up_ref, down_ref, out_ref = outs
    mine_ref, other_ref = scratch
    parity = place_ref[2]
    chip_place = lax.div(place_ref[0], 2)
    rows = mine[0].shape[0]
    for k in range(len(mine)):
        at = 0 if len(mine) == 1 else pl.multiple_of(lax.bitwise_xor(chip_place, k) * rows, 16)
        mine_ref[pl.ds(at, rows), :] = mine[k][...]
        other_ref[pl.ds(at, rows), :] = other[k][...]
    half = down_ref.shape[0] // 2
    out_half = out_ref.shape[0] // 2
    for ref, side in ((mine_ref, parity), (other_ref, 1 - parity)):
        cols = pl.multiple_of(side * half, 128)
        gate_ref[:, pl.ds(cols, half)] = ref[:half, :].T.astype(f32)
        up_ref[:, pl.ds(cols, half)] = ref[half : 2 * half, :].T.astype(f32)
        at = pl.multiple_of(side * half, 16)
        down_ref[pl.ds(at, half), :] = ref[2 * half : 3 * half, :].astype(f32)
        at = pl.multiple_of(side * out_half, 16)
        out_ref[pl.ds(at, out_half), :] = ref[3 * half :, :].astype(f32)


def run_kernel(kernel, args, outs, scratch=()):
    vmem = pl.BlockSpec(memory_space=pltpu.VMEM)
    smem = pl.BlockSpec(memory_space=pltpu.SMEM)
    flat, in_tree = jax.tree.flatten(args)
    shapes = jax.tree.map(
        lambda o: jax.ShapeDtypeStruct(*o), outs, is_leaf=lambda o: not isinstance(o[0][0], tuple)
    )
    flat_out, out_tree = jax.tree.flatten(shapes)

    def wrapped(*refs):
        ins = jax.tree.unflatten(in_tree, refs[: len(flat)])
        targets = jax.tree.unflatten(out_tree, refs[len(flat) : len(flat) + len(flat_out)])
        kernel(ins, targets, refs[len(flat) + len(flat_out) :])

    call = pl.pallas_call(
        wrapped,
        in_specs=[smem if a.dtype == jnp.int32 and a.ndim == 1 else vmem for a in flat],
        out_specs=[vmem for _ in flat_out],
        out_shape=flat_out,
        scratch_shapes=[pltpu.VMEM(s, d) for s, d in scratch],
        compiler_params=pltpu.CompilerParams(vmem_limit_bytes=56 * 2**20),
    )
    return jax.tree.unflatten(out_tree, call(*flat))


def make_body(fsdp_size, ctx_size):
    chips = ctx_size // 2

    def from_peer(x, axis, offset):
        size = fsdp_size if axis == "fsdp" else ctx_size
        return lax.ppermute(x, axis, [((i + offset) % size, i) for i in range(size)])

    def with_partner(x, bit=1):
        return lax.ppermute(x, "ctx", [(i, i ^ bit) for i in range(ctx_size)])

    def others_fsdp(x):
        return [from_peer(x, "fsdp", k) for k in range(1, fsdp_size)]

    def with_partners(parts):
        return [with_partner(p) for p in parts]

    def after(x, *others):
        return lax.optimization_barrier((x,) + others)[0]

    def pick(x, at, axis=0):
        return lax.dynamic_index_in_dim(x, at, axis, keepdims=False)

    def sum_chips(parts, ctx_place):
        if len(parts) == 4:
            far = with_partner(parts[3], 2)
            near = with_partner(parts[1], 2)
            passed = (parts[2].astype(f32) + far.astype(f32)).astype(bf16)
            across = with_partner(passed, 4)
            total = parts[0].astype(f32) + near.astype(f32) + across.astype(f32)
            total = total.astype(bf16)
            second = with_partner(total, 4)
            first = with_partner(total, 2)
            return [total, first, second, with_partner(second, 2)]
        keep, send = parts
        width = keep.shape[1]
        steps = []
        bit = 2
        while bit < ctx_size:
            side = (ctx_place // bit) % 2
            sent = with_partner(send, bit)
            total = (keep.astype(f32) + sent.astype(f32)).astype(bf16)
            if 2 * bit < ctx_size:
                halves = total.reshape(2, -1, width)
                ahead = (ctx_place // (2 * bit)) % 2
                keep, send = pick(halves, ahead), pick(halves, 1 - ahead)
            steps.append((bit, side))
            bit *= 2
        for bit, side in reversed(steps):
            other = with_partner(total, bit)
            first = jnp.where(side == 0, total, other)
            second = jnp.where(side == 0, other, total)
            total = jnp.concatenate([first, second], axis=0)
        return [total]

    def body(
        tokens,
        cotangent,
        positions,
        block_order,
        query_weight,
        key_weight,
        value_weight,
        output_weight,
        gate_weight,
        up_weight,
        down_weight,
        input_gain,
        query_gain,
        key_gain,
        mixer_gain,
        prefeed_gain,
        postfeed_gain,
    ):
        row_count = tokens.shape[1]
        width = tokens.shape[2]
        block_rows = row_count // 2
        head_dim = key_weight.shape[1]
        query_width = query_weight.shape[1]
        head_count = query_width // head_dim
        proj_width = query_width + 2 * head_dim
        proj_half = proj_width // 2
        shard_rows = query_weight.shape[0]
        out_rows = output_weight.shape[0]
        hidden_rows = down_weight.shape[0]
        half_rows = hidden_rows // 2
        ctx_place = lax.axis_index("ctx")
        fsdp_place = lax.axis_index("fsdp")
        parity = ctx_place % 2

        place = jnp.concatenate(
            [jnp.stack([ctx_place, fsdp_place, parity]).astype(jnp.int32), block_order]
        )
        tok, cot = tokens[0], cotangent[0]
        rows_width = (row_count, width)
        (proj_send,) = run_kernel(
            first_kernel,
            (parity.astype(jnp.int32).reshape(1), query_weight, key_weight, value_weight),
            (((shard_rows, proj_half), bf16),),
        )
        proj_mine = others_fsdp(proj_send)
        gain_cols, head_cols = input_gain.shape[0], query_gain.shape[0]
        (gains_own,) = run_kernel(
            gains_kernel,
            (input_gain, mixer_gain, prefeed_gain, postfeed_gain, query_gain, key_gain),
            (((8, gain_cols), f32),),
        )
        gain_parts = [gains_own] + others_fsdp(gains_own)
        gain_full = jnp.zeros((fsdp_size,) + gains_own.shape, f32)
        for k, part in enumerate(gain_parts):
            gain_full = lax.dynamic_update_index_in_dim(
                gain_full, part, (fsdp_place + k) % fsdp_size, 0
            )
        gain_full = gain_full.transpose(1, 0, 2)
        gains = gain_full[:4].reshape(4, width)
        qk_gains = gain_full[4:6, :, :head_cols].reshape(2, head_dim)

        frequency = rope_base ** (-2.0 * jnp.arange(head_dim // 2, dtype=f32) / head_dim)
        cosines, sine_terms, query_last, query_first, key_ids = run_kernel(
            table_kernel,
            (place, positions[0][:, None], frequency[None]),
            (
                ((row_count, head_dim // 2), f32),
                ((row_count, head_dim // 2), f32),
                ((row_count, 1), jnp.int32),
                ((row_count, 1), jnp.int32),
                ((2, 1, ctx_size * block_rows), jnp.int32),
            ),
        )
        proj_ready = list(
            lax.optimization_barrier((*proj_mine, gains, qk_gains, cosines, sine_terms))
        )[: fsdp_size - 1]
        proj_theirs = with_partners(proj_ready)

        out_half, pair_half, down_half = run_kernel(
            halves_kernel,
            (place, output_weight, gate_weight, up_weight, down_weight),
            (
                ((out_rows // 2, width), bf16),
                ((width, 2 * half_rows), bf16),
                ((half_rows, width), bf16),
            ),
        )
        out_mine = others_fsdp(out_half)
        pair_mine = others_fsdp(pair_half)

        normed, query_rows, own_pair, query_raw, key_raw, proj_full = run_kernel(
            pre_kernel,
            (place, tok, gains, qk_gains, cosines, sine_terms,
             query_weight, key_weight, value_weight, proj_ready, proj_theirs),
            (
                (rows_width, bf16),
                ((row_count, query_width), bf16),
                ((row_count, 2 * head_dim), bf16),
                ((row_count, query_width), f32),
                ((row_count, head_dim), f32),
                ((fsdp_size * shard_rows, proj_width), bf16),
            ),
        )
        kv_mine = [own_pair] + [from_peer(own_pair, "ctx", 2 * k) for k in range(1, chips)]
        kv_theirs = [with_partner(own_pair)] + with_partners(kv_mine[1:])
        down_mine = others_fsdp(after(down_half, own_pair))
        out_theirs = with_partners(out_mine)
        pair_ready = list(lax.optimization_barrier((*pair_mine, *kv_mine[1:])))[: fsdp_size - 1]
        pair_theirs = with_partners(pair_ready)
        down_theirs = with_partners(down_mine)
        attended, log_total, key_pairs, output_full, projected, hidden, feed_in = run_kernel(
            attend_kernel,
            (place, tok, query_rows, kv_mine, kv_theirs, query_last, query_first, key_ids,
             output_weight, out_mine, out_theirs, gains),
            (
                ((row_count, query_width), bf16),
                ((2, head_count * block_rows, 1), f32),
                ((2, ctx_size * block_rows, 2 * head_dim), bf16),
                ((fsdp_size * out_rows, width), bf16),
                (rows_width, f32),
                (rows_width, f32),
                (rows_width, bf16),
            ),
        )
        feed_all = [feed_in] + others_fsdp(feed_in)
        (output, grad_feed, grad_hidden, grad_attended, gmix, gpre, gpost,
         out_own, out_other) = run_kernel(
            feed_kernel,
            (place, cot, feed_in, hidden, projected, output_full, gains,
             attended, gate_weight, up_weight, down_weight,
             pair_ready + pair_theirs, down_mine + down_theirs),
            (
                (rows_width, f32),
                (rows_width, bf16),
                (rows_width, f32),
                ((row_count, query_width), bf16),
                ((1, width), f32),
                ((1, width), f32),
                ((1, width), f32),
                ((fsdp_size * out_rows // 2, width), f32),
                ((fsdp_size * out_rows // 2, width), bf16),
            ),
            (((row_count, fsdp_size * hidden_rows), f32),) * 2
            + (((fsdp_size * out_rows, width), f32),),
        )
        out_other = with_partner(out_other)
        grad_all = [grad_feed] + others_fsdp(grad_feed)
        query_back, pairs_mine, pairs_theirs, gqgain = run_kernel(
            attend_back_kernel,
            (query_rows, key_pairs, grad_attended, attended, log_total,
             query_last, query_first, key_ids, query_raw, qk_gains, cosines, sine_terms),
            (
                ((row_count, query_width), bf16),
                ((chips, row_count, 2 * head_dim), f32),
                ((chips, row_count, 2 * head_dim), bf16),
                ((1, head_dim), f32),
            ),
        )

        pairs_other = with_partner(pairs_theirs)
        chip_part = pairs_mine + pairs_other.astype(f32)
        chip_send = [chip_part[chips - k].astype(bf16) for k in range(1, chips)]
        chip_own = chip_part[0]
        back_parts = [from_peer(chip_send[k - 1], "ctx", 2 * k) for k in range(1, chips)]

        feed_rows = 3 * half_rows
        early_mine, early_theirs, out_chunks = run_kernel(
            weight_kernel,
            (place, feed_all, grad_all, gate_weight, up_weight, down_weight, out_own, out_other),
            (
                ((feed_rows, width), f32),
                ((feed_rows, width), bf16),
                [((out_rows // 2, width), bf16)] * fsdp_size,
            ),
            (((2 * feed_rows, width), f32),),
        )
        out_parts = [out_chunks[0]] + [
            from_peer(out_chunks[k], "fsdp", k) for k in range(1, fsdp_size)
        ]
        early_rows = feed_rows + out_rows // 2
        pieces = 4 if chips == 4 else 2
        early_parts = run_kernel(
            early_pack_kernel,
            (place, early_mine, with_partner(early_theirs), out_parts),
            [((early_rows // pieces, width), bf16)] * pieces,
            (((early_rows, width), bf16),),
        )
        early = sum_chips(early_parts, ctx_place)
        gate_grad, up_grad, down_grad, out_grad = run_kernel(
            early_last_kernel,
            (place, early, with_partners(early)),
            (
                ((width, hidden_rows), f32),
                ((width, hidden_rows), f32),
                ((hidden_rows, width), f32),
                ((out_rows, width), f32),
            ),
            (((early_rows, width), bf16),) * 2,
        )

        tokens_grad, late_mine, late_theirs, late_terms = run_kernel(
            post_kernel,
            (place, tok, chip_own, back_parts, key_raw, gains, qk_gains,
             cosines, sine_terms, normed, query_back, proj_full, grad_hidden,
             gqgain, gmix, gpre, gpost),
            (
                (rows_width, f32),
                ((width, proj_half), f32),
                ((width, proj_half), bf16),
                ((16, proj_half), bf16),
            ),
            (
                ((row_count, proj_width), bf16),
                ((width, proj_width), f32),
                ((8, proj_half), f32),
            ),
        )
        late_shape = ((shard_rows + 16, proj_half), bf16)
        late_chunks = run_kernel(
            late_pack_kernel,
            (place, late_mine, with_partner(late_theirs), late_terms),
            [late_shape] * fsdp_size,
        )
        late_parts = [late_chunks[0]] + [
            from_peer(late_chunks[k], "fsdp", k) for k in range(1, fsdp_size)
        ]
        (late,) = run_kernel(late_sum_kernel, late_parts, [late_shape])
        bit = 2
        while bit < ctx_size:
            other = with_partner(late, bit)
            (late,) = run_kernel(late_sum_kernel, [late, other], [late_shape])
            bit *= 2
        query_grad, key_grad, value_grad, wide_sums, narrow_sums = run_kernel(
            late_last_kernel,
            (place, late, with_partner(late)),
            (
                ((shard_rows, query_width), f32),
                ((shard_rows, head_dim), f32),
                ((shard_rows, head_dim), f32),
                [((gain_cols,), f32)] * 4,
                [((head_cols,), f32)] * 2,
            ),
            (((shard_rows, proj_width), f32),),
        )
        return (
            output[None],
            tokens_grad[None],
            query_grad,
            key_grad,
            value_grad,
            out_grad,
            gate_grad,
            up_grad,
            down_grad,
            wide_sums[0],
            narrow_sums[0],
            narrow_sums[1],
            wide_sums[1],
            wide_sums[2],
            wide_sums[3],
        )

    return body


def solution(mesh):
    in_specs = (
        P("fsdp", "ctx", None),
        P("fsdp", "ctx", None),
        P("fsdp", "ctx"),
        P(),
        P("fsdp", None),
        P("fsdp", None),
        P("fsdp", None),
        P("fsdp", None),
        P(None, "fsdp"),
        P(None, "fsdp"),
        P("fsdp", None),
        P("fsdp"),
        P("fsdp"),
        P("fsdp"),
        P("fsdp"),
        P("fsdp"),
        P("fsdp"),
    )
    out_specs = (
        P("fsdp", "ctx", None),
        P("fsdp", "ctx", None),
        P("fsdp", None),
        P("fsdp", None),
        P("fsdp", None),
        P("fsdp", None),
        P(None, "fsdp"),
        P(None, "fsdp"),
        P("fsdp", None),
        P("fsdp"),
        P("fsdp"),
        P("fsdp"),
        P("fsdp"),
        P("fsdp"),
        P("fsdp"),
    )
    inner = make_body(mesh.shape["fsdp"], mesh.shape["ctx"])

    return jax.shard_map(inner, mesh=mesh, in_specs=in_specs, out_specs=out_specs, check_vma=False)
```
